256 devices in a mesh: dp: 16 (over z_hi, x, core), fsdp: 16 (over y, z_lo).
Axes of the slice: x: 4, y: 4, z: 8 (z_hi: 2, z_lo: 4; z = z_hi * 4 + z_lo), core: 2. Of those that a mesh axis runs over, the one named last changes fastest.
Arguments:
- token_ids: int32 [32768], P('dp'), may hold values from 0 to 30527, as said below
- embed_table: bfloat16 [30528, 768], P('fsdp'), may hold values from -16 to 16, as said below
- w_qkv: bfloat16 [768, 2304], P('fsdp'), may hold values from -2 to 2
- w_out: bfloat16 [768, 768], P('fsdp'), may hold values from -0.21875 to 0.21875
- ln_gain: float32 [768], replicated, may hold values from 0.5 to 1.5
- ln_bias: float32 [768], replicated, may hold values from -1 to 1
- centroids_t: bfloat16 [768, 32768], P('fsdp', 'dp'), may hold values from -24 to 24
- assignments: int32 [32768], replicated, may hold values from 0 to 32767, as said below
Outputs:
- token_loss: float32 [32768], P(('dp', 'fsdp'))
- new_centroids: float32 [32768, 768], P(('dp', 'fsdp'))
The draws below stay inside these ranges and needn't reach their ends.
Inputs may be any that keep to these rules, and one draw needn't show every extreme that they name: `token_ids`: id 0 is padding; a passage may end in a run of padding. `embed_table`: token embeddings of order one. `assignments`: cluster sizes are skewed.
All inputs are finite; a program needn't handle non-finite values.
Results may differ from the reference program's by a relative error of at most 0.0055.
Values may be sent and summed in bfloat16 or wider, within the bound.
No kernel may reach another device: no remote copies, remote signals or barrier semaphores. Data moves between devices by JAX's collectives and lax.ppermute only.
A program may use at most 64 MiB of HBM per device.

```python
import math
import jax
import jax.numpy as jnp
from jax import lax

D = 768
HEADS = 12
HEAD = 64
VOCAB = 30528
SEQ = 128
CENT = 32768
TOKENS = 32768


def shared_bias(key):
    spread = 0.1
    return spread * jax.random.normal(jax.random.fold_in(key, 7), (D,), jnp.float32)


def skewed_ranks(key, count, limit):
    levels = (limit - 1).bit_length()
    level = jax.random.randint(jax.random.fold_in(key, 1), (count,), 0, levels + 1).astype(jnp.int32)
    upper = jnp.minimum(jnp.left_shift(jnp.ones((count,), jnp.int32), level), limit).astype(jnp.int32)
    return jax.random.randint(jax.random.fold_in(key, 2), (count,), 0, upper).astype(jnp.int32)


def draw_token_ids(key, part):
    passages = TOKENS // SEQ
    ranks = skewed_ranks(jax.random.fold_in(key, 31), TOKENS, VOCAB - 1)
    order = jax.random.permutation(jax.random.fold_in(key, 32), VOCAB - 1).astype(jnp.int32)
    words = order[ranks] + 1
    lengths = jax.random.randint(jax.random.fold_in(key, 33), (passages, 1), SEQ // 8, SEQ + 1).astype(jnp.int32)
    positions = jnp.arange(SEQ, dtype=jnp.int32)
    padded = positions[None, :] >= lengths
    words = jnp.where(padded, jnp.zeros_like(words.reshape(passages, SEQ)), words.reshape(passages, SEQ))
    return words.reshape(TOKENS).astype(jnp.int32)


def draw_assignments(key, part):
    ranks = skewed_ranks(jax.random.fold_in(key, 41), TOKENS, CENT)
    order = jax.random.permutation(jax.random.fold_in(key, 42), CENT).astype(jnp.int32)
    spread_part = order[ranks]
    span = CENT // 8
    first = jax.random.randint(jax.random.fold_in(key, 43), (), 0, 8).astype(jnp.int32) * span
    crowded = first + jax.random.randint(jax.random.fold_in(key, 44), (TOKENS,), 0, span).astype(jnp.int32)
    chosen = jax.random.permutation(jax.random.fold_in(key, 45), TOKENS).astype(jnp.int32) < TOKENS // 4
    return jnp.where(chosen, crowded, spread_part).astype(jnp.int32)


def draw_ln_bias(key, part):
    return shared_bias(key).astype(jnp.float32)


def draw_embed_table(key, part):
    values = jax.random.normal(jax.random.fold_in(key, 3), (VOCAB, D), jnp.float32)
    values = jnp.clip(values, -5.0, 5.0)
    return values.astype(jnp.bfloat16)


def draw_w_qkv(key, part):
    factor = 1.0 / jnp.sqrt(jnp.float32(D))
    parts = jnp.clip(jax.random.normal(jax.random.fold_in(key, 5), (D, 3 * D), jnp.float32), -5.0, 5.0) * factor
    return parts.astype(jnp.bfloat16)


def draw_centroids_t(key, part):
    values = 0.1 * jnp.clip(jax.random.normal(jax.random.fold_in(key, 11), (D, CENT), jnp.float32), -5.0, 5.0)
    return values.astype(jnp.bfloat16)


def block_levels(stream_key, dims, cuts, smallest, top_value):
    def one(axis_at, shards_of):
        heights = jax.random.uniform(jax.random.fold_in(jax.random.fold_in(stream_key, 6), axis_at), (shards_of,), jnp.float32, smallest / len(cuts), top_value / len(cuts))
        return jnp.repeat(jnp.exp(heights), dims[axis_at] // shards_of).reshape((-1,) + (1,) * (len(dims) - axis_at - 1))

    factor_of = one(*cuts[0])
    for cut in cuts[1:]:
        factor_of = factor_of * one(*cut)
    return factor_of


def centred(key, extent, deviation, most, cuts=(), kind=jnp.bfloat16):
    values = jax.random.normal(key, extent, jnp.float32) * deviation
    if len(cuts) > 0:
        values = block_levels(key, extent, cuts, -0.22, 0.18) * values
    return jnp.clip(values, min=-most, max=most).astype(kind)


def setup_inputs(seed: int = 0) -> dict:
    key_of = jax.random.split(jax.random.key(seed), 9)
    token_ids = draw_token_ids(jax.random.fold_in(key_of[8], 71), 0)
    embed_table = draw_embed_table(jax.random.fold_in(key_of[8], 71), 0)
    w_qkv = draw_w_qkv(jax.random.fold_in(key_of[8], 71), 0)
    w_out = centred(key_of[3], (D, D), D ** -0.5, 0.21875, ((0, 16),))
    ln_gain = jnp.clip(1.0 + 0.1 * jax.random.normal(key_of[4], (D,), jnp.float32), 0.5, 1.5)
    ln_bias = draw_ln_bias(jax.random.fold_in(key_of[8], 71), 0)
    centroids_t = draw_centroids_t(jax.random.fold_in(key_of[8], 71), 0)
    assignments = draw_assignments(jax.random.fold_in(key_of[8], 71), 0)
    return dict(token_ids=token_ids, embed_table=embed_table, w_qkv=w_qkv, w_out=w_out, ln_gain=ln_gain, ln_bias=ln_bias, centroids_t=centroids_t, assignments=assignments)


def layer_norm(values, ln_gain, ln_bias):
    center = values - lax.optimization_barrier(jnp.mean(values, axis=-1, keepdims=True))
    spread = lax.optimization_barrier(jnp.mean(center * center, axis=-1, keepdims=True))
    return center * lax.rsqrt(spread + 1e-05) * ln_gain + ln_bias

def reference(token_ids, embed_table, w_qkv, w_out, ln_gain, ln_bias, centroids_t, assignments):
    inputs = embed_table[token_ids]
    passages = TOKENS // SEQ
    packed = jnp.dot(inputs, w_qkv, preferred_element_type=jnp.float32).astype(jnp.bfloat16)
    packed = packed.reshape(passages, SEQ, 3, HEADS, HEAD).astype(jnp.float32)
    scores = jnp.einsum('bqhd,bkhd->bhqk', packed[:, :, 0], packed[:, :, 1]) * (1.0 / math.sqrt(HEAD))
    probs = jax.nn.softmax(scores, axis=-1).astype(jnp.bfloat16)
    context = jnp.einsum('bhqk,bkhd->bqhd', probs.astype(jnp.float32), packed[:, :, 2])
    context = context.astype(jnp.bfloat16).reshape(TOKENS, D)
    mixed = jnp.dot(context, w_out, preferred_element_type=jnp.float32) + inputs.astype(jnp.float32)
    embedded = layer_norm(mixed, ln_gain, ln_bias).astype(jnp.bfloat16)
    block = math.gcd(TOKENS, 512)

    def score_rows(pieces):
        rows, assigned = pieces
        logits = jnp.dot(rows, centroids_t, preferred_element_type=jnp.float32)
        peak = lax.optimization_barrier(jnp.max(logits, axis=1))
        total = jnp.log(lax.optimization_barrier(jnp.sum(jnp.exp(logits - peak[:, None]), axis=1))) + peak
        chosen = jnp.take_along_axis(logits, assigned[:, None], axis=1)[:, 0]
        return total - chosen
    token_loss = lax.map(score_rows, (embedded.reshape(TOKENS // block, block, D), assignments.reshape(TOKENS // block, block))).reshape(TOKENS)
    sums = jax.ops.segment_sum(embedded.astype(jnp.float32), assignments, num_segments=CENT)
    counts = jax.ops.segment_sum(jnp.ones((TOKENS,), jnp.int32), assignments, num_segments=CENT)
    previous = centroids_t.T.astype(jnp.float32)
    new_centroids = jnp.where(counts[:, None] > 0, sums / jnp.maximum(counts, 1)[:, None].astype(jnp.float32), previous)
    return (token_loss, new_centroids)
```

```python
import jax
import jax.numpy as jnp
from jax import lax
from jax.experimental import pallas as pl
from jax.experimental.pallas import tpu as pltpu
from jax.sharding import Mesh
from jax.sharding import PartitionSpec as P

HEADS = 12
HEAD = 64
SEQ = 128
DP = ("zh", "x", "core")
FS = ("y", "zl")
ALL = DP + FS
LIST = 24
SLOTS = 47
BLOCK = SLOTS + 1
F32 = jnp.float32
BF16 = jnp.bfloat16


def iota(shape, dim):
    return lax.broadcasted_iota(jnp.int32, shape, dim)


def dot(a, b, dims=((1,), (0,))):
    return lax.dot_general(a, b, (dims, ((), ())), preferred_element_type=F32)


def lists_kernel(info_ref, ids_ref, table_ref, rows_ref, count_ref):
    vocab = table_ref.shape[0]
    passages = ids_ref.shape[0]
    base = info_ref[0] * vocab
    first_slot = info_ref[1] * LIST
    earlier = iota((SEQ, SEQ), 0) < iota((SEQ, SEQ), 1)
    later = iota((SEQ, SEQ), 0) > iota((SEQ, SEQ), 1)
    owners = iota((passages, SEQ), 0) * vocab
    most = jnp.zeros((passages, 1), F32)
    found = []
    for p in range(passages):
        row = ids_ref[p : p + 1, :]
        across = jnp.broadcast_to(row, (SEQ, SEQ))
        down = across.T
        same = across == down
        new_row = jnp.max(jnp.where(same & earlier, 1.0, 0.0), axis=0, keepdims=True) < 0.5
        new_down = jnp.max(jnp.where(same & later, 1.0, 0.0), axis=1, keepdims=True) < 0.5
        mine_down = (down >= base) & (down < base + vocab)
        before = jnp.where(new_down & mine_down & (down < across), 1.0, 0.0)
        slot = jnp.sum(before, axis=0, keepdims=True).astype(jnp.int32) - first_slot
        mine = (row >= base) & (row < base + vocab)
        chosen = (iota((LIST, SEQ), 0) == slot) & mine
        found.append(jnp.max(jnp.where(chosen, (row - base).astype(F32), -1.0), axis=1, keepdims=True))
        held = (row >= owners) & (row < owners + vocab) & new_row
        most = jnp.maximum(most, jnp.sum(jnp.where(held, 1.0, 0.0), axis=1, keepdims=True))
    wanted = jnp.concatenate(found, axis=0).astype(jnp.int32)
    whole = vocab // 16 * 16
    hits = jnp.where(wanted == iota((wanted.shape[0], whole), 1), 1.0, 0.0).astype(BF16)
    rows = dot(hits, table_ref[0:whole, :])
    if whole < vocab:
        tail = table_ref[whole:vocab, :].astype(F32)
        for k in range(vocab - whole):
            rows = rows + jnp.where(wanted == whole + k, tail[k : k + 1, :], 0.0)
    rows_ref[...] = rows.astype(BF16).reshape(rows_ref.shape)
    count_ref[...] = jnp.broadcast_to(jnp.max(most, axis=0, keepdims=True), count_ref.shape).astype(
        jnp.int32
    )


def listed_rows(info, ids, table):
    passages = ids.shape[0]
    return pl.pallas_call(
        lists_kernel,
        out_shape=(
            jax.ShapeDtypeStruct((passages, LIST, table.shape[1]), BF16),
            jax.ShapeDtypeStruct((8, 128), jnp.int32),
        ),
        in_specs=[
            pl.BlockSpec(memory_space=pltpu.SMEM),
            pl.BlockSpec(memory_space=pltpu.VMEM),
            pl.BlockSpec(memory_space=pltpu.VMEM),
        ],
        out_specs=(pl.BlockSpec(memory_space=pltpu.VMEM), pl.BlockSpec(memory_space=pltpu.VMEM)),
        compiler_params=pltpu.CompilerParams(vmem_limit_bytes=40 << 20),
    )(info, ids, table)


def expand_kernel(info_ref, row_ref, vocab_ref, got_ref, out_ref):
    owners, _, width = got_ref.shape
    vocab = vocab_ref[0]
    first_slot = info_ref[1] * LIST
    row = row_ref[...]
    across = jnp.broadcast_to(row, (SEQ, SEQ))
    down = across.T

    def owner_of(ids):
        owner = jnp.zeros(ids.shape, jnp.int32)
        for k in range(1, owners):
            owner = owner + jnp.where(ids >= k * vocab, 1, 0)
        return owner

    owner_across = jnp.broadcast_to(owner_of(row), (SEQ, SEQ))
    owner_down = owner_across.T
    earlier = iota((SEQ, SEQ), 0) < iota((SEQ, SEQ), 1)
    new_row = jnp.max(jnp.where((across == down) & earlier, 1.0, 0.0), axis=0, keepdims=True) < 0.5
    before = jnp.where(new_row & (owner_across == owner_down) & (across < down), 1.0, 0.0)
    slot = jnp.sum(before, axis=1, keepdims=True).astype(jnp.int32) - first_slot
    place = owner_down[:, 0:1] * LIST + slot
    place = jnp.where((slot >= 0) & (slot < LIST), place, -1)
    hits = jnp.where(place == iota((SEQ, owners * LIST), 1), 1.0, 0.0).astype(BF16)
    out_ref[...] = dot(hits, got_ref[...].reshape(owners * LIST, width)).astype(BF16)


def expanded(info, row, vocab, got):
    return pl.pallas_call(
        expand_kernel,
        out_shape=jax.ShapeDtypeStruct((SEQ, got.shape[2]), BF16),
        in_specs=[
            pl.BlockSpec(memory_space=pltpu.SMEM),
            pl.BlockSpec(memory_space=pltpu.VMEM),
            pl.BlockSpec(memory_space=pltpu.SMEM),
            pl.BlockSpec(memory_space=pltpu.VMEM),
        ],
        out_specs=pl.BlockSpec(memory_space=pltpu.VMEM),
    )(info, row, vocab, got)


def encode_kernel(x_ref, w_ref, gain_ref, bias_ref, out_ref, packed_ref, context_ref):
    x = x_ref[...]
    part = w_ref.shape[2]
    width = x.shape[1]
    for j in range(6):
        packed_ref[:, j * part : (j + 1) * part] = dot(x, w_ref[j]).astype(BF16)
    left = iota((SEQ, 2 * HEAD), 1) < HEAD
    zero = jnp.zeros((SEQ, 2 * HEAD), BF16)
    for b in range(x.shape[0] // SEQ):
        rows = slice(b * SEQ, (b + 1) * SEQ)
        for pair in range(HEADS // 2):
            at = pair * 2 * HEAD
            q = packed_ref[rows, at : at + 2 * HEAD] * jnp.asarray(HEAD**-0.5, BF16)
            k = packed_ref[rows, width + at : width + at + 2 * HEAD]
            v = packed_ref[rows, 2 * width + at : 2 * width + at + 2 * HEAD]
            outs = []
            for one in (jnp.where(left, q, zero), jnp.where(left, zero, q)):
                s = dot(one, k, ((1,), (1,)))
                e = jnp.exp(s - jnp.max(s, axis=1, keepdims=True))
                probs = (e * (1.0 / jnp.sum(e, axis=1, keepdims=True))).astype(BF16)
                outs.append(dot(probs, v))
            context_ref[rows, at : at + 2 * HEAD] = jnp.where(left, outs[0], outs[1]).astype(BF16)
    context = context_ref[...]
    half = width // 2
    mixed = [
        dot(context, w_ref[6 + i]) + x[:, i * half : (i + 1) * half].astype(F32) for i in range(2)
    ]
    mean = sum(jnp.sum(m, axis=1, keepdims=True) for m in mixed) * (1.0 / width)
    center = [m - mean for m in mixed]
    spread = sum(jnp.sum(c * c, axis=1, keepdims=True) for c in center) * (1.0 / width)
    scale = lax.rsqrt(spread + 1e-05)
    for i in range(2):
        cols = slice(i * half, (i + 1) * half)
        out_ref[:, cols] = (center[i] * scale * gain_ref[:, cols] + bias_ref[:, cols]).astype(BF16)


def encoded(x, w, gain, bias):
    tokens, width = x.shape
    step = 2 * SEQ
    return pl.pallas_call(
        encode_kernel,
        grid=(tokens // step,),
        out_shape=jax.ShapeDtypeStruct((tokens, width), BF16),
        in_specs=[
            pl.BlockSpec((step, width), lambda i: (i, 0)),
            pl.BlockSpec(w.shape, lambda i: (0, 0, 0), pipeline_mode=pl.Buffered(1)),
            pl.BlockSpec((1, width), lambda i: (0, 0)),
            pl.BlockSpec((1, width), lambda i: (0, 0)),
        ],
        out_specs=pl.BlockSpec((step, width), lambda i: (i, 0)),
        scratch_shapes=[pltpu.VMEM((step, 3 * width), BF16), pltpu.VMEM((step, width), BF16)],
        compiler_params=pltpu.CompilerParams(vmem_limit_bytes=40 << 20),
    )(x, w, gain.reshape(1, width), bias.reshape(1, width))


def score_kernel(x_ref, local_ref, cent_ref, out_ref):
    rows = x_ref.shape[0]
    block = cent_ref.shape[1]
    s = dot(x_ref[...], cent_ref[...])
    peak = jnp.max(s, axis=1, keepdims=True)
    mass = jnp.sum(jnp.exp(s - peak), axis=1, keepdims=True)
    local = jnp.concatenate(
        [jnp.broadcast_to(local_ref[b], (SEQ, SEQ)).T[:, 0:1] for b in range(rows // SEQ)], axis=0
    )
    picked = jnp.sum(jnp.where(local == iota((rows, block), 1), s, 0.0), axis=1, keepdims=True)
    both = jnp.where(iota((rows, 128), 1) == 0, peak + jnp.log(mass), picked)
    for b in range(rows // SEQ):
        out_ref[b] = both[b * SEQ : (b + 1) * SEQ, :].T[0:8, :]


def scored(x, local, cent):
    tokens, width = x.shape
    step = 2 * SEQ
    per = step // SEQ
    return pl.pallas_call(
        score_kernel,
        grid=(tokens // step,),
        out_shape=jax.ShapeDtypeStruct((tokens // SEQ, 8, SEQ), F32),
        in_specs=[
            pl.BlockSpec((step, width), lambda i: (i, 0)),
            pl.BlockSpec((per, 1, SEQ), lambda i: (i, 0, 0)),
            pl.BlockSpec(cent.shape, lambda i: (0, 0), pipeline_mode=pl.Buffered(1)),
        ],
        out_specs=pl.BlockSpec((per, 8, SEQ), lambda i: (i, 0, 0)),
        compiler_params=pltpu.CompilerParams(vmem_limit_bytes=40 << 20),
    )(x, local.reshape(tokens // SEQ, 1, SEQ), cent)


def pack_kernel(info_ref, local_ref, mine_ref, other_ref, out_ref, hits_ref):
    dests, _, width = out_ref.shape
    per = 128
    tokens = local_ref.shape[1]
    first_slot = info_ref[1] * SLOTS
    local = local_ref[...]
    ones = jnp.ones((tokens, per), BF16)
    upper = iota((per, per), 0) < iota((per, per), 1)
    diagonal = iota((per, per), 0) == iota((per, per), 1)
    most = jnp.zeros((1, 1), F32)
    for g in range(dests):
        hits = jnp.where(local - g * per == iota((per, tokens), 0), 1.0, 0.0).astype(BF16)
        present = jnp.where(dot(hits, ones) > 0.5, 1.0, 0.0)
        rank = jnp.sum(jnp.where(upper, present, 0.0), axis=0, keepdims=True).astype(jnp.int32)
        here = jnp.sum(jnp.where(diagonal, present, 0.0), axis=0, keepdims=True)
        most = jnp.maximum(most, jnp.sum(here, axis=1, keepdims=True))
        slot = iota((BLOCK, per), 0)
        chosen = (slot < SLOTS) & (slot == rank - first_slot) & (here > 0.5)
        packing = jnp.where(chosen, 1.0, 0.0).astype(BF16)
        hits_ref[g * BLOCK : (g + 1) * BLOCK, :] = dot(packing, hits).astype(BF16)
    half = tokens // 2
    sums = dot(hits_ref[:, 0:half], mine_ref[...]) + dot(hits_ref[:, half:], other_ref[...])
    sums = sums.astype(BF16).reshape(dests, BLOCK, width)
    last = iota((dests, BLOCK, width), 1) == SLOTS
    out_ref[...] = jnp.where(last, most.reshape(1, 1, 1).astype(BF16), sums)


def packed_sums(info, local, mine, other, dests):
    tokens = local.shape[1]
    width = mine.shape[1]
    return pl.pallas_call(
        pack_kernel,
        out_shape=jax.ShapeDtypeStruct((dests, BLOCK, width), BF16),
        in_specs=[pl.BlockSpec(memory_space=pltpu.SMEM)]
        + [pl.BlockSpec(memory_space=pltpu.VMEM)] * 3,
        out_specs=pl.BlockSpec(memory_space=pltpu.VMEM),
        scratch_shapes=[pltpu.VMEM((dests * BLOCK, tokens), BF16)],
        compiler_params=pltpu.CompilerParams(vmem_limit_bytes=48 << 20),
    )(info, local, mine, other)


def count_kernel(info_ref, assign_ref, out_ref):
    dp, slabs, _ = assign_ref.shape
    targets = iota((128, SEQ), 0) + info_ref[0]
    columns = []
    for f in range(slabs):
        acc = jnp.zeros((128, SEQ), F32)
        for d in range(dp):
            acc = acc + jnp.where(assign_ref[d, f : f + 1, :] == targets, 1.0, 0.0)
        columns.append(jnp.sum(acc, axis=1, keepdims=True))
    out = jnp.zeros(out_ref.shape, F32)
    lane = iota(out_ref.shape, 1)
    for f in range(slabs):
        out = jnp.where(lane == f, columns[f], out)
    out_ref[...] = out


def counted(info, assign):
    return pl.pallas_call(
        count_kernel,
        out_shape=jax.ShapeDtypeStruct((128, 128), F32),
        in_specs=[pl.BlockSpec(memory_space=pltpu.SMEM), pl.BlockSpec(memory_space=pltpu.VMEM)],
        out_specs=pl.BlockSpec(memory_space=pltpu.VMEM),
    )(info, assign)


def unpack_kernel(info_ref, counts_ref, got_ref, out_ref):
    slabs, _, width = got_ref.shape
    counts = counts_ref[...]
    present = jnp.where(counts > 0.5, 1.0, 0.0).astype(BF16)
    lower = jnp.where(iota((128, 128), 1) < iota((128, 128), 0), 1.0, 0.0).astype(BF16)
    rank = dot(lower, present).astype(jnp.int32) - info_ref[1] * SLOTS
    slot = iota((128, BLOCK), 1)
    parts = []
    for f in range(slabs):
        chosen = (slot == rank[:, f : f + 1]) & (slot < SLOTS) & (counts[:, f : f + 1] > 0.5)
        parts.append(jnp.where(chosen, 1.0, 0.0))
    hits = jnp.concatenate(parts, axis=1).astype(BF16)
    out_ref[...] = dot(hits, got_ref[...].reshape(slabs * BLOCK, width))


def unpacked_sums(info, counts, got):
    return pl.pallas_call(
        unpack_kernel,
        out_shape=jax.ShapeDtypeStruct((128, got.shape[2]), F32),
        in_specs=[pl.BlockSpec(memory_space=pltpu.SMEM)]
        + [pl.BlockSpec(memory_space=pltpu.VMEM)] * 2,
        out_specs=pl.BlockSpec(memory_space=pltpu.VMEM),
    )(info, counts, got)


def exchanged(blocks, axis):
    return lax.all_to_all(blocks, axis, 0, 0, tiled=True)


def gathered(shard, axis):
    devices = lax.axis_size(axis)
    return exchanged(jnp.broadcast_to(shard[None], (devices,) + shard.shape), axis)


def swapped(shard, axis):
    return lax.ppermute(shard, axis, [(0, 1), (1, 0)])


def shards(token_ids, embed_table, w_qkv, w_out, ln_gain, ln_bias, centroids_t, assignments):
    core = lax.axis_index("core")
    dp_rank = lax.axis_index(DP)
    fs_rank = lax.axis_index(FS)
    fs_size = lax.axis_size(FS)
    dp_size = lax.axis_size(DP)
    x_size = lax.axis_size("x")
    vocab, width = embed_table.shape
    zero = jnp.int32(0)
    ids = token_ids.reshape(fs_size, SEQ)

    part = (w_qkv.shape[1] + w_out.shape[1]) // (2 * x_size)
    both = jnp.concatenate([w_qkv, w_out], axis=1)
    chosen = core * x_size + lax.axis_index("x")
    piece = lax.dynamic_slice_in_dim(both, chosen * part, part, 1)
    column = gathered(piece, FS).reshape(width, part)
    mine_w = gathered(column, "x")
    other_w = swapped(mine_w, "core")
    weights = jnp.where(
        core == 0,
        jnp.concatenate([mine_w, other_w], axis=0),
        jnp.concatenate([other_w, mine_w], axis=0),
    )

    rows = gathered(centroids_t, "zl").reshape(-1, centroids_t.shape[1])
    cent = gathered(rows, "y").reshape(width, -1)

    my_row = lax.dynamic_slice_in_dim(ids, fs_rank, 1, 0)
    vocab_arr = jnp.full((1,), vocab, jnp.int32)

    def info_of(first, turn):
        return jnp.stack([first, turn]).astype(jnp.int32)

    sent, most = listed_rows(info_of(fs_rank, zero), ids, embed_table)
    inputs = expanded(info_of(fs_rank, zero), my_row, vocab_arr, exchanged(sent, FS))

    def more_rows(state):
        turn, acc = state
        info = info_of(fs_rank, turn)
        again, _ = listed_rows(info, ids, embed_table)
        return turn + 1, acc + expanded(info, my_row, vocab_arr, exchanged(again, FS))

    most = most[0, 0]
    _, inputs = lax.while_loop(
        lambda state: state[0] * LIST < most, more_rows, (jnp.int32(1), inputs)
    )

    far = swapped(inputs, "zh")
    near = lax.axis_index("zh") == 0
    two = jnp.concatenate([jnp.where(near, inputs, far), jnp.where(near, far, inputs)], axis=0)
    slab = gathered(two, "x").reshape(-1, width)
    mine = encoded(slab, weights, ln_gain, ln_bias)
    other = swapped(mine, "core")

    by_dev = assignments.reshape(2, x_size, 2, fs_size, SEQ)
    of_slab = lax.dynamic_index_in_dim(by_dev, fs_rank, 3, keepdims=False)
    of_slab = jnp.transpose(of_slab, (2, 1, 0, 3))
    of_slab = jnp.where(core == 0, of_slab, of_slab[::-1])
    block = cent.shape[1]
    local = of_slab.reshape(2, -1) - dp_rank * block

    counts = counted(
        (dp_rank * block + fs_rank * (block // fs_size)).reshape(1).astype(jnp.int32),
        assignments.reshape(dp_size, fs_size, SEQ),
    )
    flat = local.reshape(1, -1)

    def one_turn(turn):
        info = info_of(zero, turn)
        got = exchanged(packed_sums(info, flat, mine, other, fs_size), FS)
        return unpacked_sums(info, counts, got), got

    sums, got = one_turn(zero)
    widest = jnp.max(got[:, SLOTS, 0:1].astype(F32)).astype(jnp.int32)
    _, sums = lax.while_loop(
        lambda state: state[0] * SLOTS < widest,
        lambda state: (state[0] + 1, state[1] + one_turn(state[0])[0]),
        (jnp.int32(1), sums),
    )

    stats = jnp.stack([scored(mine, local[0], cent), scored(other, local[1], cent)])
    stats = jnp.where(core == 0, stats, stats[::-1]).reshape(2, x_size, 2, 8, SEQ)
    stats = jnp.transpose(stats, (2, 1, 0, 3, 4)).reshape(dp_size, 8, SEQ)
    home = exchanged(stats, DP)
    lse = home[:, 0, :]
    peak = jnp.max(lse, axis=0)
    token_loss = (
        jnp.log(jnp.sum(jnp.exp(lse - peak[None, :]), axis=0)) + peak - jnp.sum(home[:, 1, :], axis=0)
    )

    total = jnp.sum(counts[:, 0:fs_size], axis=1, keepdims=True)
    previous = lax.dynamic_slice_in_dim(cent, fs_rank * 128, 128, 1).T.astype(F32)
    new_centroids = jnp.where(total > 0, sums / jnp.maximum(total, 1.0), previous)
    return token_loss, new_centroids


def solution(mesh):
    finer = Mesh(mesh.devices.reshape(2, 4, 2, 4, 4), ALL)
    placed = (P(DP), P(FS, None), P(FS, None), P(FS, None), P(), P(), P(FS, DP), P())
    return jax.shard_map(
        shards, mesh=finer, in_specs=placed, out_specs=(P(ALL), P(ALL, None)), check_vma=False
    )
```

```python
import jax
import jax.numpy as jnp
from jax import lax
from jax.experimental import pallas as pl
from jax.experimental.pallas import tpu as pltpu
from jax.sharding import Mesh
from jax.sharding import PartitionSpec as P

HEADS = 12
HEAD = 64
SEQ = 128
DP = ("zh", "x", "core")
FS = ("y", "zl")
ALL = DP + FS
LIST = 16
SLOTS = 39
BLOCK = SLOTS + 1
ROOM = 48
F32 = jnp.float32
BF16 = jnp.bfloat16


def iota(shape, dim):
    return lax.broadcasted_iota(jnp.int32, shape, dim)


def dot(a, b, dims=((1,), (0,))):
    return lax.dot_general(a, b, (dims, ((), ())), preferred_element_type=F32)


def lists_kernel(info_ref, ids_ref, table_ref, rows_ref, count_ref, found_ref):
    vocab = table_ref.shape[0]
    passages = ids_ref.shape[0]
    base = info_ref[0] * vocab
    first_slot = info_ref[1] * LIST
    earlier = iota((SEQ, SEQ), 0) < iota((SEQ, SEQ), 1)
    later = iota((SEQ, SEQ), 0) > iota((SEQ, SEQ), 1)
    owners = iota((passages, SEQ), 0) * vocab

    def passage(p, most):
        row = ids_ref[pl.ds(p, 1), :]
        across = jnp.broadcast_to(row, (SEQ, SEQ))
        down = across.T
        same = across == down
        new_row = jnp.max(jnp.where(same & earlier, 1.0, 0.0), axis=0, keepdims=True) < 0.5
        new_down = jnp.max(jnp.where(same & later, 1.0, 0.0), axis=1, keepdims=True) < 0.5
        mine_down = (down >= base) & (down < base + vocab)
        before = jnp.where(new_down & mine_down & (down < across), 1.0, 0.0)
        slot = jnp.sum(before, axis=0, keepdims=True).astype(jnp.int32) - first_slot
        mine = (row >= base) & (row < base + vocab)
        chosen = (iota((LIST, SEQ), 0) == slot) & mine
        found = jnp.max(jnp.where(chosen, row - base, -1).astype(F32), axis=1, keepdims=True)
        found_ref[pl.ds(pl.multiple_of(p * LIST, LIST), LIST), :] = jnp.broadcast_to(found, (LIST, 128))
        held = (row >= owners) & (row < owners + vocab) & new_row
        return jnp.maximum(most, jnp.sum(jnp.where(held, 1.0, 0.0), axis=1, keepdims=True))

    most = lax.fori_loop(0, passages, passage, jnp.zeros((passages, 1), F32), unroll=4)
    wanted = found_ref[:, 0:1].astype(jnp.int32)
    whole = vocab // 16 * 16
    hits = jnp.where(wanted == iota((wanted.shape[0], whole), 1), 1.0, 0.0).astype(BF16)
    rows = dot(hits, table_ref[0:whole, :])
    if whole < vocab:
        tail = table_ref[whole:vocab, :].astype(F32)
        for k in range(vocab - whole):
            rows = rows + jnp.where(wanted == whole + k, tail[k : k + 1, :], 0.0)
    rows_ref[...] = rows.astype(BF16).reshape(rows_ref.shape)
    count_ref[...] = jnp.broadcast_to(jnp.max(most, axis=0, keepdims=True), count_ref.shape).astype(
        jnp.int32
    )


def listed_rows(info, ids, table):
    passages = ids.shape[0]
    return pl.pallas_call(
        lists_kernel,
        out_shape=(
            jax.ShapeDtypeStruct((passages, LIST, table.shape[1]), BF16),
            jax.ShapeDtypeStruct((8, 128), jnp.int32),
        ),
        in_specs=[
            pl.BlockSpec(memory_space=pltpu.SMEM),
            pl.BlockSpec(memory_space=pltpu.VMEM),
            pl.BlockSpec(memory_space=pltpu.VMEM),
        ],
        out_specs=(pl.BlockSpec(memory_space=pltpu.VMEM), pl.BlockSpec(memory_space=pltpu.VMEM)),
        scratch_shapes=[pltpu.VMEM((passages * LIST, 128), F32)],
        compiler_params=pltpu.CompilerParams(vmem_limit_bytes=40 << 20),
    )(info, ids, table)


def expand_kernel(info_ref, row_ref, vocab_ref, got_ref, out_ref):
    owners, _, width = got_ref.shape
    vocab = vocab_ref[0]
    first_slot = info_ref[1] * LIST
    row = row_ref[...]
    across = jnp.broadcast_to(row, (SEQ, SEQ))
    down = across.T

    def owner_of(ids):
        owner = jnp.zeros(ids.shape, jnp.int32)
        for k in range(1, owners):
            owner = owner + jnp.where(ids >= k * vocab, 1, 0)
        return owner

    owner_across = jnp.broadcast_to(owner_of(row), (SEQ, SEQ))
    owner_down = owner_across.T
    earlier = iota((SEQ, SEQ), 0) < iota((SEQ, SEQ), 1)
    new_row = jnp.max(jnp.where((across == down) & earlier, 1.0, 0.0), axis=0, keepdims=True) < 0.5
    before = jnp.where(new_row & (owner_across == owner_down) & (across < down), 1.0, 0.0)
    slot = jnp.sum(before, axis=1, keepdims=True).astype(jnp.int32) - first_slot
    place = owner_down[:, 0:1] * LIST + slot
    place = jnp.where((slot >= 0) & (slot < LIST), place, -1)
    hits = jnp.where(place == iota((SEQ, owners * LIST), 1), 1.0, 0.0).astype(BF16)
    out_ref[...] = dot(hits, got_ref[...].reshape(owners * LIST, width)).astype(BF16)


def expanded(info, row, vocab, got):
    return pl.pallas_call(
        expand_kernel,
        out_shape=jax.ShapeDtypeStruct((SEQ, got.shape[2]), BF16),
        in_specs=[
            pl.BlockSpec(memory_space=pltpu.SMEM),
            pl.BlockSpec(memory_space=pltpu.VMEM),
            pl.BlockSpec(memory_space=pltpu.SMEM),
            pl.BlockSpec(memory_space=pltpu.VMEM),
        ],
        out_specs=pl.BlockSpec(memory_space=pltpu.VMEM),
    )(info, row, vocab, got)


def put(sources, targets, sems):
    copies = [
        pltpu.make_async_copy(src, dst, sems.at[k])
        for k, (src, dst) in enumerate(zip(sources, targets, strict=True))
    ]
    for c in copies:
        c.start()
    for c in copies:
        c.wait()


def encode_kernel(info_ref, *refs):
    x_size = 4
    x_parts, w_parts = refs[0:x_size], refs[x_size : 3 * x_size]
    gain_ref, bias_ref, out_ref = refs[3 * x_size : 3 * x_size + 3]
    x_ref, w_ref, packed_ref, scores_ref, probs_ref, context_ref, sems = refs[3 * x_size + 3 :]
    core, at_x = info_ref[0], info_ref[1]
    places = [
        half * x_size + lax.rem(at_x - k + x_size, x_size)
        for half in (core, 1 - core)
        for k in range(x_size)
    ]
    put(
        x_parts + w_parts,
        [x_ref.at[k] for k in range(x_size)] + [w_ref.at[p] for p in places],
        sems,
    )
    part = w_ref.shape[2]
    tokens, width = x_ref.shape[1:]
    left = iota((SEQ, 2 * HEAD), 1) < HEAD
    zero = jnp.zeros((SEQ, 2 * HEAD), BF16)
    pairs = HEADS // 2
    passages = tokens // SEQ

    def stacked(values):
        return jnp.concatenate([jnp.where(left, values, zero), jnp.where(left, zero, values)], axis=0)

    def step(i, _):
        x = x_ref[i]
        for j in range(6):
            packed_ref[:, j * part : (j + 1) * part] = dot(x, w_ref[j]).astype(BF16)
        for b in range(passages):
            rows = slice(b * SEQ, (b + 1) * SEQ)
            for pair in range(pairs):
                at = pair * 2 * HEAD
                q = packed_ref[rows, at : at + 2 * HEAD] * jnp.asarray(HEAD**-0.5, BF16)
                k = packed_ref[rows, width + at : width + at + 2 * HEAD]
                scores_ref[b * pairs + pair] = dot(q, stacked(k), ((1,), (1,)))
        for n in range(passages * pairs):
            for h in range(2):
                s = scores_ref[n, :, h * SEQ : (h + 1) * SEQ]
                e = jnp.exp(s - jnp.max(s, axis=1, keepdims=True))
                probs = e * (1.0 / jnp.sum(e, axis=1, keepdims=True))
                probs_ref[n, :, h * SEQ : (h + 1) * SEQ] = probs.astype(BF16)
        for b in range(passages):
            rows = slice(b * SEQ, (b + 1) * SEQ)
            for pair in range(pairs):
                at = pair * 2 * HEAD
                v = packed_ref[rows, 2 * width + at : 2 * width + at + 2 * HEAD]
                context_ref[rows, at : at + 2 * HEAD] = dot(
                    probs_ref[b * pairs + pair], stacked(v)
                ).astype(BF16)
        context = context_ref[...]
        half = width // 2
        mixed = [
            dot(context, w_ref[6 + k]) + x[:, k * half : (k + 1) * half].astype(F32) for k in range(2)
        ]
        mean = sum(jnp.sum(m, axis=1, keepdims=True) for m in mixed) * (1.0 / width)
        center = [m - mean for m in mixed]
        spread = sum(jnp.sum(c * c, axis=1, keepdims=True) for c in center) * (1.0 / width)
        scale = lax.rsqrt(spread + 1e-05)
        for k in range(2):
            cols = slice(k * half, (k + 1) * half)
            out_ref[pl.ds(i * tokens, tokens), cols] = (
                center[k] * scale * gain_ref[:, cols] + bias_ref[:, cols]
            ).astype(BF16)
        return 0

    lax.fori_loop(0, x_size, step, 0)


def encoded(info, x_parts, w_parts, gain, bias):
    tokens, width = x_parts[0].shape
    part = w_parts[0].shape[1]
    count = len(x_parts) + len(w_parts)
    pairs = tokens // SEQ * HEADS // 2
    return pl.pallas_call(
        encode_kernel,
        out_shape=jax.ShapeDtypeStruct((len(x_parts) * tokens, width), BF16),
        in_specs=[pl.BlockSpec(memory_space=pltpu.SMEM)]
        + [pl.BlockSpec(memory_space=pl.ANY)] * count
        + [pl.BlockSpec(memory_space=pltpu.VMEM)] * 2,
        out_specs=pl.BlockSpec(memory_space=pltpu.VMEM),
        scratch_shapes=[
            pltpu.VMEM((len(x_parts), tokens, width), BF16),
            pltpu.VMEM((len(w_parts), width, part), BF16),
            pltpu.VMEM((tokens, 3 * width), BF16),
            pltpu.VMEM((pairs, SEQ, 2 * SEQ), F32),
            pltpu.VMEM((pairs, SEQ, 2 * SEQ), BF16),
            pltpu.VMEM((tokens, width), BF16),
            pltpu.SemaphoreType.DMA((count,)),
        ],
        compiler_params=pltpu.CompilerParams(vmem_limit_bytes=40 << 20),
    )(info, *x_parts, *w_parts, gain.reshape(1, width), bias.reshape(1, width))


def score_kernel(info_ref, mine_ref, other_ref, local_ref, *refs):
    own, (back_ref, low_ref, high_ref, ahead_ref) = refs[0:4], refs[4:8]
    out_ref, old_ref, cent_ref, sems = refs[8:]
    step = pl.program_id(0)
    shard = own[0].shape[0]

    @pl.when(step == 0)
    def _():
        at_y, at_zl = info_ref[0], info_ref[1]
        targets = []
        for back in range(4):
            for k in range(4):
                place = 4 * lax.rem(at_y - back + 4, 4) + lax.rem(at_zl - k + 4, 4)
                targets.append(cent_ref.at[pl.ds(pl.multiple_of(place * shard, shard), shard), :])
        far = [low_ref] * 2 + [high_ref] * 2
        spots = [(back_ref, k) for k in range(4)]
        spots += [(ref, k % 2) for k, ref in enumerate(far)]
        spots += [(ahead_ref, k) for k in range(4)]
        put(list(own) + [ref.at[pl.ds(k * shard, shard), :] for ref, k in spots], targets, sems)

    rows = mine_ref.shape[0]
    block = cent_ref.shape[1]
    half = pl.num_programs(0) // 2
    x = jnp.where(step < half, mine_ref[...], other_ref[...])
    s = dot(x, cent_ref[...])
    peak = jnp.max(s, axis=1, keepdims=True)
    mass = jnp.sum(jnp.exp(s - peak), axis=1, keepdims=True)
    local = jnp.concatenate(
        [jnp.broadcast_to(local_ref[b], (SEQ, SEQ)).T[:, 0:1] for b in range(rows // SEQ)], axis=0
    )
    picked = jnp.sum(jnp.where(local == iota((rows, block), 1), s, 0.0), axis=1, keepdims=True)
    both = jnp.where(iota((rows, 128), 1) == 0, peak + jnp.log(mass), picked)
    for b in range(rows // SEQ):
        out_ref[b] = both[b * SEQ : (b + 1) * SEQ, :].T[0:8, :]

    @pl.when(step == pl.num_programs(0) - 1)
    def _():
        per = old_ref.shape[0]
        old = cent_ref[:, pl.ds(pl.multiple_of(info_ref[2] * per, per), per)]
        old_ref[...] = old.astype(F32).T


def scored(info, mine, other, local, parts):
    tokens, width = mine.shape
    block = parts[0].shape[1]
    step = 2 * SEQ
    per = step // SEQ
    half = tokens // step
    return pl.pallas_call(
        score_kernel,
        grid=(2 * half,),
        out_shape=(
            jax.ShapeDtypeStruct((2 * tokens // SEQ, 8, SEQ), F32),
            jax.ShapeDtypeStruct((SEQ, width), F32),
        ),
        in_specs=[
            pl.BlockSpec(memory_space=pltpu.SMEM),
            pl.BlockSpec((step, width), lambda i: (jnp.minimum(i, half - 1), 0)),
            pl.BlockSpec((step, width), lambda i: (jnp.maximum(i - half, 0), 0)),
            pl.BlockSpec((per, 1, SEQ), lambda i: (i, 0, 0)),
        ]
        + [pl.BlockSpec(memory_space=pl.ANY)] * len(parts),
        out_specs=(
            pl.BlockSpec((per, 8, SEQ), lambda i: (i, 0, 0)),
            pl.BlockSpec((SEQ, width), lambda i: (0, 0)),
        ),
        scratch_shapes=[
            pltpu.VMEM((width, block), BF16),
            pltpu.SemaphoreType.DMA((16,)),
        ],
        compiler_params=pltpu.CompilerParams(vmem_limit_bytes=40 << 20),
    )(info, mine, other, local.reshape(2 * tokens // SEQ, 1, SEQ), *parts)


def pack_kernel(info_ref, local_ref, mine_ref, other_ref, out_ref, hits_ref):
    dests, _, width = out_ref.shape
    per = 128
    tokens = local_ref.shape[1]
    first_slot = info_ref[1] * SLOTS
    local = local_ref[...]
    upper = iota((per, per), 0) < iota((per, per), 1)
    diagonal = iota((per, per), 0) == iota((per, per), 1)

    def group(g, most):
        match = jnp.where(local - g * per == iota((per, tokens), 0), 1.0, 0.0)
        hits = match.astype(BF16)
        present = jnp.broadcast_to(jnp.max(match, axis=1, keepdims=True), (per, per))
        rank = jnp.sum(jnp.where(upper, present, 0.0), axis=0, keepdims=True).astype(jnp.int32)
        here = jnp.sum(jnp.where(diagonal, present, 0.0), axis=0, keepdims=True)
        slot = iota((ROOM, per), 0)
        chosen = (slot < SLOTS) & (slot == rank - first_slot) & (here > 0.5)
        packing = jnp.where(chosen, 1.0, 0.0).astype(BF16)
        hits_ref[pl.ds(pl.multiple_of(g * ROOM, ROOM), ROOM), :] = dot(packing, hits).astype(BF16)
        return jnp.maximum(most, jnp.sum(here, axis=1, keepdims=True))

    most = lax.fori_loop(0, dests, group, jnp.zeros((1, 1), F32), unroll=4)
    half = tokens // 2
    sums = dot(hits_ref[:, 0:half], mine_ref[...]) + dot(hits_ref[:, half:], other_ref[...])
    sums = sums.reshape(dests, ROOM, width)[:, 0:BLOCK, :]
    last = iota((dests, BLOCK, width), 1) == SLOTS
    out_ref[...] = jnp.where(last, most.reshape(1, 1, 1), sums).astype(BF16)


def packed_sums(info, local, mine, other, dests):
    tokens = local.shape[1]
    width = mine.shape[1]
    return pl.pallas_call(
        pack_kernel,
        out_shape=jax.ShapeDtypeStruct((dests, BLOCK, width), BF16),
        in_specs=[pl.BlockSpec(memory_space=pltpu.SMEM)]
        + [pl.BlockSpec(memory_space=pltpu.VMEM)] * 3,
        out_specs=pl.BlockSpec(memory_space=pltpu.VMEM),
        scratch_shapes=[pltpu.VMEM((dests * ROOM, tokens), BF16)],
        compiler_params=pltpu.CompilerParams(vmem_limit_bytes=48 << 20),
    )(info, local, mine, other)


def count_kernel(info_ref, assign_ref, out_ref):
    dp, slabs, _ = assign_ref.shape
    targets = iota((128, SEQ), 0) + info_ref[0]
    lane = iota(out_ref.shape, 1)

    def slab(f, out):
        acc = jnp.zeros((128, SEQ), F32)
        for d in range(dp):
            acc = acc + jnp.where(assign_ref[d, pl.ds(f, 1), :] == targets, 1.0, 0.0)
        return jnp.where(lane == f, jnp.sum(acc, axis=1, keepdims=True), out)

    out_ref[...] = lax.fori_loop(0, slabs, slab, jnp.zeros(out_ref.shape, F32))


def counted(info, assign):
    return pl.pallas_call(
        count_kernel,
        out_shape=jax.ShapeDtypeStruct((128, 128), F32),
        in_specs=[pl.BlockSpec(memory_space=pltpu.SMEM), pl.BlockSpec(memory_space=pltpu.VMEM)],
        out_specs=pl.BlockSpec(memory_space=pltpu.VMEM),
    )(info, assign)


def unpack_kernel(info_ref, counts_ref, got_ref, out_ref):
    slabs, _, width = got_ref.shape
    counts = counts_ref[...]
    present = jnp.where(counts > 0.5, 1.0, 0.0).astype(BF16)
    lower = jnp.where(iota((128, 128), 1) < iota((128, 128), 0), 1.0, 0.0).astype(BF16)
    rank = dot(lower, present).astype(jnp.int32) - info_ref[1] * SLOTS
    slot = iota((128, BLOCK), 1)
    parts = []
    for f in range(slabs):
        chosen = (slot == rank[:, f : f + 1]) & (slot < SLOTS) & (counts[:, f : f + 1] > 0.5)
        parts.append(jnp.where(chosen, 1.0, 0.0))
    hits = jnp.concatenate(parts, axis=1).astype(BF16)
    out_ref[...] = dot(hits, got_ref[...].reshape(slabs * BLOCK, width))


def unpacked_sums(info, counts, got):
    return pl.pallas_call(
        unpack_kernel,
        out_shape=jax.ShapeDtypeStruct((128, got.shape[2]), F32),
        in_specs=[pl.BlockSpec(memory_space=pltpu.SMEM)]
        + [pl.BlockSpec(memory_space=pltpu.VMEM)] * 2,
        out_specs=pl.BlockSpec(memory_space=pltpu.VMEM),
    )(info, counts, got)


def exchanged(blocks, axis):
    return lax.all_to_all(blocks, axis, 0, 0, tiled=True)


def gathered(shard, axis):
    devices = lax.axis_size(axis)
    return exchanged(jnp.broadcast_to(shard[None], (devices,) + shard.shape), axis)


def swapped(shard, axis):
    return lax.ppermute(shard, axis, [(0, 1), (1, 0)])


def turned(shard, axis, by):
    devices = lax.axis_size(axis)
    return lax.ppermute(shard, axis, [(i, (i + by) % devices) for i in range(devices)])


def backwards(values, here):
    for dim, at in enumerate(here):
        size = values.shape[dim]
        values = jnp.take(values, (at - jnp.arange(size)) % size, axis=dim)
    return values


def shards(token_ids, embed_table, w_qkv, w_out, ln_gain, ln_bias, centroids_t, assignments):
    core = lax.axis_index("core")
    dp_rank = lax.axis_index(DP)
    fs_rank = lax.axis_index(FS)
    fs_size = lax.axis_size(FS)
    dp_size = lax.axis_size(DP)
    x_size = lax.axis_size("x")
    vocab, width = embed_table.shape
    zero = jnp.int32(0)
    ids = token_ids.reshape(fs_size, SEQ)

    at_x = lax.axis_index("x")

    rows = [centroids_t] + [turned(centroids_t, "zl", k) for k in range(1, 4)]

    part = (w_qkv.shape[1] + w_out.shape[1]) // (2 * x_size)
    both = jnp.concatenate([w_qkv, w_out], axis=1)
    piece = lax.dynamic_slice_in_dim(both, (core * x_size + at_x) * part, part, 1)
    column = gathered(piece, FS).reshape(width, part)

    def info_of(*values):
        return jnp.stack(values).astype(jnp.int32)

    my_row = lax.dynamic_slice_in_dim(ids, fs_rank, 1, 0)
    vocab_arr = jnp.full((1,), vocab, jnp.int32)
    sent, most = listed_rows(info_of(fs_rank, zero), ids, embed_table)
    sent, column, *rows = lax.optimization_barrier((sent, column, *rows))
    mine_w = [column] + [turned(column, "x", k) for k in range(1, x_size)]
    got = exchanged(sent, FS)
    inputs = expanded(info_of(fs_rank, zero), my_row, vocab_arr, got)

    def more_rows(state):
        turn, acc = state
        info = info_of(fs_rank, turn)
        again, _ = listed_rows(info, ids, embed_table)
        return turn + 1, acc + expanded(info, my_row, vocab_arr, exchanged(again, FS))

    most = most[0, 0]
    _, inputs = lax.while_loop(
        lambda state: state[0] * LIST < most, more_rows, (jnp.int32(1), inputs)
    )

    two = jnp.concatenate([inputs, swapped(inputs, "zh")], axis=0)
    other_w = [swapped(w, "core") for w in mine_w]

    near = jnp.concatenate(rows, axis=0)
    back = turned(near, "y", 1)
    ahead = turned(near, "y", 3)
    two, back, ahead = lax.optimization_barrier((two, back, ahead))
    pieces = [two] + [turned(two, "x", k) for k in range(1, x_size)]
    half = near.shape[0] // 2
    far_low = turned(back[:half], "y", 1)
    far_high = turned(ahead[half:], "y", 3)
    two, far_low, far_high = lax.optimization_barrier((two, far_low, far_high))
    pieces[0] = two

    mine = encoded(info_of(core, at_x), pieces, mine_w + other_w, ln_gain, ln_bias)
    other = swapped(mine, "core")

    by_dev = assignments.reshape(2, x_size, 2, fs_size, SEQ)
    of_slab = lax.dynamic_index_in_dim(by_dev, fs_rank, 3, keepdims=False)
    of_slab = jnp.transpose(of_slab, (2, 1, 0, 3))
    here = (core, at_x, lax.axis_index("zh"))
    of_slab = backwards(of_slab, here)
    block = centroids_t.shape[1]
    local = of_slab.reshape(1, -1) - dp_rank * block

    counts = counted(
        info_of(dp_rank * block + fs_rank * (block // fs_size)),
        assignments.reshape(dp_size, fs_size, SEQ),
    )

    def one_turn(turn):
        info = info_of(zero, turn)
        got = exchanged(packed_sums(info, local, mine, other, fs_size), FS)
        return unpacked_sums(info, counts, got)

    packed = packed_sums(info_of(zero, zero), local, mine, other, fs_size)
    packed, mine, other = lax.optimization_barrier((packed, mine, other))
    got = exchanged(packed, FS)
    stats, previous = scored(
        info_of(lax.axis_index("y"), lax.axis_index("zl"), fs_rank),
        mine,
        other,
        local,
        rows + [back, far_low, far_high, ahead],
    )
    stats, got = lax.optimization_barrier((stats, got))
    stats = backwards(stats.reshape(2, x_size, 2, 8, SEQ), here)
    stats = jnp.transpose(stats, (2, 1, 0, 3, 4)).reshape(dp_size, 8, SEQ)
    sums = unpacked_sums(info_of(zero, zero), counts, got)
    widest = jnp.max(got[:, SLOTS, 0:1].astype(F32)).astype(jnp.int32)
    _, sums = lax.while_loop(
        lambda state: state[0] * SLOTS < widest,
        lambda state: (state[0] + 1, state[1] + one_turn(state[0])),
        (jnp.int32(1), sums),
    )

    home = exchanged(stats, DP)
    lse = home[:, 0, :]
    peak = jnp.max(lse, axis=0)
    token_loss = (
        jnp.log(jnp.sum(jnp.exp(lse - peak[None, :]), axis=0)) + peak - jnp.sum(home[:, 1, :], axis=0)
    )

    total = jnp.sum(counts[:, 0:fs_size], axis=1, keepdims=True)
    new_centroids = jnp.where(total > 0, sums / jnp.maximum(total, 1.0), previous)
    return token_loss, new_centroids


def solution(mesh):
    finer = Mesh(mesh.devices.reshape(2, 4, 2, 4, 4), ALL)
    placed = (P(DP), P(FS, None), P(FS, None), P(FS, None), P(), P(), P(FS, DP), P())
    return jax.shard_map(
        shards, mesh=finer, in_specs=placed, out_specs=(P(ALL), P(ALL, None)), check_vma=False
    )
```

```python
import jax
import jax.numpy as jnp
from jax import lax
from jax.experimental import pallas as pl
from jax.experimental.pallas import tpu as pltpu
from jax.sharding import Mesh
from jax.sharding import PartitionSpec as P

HEADS = 12
HEAD = 64
SEQ = 128
DP = ("zh", "x", "core")
FS = ("y", "zl")
ALL = DP + FS
LIST = 16
SLOTS = 39
BLOCK = SLOTS + 1
ROOM = 48
F32 = jnp.float32
BF16 = jnp.bfloat16


RING = ((0, 0, 2), (1, 0, 2), (2, 0, 1), (2, 1, 1), (3, 0, 2))


def iota(shape, dim):
    return lax.broadcasted_iota(jnp.int32, shape, dim)


def dot(a, b, dims=((1,), (0,))):
    return lax.dot_general(a, b, (dims, ((), ())), preferred_element_type=F32)


def lists_kernel(info_ref, ids_ref, table_ref, rows_ref, count_ref, found_ref):
    vocab = table_ref.shape[0]
    passages = ids_ref.shape[0]
    base = info_ref[0] * vocab
    first_slot = info_ref[1] * LIST
    earlier = iota((SEQ, SEQ), 0) < iota((SEQ, SEQ), 1)
    later = iota((SEQ, SEQ), 0) > iota((SEQ, SEQ), 1)
    owners = iota((passages, SEQ), 0) * vocab

    def passage(p, most):
        row = ids_ref[pl.ds(p, 1), :]
        across = jnp.broadcast_to(row, (SEQ, SEQ))
        down = across.T
        same = across == down
        new_row = jnp.max(jnp.where(same & earlier, 1.0, 0.0), axis=0, keepdims=True) < 0.5
        new_down = jnp.max(jnp.where(same & later, 1.0, 0.0), axis=1, keepdims=True) < 0.5
        mine_down = (down >= base) & (down < base + vocab)
        before = jnp.where(new_down & mine_down & (down < across), 1.0, 0.0)
        slot = jnp.sum(before, axis=0, keepdims=True).astype(jnp.int32) - first_slot
        mine = (row >= base) & (row < base + vocab)
        chosen = (iota((LIST, SEQ), 0) == slot) & mine
        found = jnp.max(jnp.where(chosen, row - base, -1).astype(F32), axis=1, keepdims=True)
        found_ref[pl.ds(pl.multiple_of(p * LIST, LIST), LIST), :] = jnp.broadcast_to(found, (LIST, 128))
        held = (row >= owners) & (row < owners + vocab) & new_row
        return jnp.maximum(most, jnp.sum(jnp.where(held, 1.0, 0.0), axis=1, keepdims=True))

    most = lax.fori_loop(0, passages, passage, jnp.zeros((passages, 1), F32), unroll=4)
    wanted = found_ref[:, 0:1].astype(jnp.int32)
    whole = vocab // 16 * 16
    hits = jnp.where(wanted == iota((wanted.shape[0], whole), 1), 1.0, 0.0).astype(BF16)
    rows = dot(hits, table_ref[0:whole, :])
    if whole < vocab:
        tail = table_ref[whole:vocab, :].astype(F32)
        for k in range(vocab - whole):
            rows = rows + jnp.where(wanted == whole + k, tail[k : k + 1, :], 0.0)
    rows_ref[...] = rows.astype(BF16).reshape(rows_ref.shape)
    count_ref[...] = jnp.broadcast_to(jnp.max(most, axis=0, keepdims=True), count_ref.shape).astype(
        jnp.int32
    )


def listed_rows(info, ids, table):
    passages = ids.shape[0]
    return pl.pallas_call(
        lists_kernel,
        out_shape=(
            jax.ShapeDtypeStruct((passages, LIST, table.shape[1]), BF16),
            jax.ShapeDtypeStruct((8, 128), jnp.int32),
        ),
        in_specs=[
            pl.BlockSpec(memory_space=pltpu.SMEM),
            pl.BlockSpec(memory_space=pltpu.VMEM),
            pl.BlockSpec(memory_space=pltpu.VMEM),
        ],
        out_specs=(pl.BlockSpec(memory_space=pltpu.VMEM), pl.BlockSpec(memory_space=pltpu.VMEM)),
        scratch_shapes=[pltpu.VMEM((passages * LIST, 128), F32)],
        compiler_params=pltpu.CompilerParams(vmem_limit_bytes=40 << 20),
    )(info, ids, table)


def expand_kernel(info_ref, row_ref, vocab_ref, got_ref, out_ref):
    owners, _, width = got_ref.shape
    vocab = vocab_ref[0]
    first_slot = info_ref[1] * LIST
    row = row_ref[...]
    across = jnp.broadcast_to(row, (SEQ, SEQ))
    down = across.T

    def owner_of(ids):
        owner = jnp.zeros(ids.shape, jnp.int32)
        for k in range(1, owners):
            owner = owner + jnp.where(ids >= k * vocab, 1, 0)
        return owner

    owner_across = jnp.broadcast_to(owner_of(row), (SEQ, SEQ))
    owner_down = owner_across.T
    earlier = iota((SEQ, SEQ), 0) < iota((SEQ, SEQ), 1)
    new_row = jnp.max(jnp.where((across == down) & earlier, 1.0, 0.0), axis=0, keepdims=True) < 0.5
    before = jnp.where(new_row & (owner_across == owner_down) & (across < down), 1.0, 0.0)
    slot = jnp.sum(before, axis=1, keepdims=True).astype(jnp.int32) - first_slot
    place = owner_down[:, 0:1] * LIST + slot
    place = jnp.where((slot >= 0) & (slot < LIST), place, -1)
    hits = jnp.where(place == iota((SEQ, owners * LIST), 1), 1.0, 0.0).astype(BF16)
    out_ref[...] = dot(hits, got_ref[...].reshape(owners * LIST, width)).astype(BF16)


def expanded(info, row, vocab, got):
    return pl.pallas_call(
        expand_kernel,
        out_shape=jax.ShapeDtypeStruct((SEQ, got.shape[2]), BF16),
        in_specs=[
            pl.BlockSpec(memory_space=pltpu.SMEM),
            pl.BlockSpec(memory_space=pltpu.VMEM),
            pl.BlockSpec(memory_space=pltpu.SMEM),
            pl.BlockSpec(memory_space=pltpu.VMEM),
        ],
        out_specs=pl.BlockSpec(memory_space=pltpu.VMEM),
    )(info, row, vocab, got)


def put(sources, targets, sems):
    copies = [
        pltpu.make_async_copy(src, dst, sems.at[k])
        for k, (src, dst) in enumerate(zip(sources, targets, strict=True))
    ]
    for c in copies:
        c.start()
    for c in copies:
        c.wait()


def encode_kernel(info_ref, *refs):
    x_size = 4
    x_parts, w_parts = refs[0 : 2 * x_size], refs[2 * x_size : 2 * x_size + 10]
    gain_ref, bias_ref, out_ref = refs[2 * x_size + 10 : 2 * x_size + 13]
    x_ref, w_ref, packed_ref, scores_ref, probs_ref, context_ref, sems = refs[2 * x_size + 13 :]
    core, at_x = info_ref[0], info_ref[1]
    depth = w_ref.shape[1]
    places = []
    for side in (core, 1 - core):
        for back, first, count in RING:
            place = side * x_size + lax.rem(at_x - back + x_size, x_size)
            places.append(w_ref.at[place, pl.ds(first * (depth // 2), count * (depth // 2)), :])
    put(
        x_parts + w_parts,
        [x_ref.at[k, pl.ds(z * SEQ, SEQ), :] for z in range(2) for k in range(x_size)] + places,
        sems,
    )
    part = w_ref.shape[2]
    tokens, width = x_ref.shape[1:]
    left = iota((SEQ, 2 * HEAD), 1) < HEAD
    zero = jnp.zeros((SEQ, 2 * HEAD), BF16)
    pairs = HEADS // 2
    passages = tokens // SEQ

    def stacked(values):
        return jnp.concatenate([jnp.where(left, values, zero), jnp.where(left, zero, values)], axis=0)

    def step(i, _):
        x = x_ref[i]
        for j in range(6):
            packed_ref[:, j * part : (j + 1) * part] = dot(x, w_ref[j]).astype(BF16)
        for b in range(passages):
            rows = slice(b * SEQ, (b + 1) * SEQ)
            for pair in range(pairs):
                at = pair * 2 * HEAD
                q = packed_ref[rows, at : at + 2 * HEAD] * jnp.asarray(HEAD**-0.5, BF16)
                k = packed_ref[rows, width + at : width + at + 2 * HEAD]
                scores_ref[b * pairs + pair] = dot(q, stacked(k), ((1,), (1,)))
        for n in range(passages * pairs):
            for h in range(2):
                s = scores_ref[n, :, h * SEQ : (h + 1) * SEQ]
                e = jnp.exp(s - jnp.max(s, axis=1, keepdims=True))
                probs = e * (1.0 / jnp.sum(e, axis=1, keepdims=True))
                probs_ref[n, :, h * SEQ : (h + 1) * SEQ] = probs.astype(BF16)
        for b in range(passages):
            rows = slice(b * SEQ, (b + 1) * SEQ)
            for pair in range(pairs):
                at = pair * 2 * HEAD
                v = packed_ref[rows, 2 * width + at : 2 * width + at + 2 * HEAD]
                context_ref[rows, at : at + 2 * HEAD] = dot(
                    probs_ref[b * pairs + pair], stacked(v)
                ).astype(BF16)
        context = context_ref[...]
        half = width // 2
        mixed = [
            dot(context, w_ref[6 + k]) + x[:, k * half : (k + 1) * half].astype(F32) for k in range(2)
        ]
        mean = sum(jnp.sum(m, axis=1, keepdims=True) for m in mixed) * (1.0 / width)
        center = [m - mean for m in mixed]
        spread = sum(jnp.sum(c * c, axis=1, keepdims=True) for c in center) * (1.0 / width)
        scale = lax.rsqrt(spread + 1e-05)
        for k in range(2):
            cols = slice(k * half, (k + 1) * half)
            out_ref[pl.ds(i * tokens, tokens), cols] = (
                center[k] * scale * gain_ref[:, cols] + bias_ref[:, cols]
            ).astype(BF16)
        return 0

    lax.fori_loop(0, x_size, step, 0)


def encoded(info, x_parts, w_parts, gain, bias):
    tokens, width = 2 * SEQ, x_parts[0].shape[1]
    chunks = len(x_parts) // 2
    depth, part = w_parts[0].shape
    count = len(x_parts) + len(w_parts)
    pairs = tokens // SEQ * HEADS // 2
    return pl.pallas_call(
        encode_kernel,
        out_shape=jax.ShapeDtypeStruct((chunks * tokens, width), BF16),
        in_specs=[pl.BlockSpec(memory_space=pltpu.SMEM)]
        + [pl.BlockSpec(memory_space=pl.ANY)] * count
        + [pl.BlockSpec(memory_space=pltpu.VMEM)] * 2,
        out_specs=pl.BlockSpec(memory_space=pltpu.VMEM),
        scratch_shapes=[
            pltpu.VMEM((chunks, tokens, width), BF16),
            pltpu.VMEM((chunks * 2, depth, part), BF16),
            pltpu.VMEM((tokens, 3 * width), BF16),
            pltpu.VMEM((pairs, SEQ, 2 * SEQ), F32),
            pltpu.VMEM((pairs, SEQ, 2 * SEQ), BF16),
            pltpu.VMEM((tokens, width), BF16),
            pltpu.SemaphoreType.DMA((count,)),
        ],
        compiler_params=pltpu.CompilerParams(vmem_limit_bytes=40 << 20),
    )(info, *x_parts, *w_parts, gain.reshape(1, width), bias.reshape(1, width))


def score_kernel(info_ref, mine_ref, other_ref, local_ref, *refs):
    parts = refs[0:5]
    out_ref, old_ref, cent_ref, sems = refs[5:]
    quarters = 4
    step = pl.program_id(0)

    @pl.when(step == 0)
    def _():
        shard = parts[0].shape[0] // quarters
        sources, targets = [], []
        for ref, (back, first, count) in zip(parts, RING, strict=True):
            owner = lax.rem(info_ref[0] - back + 4, 4) * quarters
            for k in range(2 * count):
                place = owner + lax.rem(info_ref[2] - 2 * first - k + quarters, quarters)
                sources.append(ref.at[pl.ds(k * shard, shard), :])
                targets.append(cent_ref.at[pl.ds(pl.multiple_of(place * shard, shard), shard), :])
        put(sources, targets, sems)

    rows = mine_ref.shape[0]
    block = cent_ref.shape[1]
    half = pl.num_programs(0) // 2
    x = jnp.where(step < half, mine_ref[...], other_ref[...])
    s = dot(x, cent_ref[...])
    peak = jnp.max(s, axis=1, keepdims=True)
    mass = jnp.sum(jnp.exp(s - peak), axis=1, keepdims=True)
    local = jnp.concatenate(
        [jnp.broadcast_to(local_ref[b], (SEQ, SEQ)).T[:, 0:1] for b in range(rows // SEQ)], axis=0
    )
    picked = jnp.sum(jnp.where(local == iota((rows, block), 1), s, 0.0), axis=1, keepdims=True)
    both = jnp.where(iota((rows, 128), 1) == 0, peak + jnp.log(mass), picked)
    for b in range(rows // SEQ):
        out_ref[b] = both[b * SEQ : (b + 1) * SEQ, :].T[0:8, :]

    @pl.when(step == pl.num_programs(0) - 1)
    def _():
        per = old_ref.shape[0]
        old = cent_ref[:, pl.ds(pl.multiple_of(info_ref[1] * per, per), per)]
        old_ref[...] = old.astype(F32).T


def scored(info, mine, other, local, parts):
    tokens, width = mine.shape
    block = parts[0].shape[1]
    step = 2 * SEQ
    per = step // SEQ
    half = tokens // step
    return pl.pallas_call(
        score_kernel,
        grid=(2 * half,),
        out_shape=(
            jax.ShapeDtypeStruct((2 * tokens // SEQ, 8, SEQ), F32),
            jax.ShapeDtypeStruct((SEQ, width), F32),
        ),
        in_specs=[
            pl.BlockSpec(memory_space=pltpu.SMEM),
            pl.BlockSpec((step, width), lambda i: (jnp.minimum(i, half - 1), 0)),
            pl.BlockSpec((step, width), lambda i: (jnp.maximum(i - half, 0), 0)),
            pl.BlockSpec((per, 1, SEQ), lambda i: (i, 0, 0)),
        ]
        + [pl.BlockSpec(memory_space=pl.ANY)] * len(parts),
        out_specs=(
            pl.BlockSpec((per, 8, SEQ), lambda i: (i, 0, 0)),
            pl.BlockSpec((SEQ, width), lambda i: (0, 0)),
        ),
        scratch_shapes=[
            pltpu.VMEM((width, block), BF16),
            pltpu.SemaphoreType.DMA((16,)),
        ],
        compiler_params=pltpu.CompilerParams(vmem_limit_bytes=40 << 20),
    )(info, mine, other, local.reshape(2 * tokens // SEQ, 1, SEQ), *parts)


def choose_kernel(info_ref, local_ref, out_ref, most_ref):
    tokens = local_ref.shape[1]
    per = 128
    dests = out_ref.shape[0] // ROOM
    first_slot = info_ref[1] * SLOTS
    local = local_ref[...]
    upper = iota((per, per), 0) < iota((per, per), 1)
    diagonal = iota((per, per), 0) == iota((per, per), 1)

    def group(g, most):
        match = jnp.where(local - g * per == iota((per, tokens), 0), 1.0, 0.0)
        hits = match.astype(BF16)
        present = jnp.broadcast_to(jnp.max(match, axis=1, keepdims=True), (per, per))
        rank = jnp.sum(jnp.where(upper, present, 0.0), axis=0, keepdims=True).astype(jnp.int32)
        here = jnp.sum(jnp.where(diagonal, present, 0.0), axis=0, keepdims=True)
        slot = iota((ROOM, per), 0)
        chosen = (slot < SLOTS) & (slot == rank - first_slot) & (here > 0.5)
        packing = jnp.where(chosen, 1.0, 0.0).astype(BF16)
        out_ref[pl.ds(pl.multiple_of(g * ROOM, ROOM), ROOM), :] = dot(packing, hits).astype(BF16)
        return jnp.maximum(most, jnp.sum(here, axis=1, keepdims=True))

    most = lax.fori_loop(0, dests, group, jnp.zeros((1, 1), F32), unroll=4)
    most_ref[...] = jnp.broadcast_to(most, most_ref.shape)


def choices(info, local, dests):
    return pl.pallas_call(
        choose_kernel,
        out_shape=(
            jax.ShapeDtypeStruct((dests * ROOM, local.shape[1]), BF16),
            jax.ShapeDtypeStruct((8, 128), F32),
        ),
        in_specs=[pl.BlockSpec(memory_space=pltpu.SMEM), pl.BlockSpec(memory_space=pltpu.VMEM)],
        out_specs=(pl.BlockSpec(memory_space=pltpu.VMEM), pl.BlockSpec(memory_space=pltpu.VMEM)),
        compiler_params=pltpu.CompilerParams(vmem_limit_bytes=40 << 20),
    )(info, local)


def pack_kernel(hits_ref, most_ref, mine_ref, other_ref, out_ref):
    dests, _, width = out_ref.shape
    half = mine_ref.shape[0]
    sums = dot(hits_ref[:, 0:half], mine_ref[...]) + dot(hits_ref[:, half:], other_ref[...])
    sums = sums.reshape(dests, ROOM, width)[:, 0:BLOCK, :]
    last = iota((dests, BLOCK, width), 1) == SLOTS
    out_ref[...] = jnp.where(last, most_ref[0:1, 0:1].reshape(1, 1, 1), sums).astype(BF16)


def packed_sums(chosen, mine, other):
    hits, most = chosen
    width = mine.shape[1]
    return pl.pallas_call(
        pack_kernel,
        out_shape=jax.ShapeDtypeStruct((hits.shape[0] // ROOM, BLOCK, width), BF16),
        in_specs=[pl.BlockSpec(memory_space=pltpu.VMEM)] * 4,
        out_specs=pl.BlockSpec(memory_space=pltpu.VMEM),
        compiler_params=pltpu.CompilerParams(vmem_limit_bytes=40 << 20),
    )(hits, most, mine, other)


def count_kernel(info_ref, assign_ref, out_ref):
    dp, slabs, _ = assign_ref.shape
    targets = iota((128, SEQ), 0) + info_ref[0]
    lane = iota(out_ref.shape, 1)

    def slab(f, out):
        acc = jnp.zeros((128, SEQ), F32)
        for d in range(dp):
            acc = acc + jnp.where(assign_ref[d, pl.ds(f, 1), :] == targets, 1.0, 0.0)
        return jnp.where(lane == f, jnp.sum(acc, axis=1, keepdims=True), out)

    out_ref[...] = lax.fori_loop(0, slabs, slab, jnp.zeros(out_ref.shape, F32))


def counted(info, assign):
    return pl.pallas_call(
        count_kernel,
        out_shape=jax.ShapeDtypeStruct((128, 128), F32),
        in_specs=[pl.BlockSpec(memory_space=pltpu.SMEM), pl.BlockSpec(memory_space=pltpu.VMEM)],
        out_specs=pl.BlockSpec(memory_space=pltpu.VMEM),
    )(info, assign)


def unpack_kernel(info_ref, counts_ref, got_ref, out_ref):
    slabs, _, width = got_ref.shape
    counts = counts_ref[...]
    present = jnp.where(counts > 0.5, 1.0, 0.0).astype(BF16)
    lower = jnp.where(iota((128, 128), 1) < iota((128, 128), 0), 1.0, 0.0).astype(BF16)
    rank = dot(lower, present).astype(jnp.int32) - info_ref[1] * SLOTS
    slot = iota((128, BLOCK), 1)
    parts = []
    for f in range(slabs):
        chosen = (slot == rank[:, f : f + 1]) & (slot < SLOTS) & (counts[:, f : f + 1] > 0.5)
        parts.append(jnp.where(chosen, 1.0, 0.0))
    hits = jnp.concatenate(parts, axis=1).astype(BF16)
    out_ref[...] = dot(hits, got_ref[...].reshape(slabs * BLOCK, width))


def unpacked_sums(info, counts, got):
    return pl.pallas_call(
        unpack_kernel,
        out_shape=jax.ShapeDtypeStruct((128, got.shape[2]), F32),
        in_specs=[pl.BlockSpec(memory_space=pltpu.SMEM)]
        + [pl.BlockSpec(memory_space=pltpu.VMEM)] * 2,
        out_specs=pl.BlockSpec(memory_space=pltpu.VMEM),
    )(info, counts, got)


def exchanged(blocks, axis):
    return lax.all_to_all(blocks, axis, 0, 0, tiled=True)


def gathered(shard, axis):
    devices = lax.axis_size(axis)
    return exchanged(jnp.broadcast_to(shard[None], (devices,) + shard.shape), axis)


def swapped(shard, axis):
    return lax.ppermute(shard, axis, [(0, 1), (1, 0)])


def turned(shard, axis, by):
    devices = lax.axis_size(axis)
    return lax.ppermute(shard, axis, [(i, (i + by) % devices) for i in range(devices)])


def neighbours(block, axis):
    return turned(block, axis, 1), turned(block, axis, lax.axis_size(axis) - 1)


def far_halves(back, ahead, axis):
    half = back.shape[0] // 2
    return turned(back[:half], axis, 1), turned(ahead[half:], axis, lax.axis_size(axis) - 1)


def backwards(values, here):
    for dim, at in enumerate(here):
        size = values.shape[dim]
        values = jnp.take(values, (at - jnp.arange(size)) % size, axis=dim)
    return values


def shards(token_ids, embed_table, w_qkv, w_out, ln_gain, ln_bias, centroids_t, assignments):
    core = lax.axis_index("core")
    dp_rank = lax.axis_index(DP)
    fs_rank = lax.axis_index(FS)
    fs_size = lax.axis_size(FS)
    dp_size = lax.axis_size(DP)
    x_size = lax.axis_size("x")
    vocab, width = embed_table.shape
    zero = jnp.int32(0)
    ids = token_ids.reshape(fs_size, SEQ)

    at_x = lax.axis_index("x")

    def info_of(*values):
        return jnp.stack(values).astype(jnp.int32)

    by_dev = assignments.reshape(2, x_size, 2, fs_size, SEQ)
    of_slab = lax.dynamic_index_in_dim(by_dev, fs_rank, 3, keepdims=False)
    of_slab = jnp.transpose(of_slab, (2, 1, 0, 3))
    here = (core, at_x, lax.axis_index("zh"))
    of_slab = backwards(of_slab, here)
    block = centroids_t.shape[1]
    local = of_slab.reshape(1, -1) - dp_rank * block
    chosen = choices(info_of(zero, zero), local, fs_size)
    counts = counted(
        info_of(dp_rank * block + fs_rank * (block // fs_size)),
        assignments.reshape(dp_size, fs_size, SEQ),
    )

    part = (w_qkv.shape[1] + w_out.shape[1]) // (2 * x_size)
    both = jnp.concatenate([w_qkv, w_out], axis=1)
    piece = lax.dynamic_slice_in_dim(both, (core * x_size + at_x) * part, part, 1)
    column = gathered(piece, FS).reshape(width, part)

    my_row = lax.dynamic_slice_in_dim(ids, fs_rank, 1, 0)
    vocab_arr = jnp.full((1,), vocab, jnp.int32)
    sent, most = listed_rows(info_of(fs_rank, zero), ids, embed_table)
    sent, column = lax.optimization_barrier((sent, column))
    w_back, w_ahead = neighbours(column, "x")

    sent, start = lax.optimization_barrier((sent, centroids_t))
    rows = [start] + [turned(start, "zl", k) for k in range(1, 4)]

    got = exchanged(sent, FS)
    got, chosen = lax.optimization_barrier((got, chosen))
    inputs = expanded(info_of(fs_rank, zero), my_row, vocab_arr, got)

    def more_rows(state):
        turn, acc = state
        info = info_of(fs_rank, turn)
        again, _ = listed_rows(info, ids, embed_table)
        return turn + 1, acc + expanded(info, my_row, vocab_arr, exchanged(again, FS))

    most = most[0, 0]
    _, inputs = lax.while_loop(
        lambda state: state[0] * LIST < most, more_rows, (jnp.int32(1), inputs)
    )

    inputs, w_back, w_ahead, *rows = lax.optimization_barrier((inputs, w_back, w_ahead, *rows))
    far = swapped(inputs, "zh")
    pieces = [inputs] + [turned(inputs, "x", k) for k in range(1, x_size)]
    mine_w = [column, w_back, *far_halves(w_back, w_ahead, "x"), w_ahead]
    other_w = [swapped(w, "core") for w in mine_w]

    near = jnp.concatenate(rows, axis=0)
    back, ahead = neighbours(near, "y")
    far, counts = lax.optimization_barrier((far, counts))
    pieces += [far] + [turned(far, "x", k) for k in range(1, x_size)]
    pieces[0], back, ahead = lax.optimization_barrier((inputs, back, ahead))
    far_low, far_high = far_halves(back, ahead, "y")

    mine = encoded(info_of(core, at_x), pieces, mine_w + other_w, ln_gain, ln_bias)
    mine, far_low, far_high = lax.optimization_barrier((mine, far_low, far_high))
    other = swapped(mine, "core")

    def one_turn(turn):
        info = info_of(zero, turn)
        got = exchanged(packed_sums(choices(info, local, fs_size), mine, other), FS)
        return unpacked_sums(info, counts, got)

    packed = packed_sums(chosen, mine, other)
    packed, mine, other = lax.optimization_barrier((packed, mine, other))
    got = exchanged(packed, FS)

    stats, previous = scored(
        info_of(lax.axis_index("y"), fs_rank, lax.axis_index("zl")),
        mine,
        other,
        local,
        [near, back, far_low, far_high, ahead],
    )
    stats, got = lax.optimization_barrier((stats, got))
    stats = backwards(stats.reshape(2, x_size, 2, 8, SEQ), here)
    stats = jnp.transpose(stats, (2, 1, 0, 3, 4)).reshape(dp_size, 8, SEQ)
    sums = unpacked_sums(info_of(zero, zero), counts, got)
    widest = jnp.max(got[:, SLOTS, 0:1].astype(F32)).astype(jnp.int32)
    _, sums = lax.while_loop(
        lambda state: state[0] * SLOTS < widest,
        lambda state: (state[0] + 1, state[1] + one_turn(state[0])),
        (jnp.int32(1), sums),
    )

    home = exchanged(stats, DP)
    lse = home[:, 0, :]
    peak = jnp.max(lse, axis=0)
    token_loss = (
        jnp.log(jnp.sum(jnp.exp(lse - peak[None, :]), axis=0)) + peak - jnp.sum(home[:, 1, :], axis=0)
    )

    total = jnp.sum(counts[:, 0:fs_size], axis=1, keepdims=True)
    new_centroids = jnp.where(total > 0, sums / jnp.maximum(total, 1.0), previous)
    return token_loss, new_centroids


def solution(mesh):
    finer = Mesh(mesh.devices.reshape(2, 4, 2, 4, 4), ALL)
    placed = (P(DP), P(FS, None), P(FS, None), P(FS, None), P(), P(), P(FS, DP), P())
    return jax.shard_map(
        shards, mesh=finer, in_specs=placed, out_specs=(P(ALL), P(ALL, None)), check_vma=False
    )
```

```python
import jax
import jax.numpy as jnp
from jax import lax
from jax.experimental import pallas as pl
from jax.experimental.pallas import tpu as pltpu
from jax.sharding import Mesh
from jax.sharding import PartitionSpec as P

HEADS = 12
HEAD = 64
SEQ = 128
DP = ("zh", "x", "core")
FS = ("y", "zl")
ALL = DP + FS
LIST = 16
SLOTS = 39
BLOCK = SLOTS + 1
ROOM = 48
F32 = jnp.float32
BF16 = jnp.bfloat16


RING = ((0, 0, 2), (1, 0, 2), (2, 0, 1), (2, 1, 1), (3, 0, 2))


def iota(shape, dim):
    return lax.broadcasted_iota(jnp.int32, shape, dim)


def dot(a, b, dims=((1,), (0,))):
    return lax.dot_general(a, b, (dims, ((), ())), preferred_element_type=F32)


def lists_kernel(info_ref, ids_ref, table_ref, rows_ref, count_ref, found_ref):
    vocab = table_ref.shape[0]
    passages = ids_ref.shape[0]
    base = info_ref[0] * vocab
    first_slot = info_ref[1] * LIST
    earlier = iota((SEQ, SEQ), 0) < iota((SEQ, SEQ), 1)
    later = iota((SEQ, SEQ), 0) > iota((SEQ, SEQ), 1)
    owners = iota((passages, SEQ), 0) * vocab

    def passage(p, most):
        row = ids_ref[pl.ds(p, 1), :]
        across = jnp.broadcast_to(row, (SEQ, SEQ))
        down = across.T
        same = across == down
        new_row = jnp.max(jnp.where(same & earlier, 1.0, 0.0), axis=0, keepdims=True) < 0.5
        new_down = jnp.max(jnp.where(same & later, 1.0, 0.0), axis=1, keepdims=True) < 0.5
        mine_down = (down >= base) & (down < base + vocab)
        before = jnp.where(new_down & mine_down & (down < across), 1.0, 0.0)
        slot = jnp.sum(before, axis=0, keepdims=True).astype(jnp.int32) - first_slot
        mine = (row >= base) & (row < base + vocab)
        chosen = (iota((LIST, SEQ), 0) == slot) & mine
        found = jnp.max(jnp.where(chosen, row - base, -1).astype(F32), axis=1, keepdims=True)
        found_ref[pl.ds(pl.multiple_of(p * LIST, LIST), LIST), :] = jnp.broadcast_to(found, (LIST, 128))
        held = (row >= owners) & (row < owners + vocab) & new_row
        return jnp.maximum(most, jnp.sum(jnp.where(held, 1.0, 0.0), axis=1, keepdims=True))

    most = lax.fori_loop(0, passages, passage, jnp.zeros((passages, 1), F32), unroll=4)
    wanted = found_ref[:, 0:1].astype(jnp.int32)
    whole = vocab // 16 * 16
    hits = jnp.where(wanted == iota((wanted.shape[0], whole), 1), 1.0, 0.0).astype(BF16)
    rows = dot(hits, table_ref[0:whole, :])
    if whole < vocab:
        tail = table_ref[whole:vocab, :].astype(F32)
        for k in range(vocab - whole):
            rows = rows + jnp.where(wanted == whole + k, tail[k : k + 1, :], 0.0)
    rows = rows.astype(BF16)
    half = rows_ref.shape[2]
    for side in range(2):
        rows_ref[:, side * LIST : (side + 1) * LIST, :] = rows[:, side * half : (side + 1) * half].reshape(
            passages, LIST, half
        )
    count_ref[...] = jnp.broadcast_to(jnp.max(most, axis=0, keepdims=True), count_ref.shape).astype(
        jnp.int32
    )


def lists_with_weights_kernel(info_ref, ids_ref, table_ref, qkv_ref, wout_ref, rows_ref, count_ref, found_ref):
    part = rows_ref.shape[2]
    column = info_ref[2] * part
    within = qkv_ref.shape[1]

    def spread(piece):
        for p in range(rows_ref.shape[0]):
            rows_ref[p, 2 * LIST :, :] = piece

    @pl.when(column < within)
    def _():
        spread(qkv_ref[:, pl.ds(pl.multiple_of(column, part), part)])

    @pl.when(column >= within)
    def _():
        spread(wout_ref[:, pl.ds(pl.multiple_of(column - within, part), part)])

    lists_kernel(info_ref, ids_ref, table_ref, rows_ref, count_ref, found_ref)


def listed_rows(info, ids, table, weights=()):
    passages = ids.shape[0]
    half = table.shape[1] // 2
    rows = 2 * LIST + (weights[0].shape[0] if weights else 0)
    return pl.pallas_call(
        lists_with_weights_kernel if weights else lists_kernel,
        out_shape=(
            jax.ShapeDtypeStruct((passages, rows, half), BF16),
            jax.ShapeDtypeStruct((8, 128), jnp.int32),
        ),
        in_specs=[pl.BlockSpec(memory_space=pltpu.SMEM)]
        + [pl.BlockSpec(memory_space=pltpu.VMEM)] * (2 + len(weights)),
        out_specs=(pl.BlockSpec(memory_space=pltpu.VMEM), pl.BlockSpec(memory_space=pltpu.VMEM)),
        scratch_shapes=[pltpu.VMEM((passages * LIST, 128), F32)],
        compiler_params=pltpu.CompilerParams(vmem_limit_bytes=40 << 20),
    )(info, ids, table, *weights)


def expand_kernel(info_ref, row_ref, got_ref, out_ref):
    owners, _, half = got_ref.shape
    vocab = info_ref[2]
    first_slot = info_ref[1] * LIST
    row = row_ref[...]
    across = jnp.broadcast_to(row, (SEQ, SEQ))
    down = across.T

    def owner_of(ids):
        owner = jnp.zeros(ids.shape, jnp.int32)
        for k in range(1, owners):
            owner = owner + jnp.where(ids >= k * vocab, 1, 0)
        return owner

    owner_across = jnp.broadcast_to(owner_of(row), (SEQ, SEQ))
    owner_down = owner_across.T
    earlier = iota((SEQ, SEQ), 0) < iota((SEQ, SEQ), 1)
    new_row = jnp.max(jnp.where((across == down) & earlier, 1.0, 0.0), axis=0, keepdims=True) < 0.5
    before = jnp.where(new_row & (owner_across == owner_down) & (across < down), 1.0, 0.0)
    slot = jnp.sum(before, axis=1, keepdims=True).astype(jnp.int32) - first_slot
    place = owner_down[:, 0:1] * LIST + slot
    place = jnp.where((slot >= 0) & (slot < LIST), place, -1)
    hits = jnp.where(place == iota((SEQ, owners * LIST), 1), 1.0, 0.0).astype(BF16)
    top = out_ref.shape[0] - 2 * SEQ
    if top:
        out_ref[0:top, :] = got_ref[:, 2 * LIST :, :].reshape(top, half)
    for side in range(2):
        rows = got_ref[:, side * LIST : (side + 1) * LIST, :].reshape(owners * LIST, half)
        out_ref[top + side * SEQ : top + (side + 1) * SEQ, :] = dot(hits, rows).astype(BF16)


def expanded(info, row, got):
    owners, rows, half = got.shape
    return pl.pallas_call(
        expand_kernel,
        out_shape=jax.ShapeDtypeStruct((owners * (rows - 2 * LIST) + 2 * SEQ, half), BF16),
        in_specs=[
            pl.BlockSpec(memory_space=pltpu.SMEM),
            pl.BlockSpec(memory_space=pltpu.VMEM),
            pl.BlockSpec(memory_space=pltpu.VMEM),
        ],
        out_specs=pl.BlockSpec(memory_space=pltpu.VMEM),
    )(info, row, got)


def put(sources, targets, sems):
    copies = [
        pltpu.make_async_copy(src, dst, sems.at[k])
        for k, (src, dst) in enumerate(zip(sources, targets, strict=True))
    ]
    for c in copies:
        c.start()
    for c in copies:
        c.wait()


def encode_kernel(info_ref, *refs):
    rings, fars = refs[0:10], refs[10:14]
    gain_ref, bias_ref, out_ref = refs[14:17]
    x_ref, w_ref, packed_ref, scores_ref, probs_ref, context_ref, sems = refs[17:]
    x_size = len(fars)
    core, at_x = info_ref[0], info_ref[1]
    depth, part = w_ref.shape[1:]
    joined = (depth + 2 * SEQ) // 2
    sources, targets = [], []

    def tokens_to(chunk, passage, ref, row):
        for side in range(2):
            sources.append(ref.at[pl.ds(row + side * SEQ, SEQ), :])
            targets.append(x_ref.at[chunk, pl.ds(passage * SEQ, SEQ), pl.ds(side * part, part)])

    for ref, (core_at, (back, first, count)) in zip(
        rings, [(c, r) for c in (core, 1 - core) for r in RING], strict=True
    ):
        place = core_at * x_size + lax.rem(at_x - back + x_size, x_size)
        start = first * joined
        rows = min(count * joined, depth - start)
        sources.append(ref.at[pl.ds(0, rows), :])
        targets.append(w_ref.at[place, pl.ds(start, rows), :])
    for ref, (back, first, count) in zip(rings[0:5], RING, strict=True):
        if (first + count) * joined > depth:
            tokens_to(back, 0, ref, depth - first * joined)
    for back, ref in enumerate(fars):
        tokens_to(back, 1, ref, 0)
    put(sources, targets, sems)
    tokens, width = x_ref.shape[1:]
    left = iota((SEQ, 2 * HEAD), 1) < HEAD
    zero = jnp.zeros((SEQ, 2 * HEAD), BF16)
    pairs = HEADS // 2
    passages = tokens // SEQ

    def stacked(values):
        return jnp.concatenate([jnp.where(left, values, zero), jnp.where(left, zero, values)], axis=0)

    def step(i, _):
        x = x_ref[i]
        for j in range(6):
            packed_ref[:, j * part : (j + 1) * part] = dot(x, w_ref[j]).astype(BF16)
        for b in range(passages):
            rows = slice(b * SEQ, (b + 1) * SEQ)
            for pair in range(pairs):
                at = pair * 2 * HEAD
                q = packed_ref[rows, at : at + 2 * HEAD] * jnp.asarray(HEAD**-0.5, BF16)
                k = packed_ref[rows, width + at : width + at + 2 * HEAD]
                scores_ref[b * pairs + pair] = dot(q, stacked(k), ((1,), (1,)))
        for n in range(passages * pairs):
            for h in range(2):
                s = scores_ref[n, :, h * SEQ : (h + 1) * SEQ]
                e = jnp.exp(s - jnp.max(s, axis=1, keepdims=True))
                probs = e * (1.0 / jnp.sum(e, axis=1, keepdims=True))
                probs_ref[n, :, h * SEQ : (h + 1) * SEQ] = probs.astype(BF16)
        for b in range(passages):
            rows = slice(b * SEQ, (b + 1) * SEQ)
            for pair in range(pairs):
                at = pair * 2 * HEAD
                v = packed_ref[rows, 2 * width + at : 2 * width + at + 2 * HEAD]
                context_ref[rows, at : at + 2 * HEAD] = dot(
                    probs_ref[b * pairs + pair], stacked(v)
                ).astype(BF16)
        context = context_ref[...]
        half = width // 2
        mixed = [
            dot(context, w_ref[6 + k]) + x[:, k * half : (k + 1) * half].astype(F32) for k in range(2)
        ]
        mean = sum(jnp.sum(m, axis=1, keepdims=True) for m in mixed) * (1.0 / width)
        center = [m - mean for m in mixed]
        spread = sum(jnp.sum(c * c, axis=1, keepdims=True) for c in center) * (1.0 / width)
        scale = lax.rsqrt(spread + 1e-05)
        for k in range(2):
            cols = slice(k * half, (k + 1) * half)
            out_ref[pl.ds(i * tokens, tokens), cols] = (
                center[k] * scale * gain_ref[:, cols] + bias_ref[:, cols]
            ).astype(BF16)
        return 0

    lax.fori_loop(0, x_size, step, 0)


def encoded(info, rings, fars, gain, bias):
    part = fars[0].shape[1]
    tokens, width, chunks = 2 * SEQ, 2 * part, len(fars)
    pairs = tokens // SEQ * HEADS // 2
    return pl.pallas_call(
        encode_kernel,
        out_shape=jax.ShapeDtypeStruct((chunks * tokens, width), BF16),
        in_specs=[pl.BlockSpec(memory_space=pltpu.SMEM)]
        + [pl.BlockSpec(memory_space=pl.ANY)] * (len(rings) + chunks)
        + [pl.BlockSpec(memory_space=pltpu.VMEM)] * 2,
        out_specs=pl.BlockSpec(memory_space=pltpu.VMEM),
        scratch_shapes=[
            pltpu.VMEM((chunks, tokens, width), BF16),
            pltpu.VMEM((chunks * 2, width, part), BF16),
            pltpu.VMEM((tokens, 3 * width), BF16),
            pltpu.VMEM((pairs, SEQ, 2 * SEQ), F32),
            pltpu.VMEM((pairs, SEQ, 2 * SEQ), BF16),
            pltpu.VMEM((tokens, width), BF16),
            pltpu.SemaphoreType.DMA((len(rings) + 4 * chunks,)),
        ],
        compiler_params=pltpu.CompilerParams(vmem_limit_bytes=40 << 20),
    )(info, *rings, *fars, gain.reshape(1, width), bias.reshape(1, width))


def score_kernel(info_ref, mine_ref, other_ref, local_ref, *refs):
    parts = refs[0:5]
    out_ref, old_ref, cent_ref, sems = refs[5:]
    step = pl.program_id(0)

    @pl.when(step == 0)
    def _():
        rows_of = parts[0].shape[0]
        targets = []
        for back, first, count in RING:
            start = lax.rem(info_ref[0] - back + 4, 4) * rows_of + first * (rows_of // 2)
            start = pl.multiple_of(start, rows_of // 2)
            targets.append(cent_ref.at[pl.ds(start, count * (rows_of // 2)), :])
        put(parts, targets, sems)

    rows = mine_ref.shape[0]
    block = cent_ref.shape[1]
    half = pl.num_programs(0) // 2
    x = jnp.where(step < half, mine_ref[...], other_ref[...])
    s = dot(x, cent_ref[...])
    peak = jnp.max(s, axis=1, keepdims=True)
    mass = jnp.sum(jnp.exp(s - peak), axis=1, keepdims=True)
    local = jnp.concatenate(
        [jnp.broadcast_to(local_ref[b], (SEQ, SEQ)).T[:, 0:1] for b in range(rows // SEQ)], axis=0
    )
    picked = jnp.sum(jnp.where(local == iota((rows, block), 1), s, 0.0), axis=1, keepdims=True)
    both = jnp.where(iota((rows, 128), 1) == 0, peak + jnp.log(mass), picked)
    for b in range(rows // SEQ):
        out_ref[b] = both[b * SEQ : (b + 1) * SEQ, :].T[0:8, :]

    @pl.when(step == pl.num_programs(0) - 1)
    def _():
        per = old_ref.shape[0]
        old = cent_ref[:, pl.ds(pl.multiple_of(info_ref[1] * per, per), per)]
        old_ref[...] = old.astype(F32).T


def scored(info, mine, other, local, parts):
    tokens, width = mine.shape
    block = parts[0].shape[1]
    step = 2 * SEQ
    per = step // SEQ
    half = tokens // step
    return pl.pallas_call(
        score_kernel,
        grid=(2 * half,),
        out_shape=(
            jax.ShapeDtypeStruct((2 * tokens // SEQ, 8, SEQ), F32),
            jax.ShapeDtypeStruct((SEQ, width), F32),
        ),
        in_specs=[
            pl.BlockSpec(memory_space=pltpu.SMEM),
            pl.BlockSpec((step, width), lambda i: (jnp.minimum(i, half - 1), 0)),
            pl.BlockSpec((step, width), lambda i: (jnp.maximum(i - half, 0), 0)),
            pl.BlockSpec((per, 1, SEQ), lambda i: (i, 0, 0)),
        ]
        + [pl.BlockSpec(memory_space=pl.ANY)] * len(parts),
        out_specs=(
            pl.BlockSpec((per, 8, SEQ), lambda i: (i, 0, 0)),
            pl.BlockSpec((SEQ, width), lambda i: (0, 0)),
        ),
        scratch_shapes=[
            pltpu.VMEM((width, block), BF16),
            pltpu.SemaphoreType.DMA((len(parts),)),
        ],
        compiler_params=pltpu.CompilerParams(vmem_limit_bytes=40 << 20),
    )(info, mine, other, local.reshape(2 * tokens // SEQ, 1, SEQ), *parts)


def choose_kernel(info_ref, local_ref, out_ref, most_ref):
    tokens = local_ref.shape[1]
    per = 128
    dests = out_ref.shape[0] // ROOM
    first_slot = info_ref[1] * SLOTS
    local = local_ref[...]
    upper = iota((per, per), 0) < iota((per, per), 1)
    diagonal = iota((per, per), 0) == iota((per, per), 1)

    def group(g, most):
        match = jnp.where(local - g * per == iota((per, tokens), 0), 1.0, 0.0)
        hits = match.astype(BF16)
        present = jnp.broadcast_to(jnp.max(match, axis=1, keepdims=True), (per, per))
        rank = jnp.sum(jnp.where(upper, present, 0.0), axis=0, keepdims=True).astype(jnp.int32)
        here = jnp.sum(jnp.where(diagonal, present, 0.0), axis=0, keepdims=True)
        slot = iota((ROOM, per), 0)
        chosen = (slot < SLOTS) & (slot == rank - first_slot) & (here > 0.5)
        packing = jnp.where(chosen, 1.0, 0.0).astype(BF16)
        out_ref[pl.ds(pl.multiple_of(g * ROOM, ROOM), ROOM), :] = dot(packing, hits).astype(BF16)
        return jnp.maximum(most, jnp.sum(here, axis=1, keepdims=True))

    most = lax.fori_loop(0, dests, group, jnp.zeros((1, 1), F32), unroll=4)
    most_ref[...] = jnp.broadcast_to(most, most_ref.shape)


def choices(info, local, dests):
    return pl.pallas_call(
        choose_kernel,
        out_shape=(
            jax.ShapeDtypeStruct((dests * ROOM, local.shape[1]), BF16),
            jax.ShapeDtypeStruct((8, 128), F32),
        ),
        in_specs=[pl.BlockSpec(memory_space=pltpu.SMEM), pl.BlockSpec(memory_space=pltpu.VMEM)],
        out_specs=(pl.BlockSpec(memory_space=pltpu.VMEM), pl.BlockSpec(memory_space=pltpu.VMEM)),
        compiler_params=pltpu.CompilerParams(vmem_limit_bytes=40 << 20),
    )(info, local)


def pack_kernel(hits_ref, most_ref, mine_ref, other_ref, out_ref):
    dests, _, width = out_ref.shape
    half = mine_ref.shape[0]
    sums = dot(hits_ref[:, 0:half], mine_ref[...]) + dot(hits_ref[:, half:], other_ref[...])
    sums = sums.reshape(dests, ROOM, width)[:, 0:BLOCK, :]
    last = iota((dests, BLOCK, width), 1) == SLOTS
    out_ref[...] = jnp.where(last, most_ref[0:1, 0:1].reshape(1, 1, 1), sums).astype(BF16)


def packed_sums(chosen, mine, other):
    hits, most = chosen
    width = mine.shape[1]
    return pl.pallas_call(
        pack_kernel,
        out_shape=jax.ShapeDtypeStruct((hits.shape[0] // ROOM, BLOCK, width), BF16),
        in_specs=[pl.BlockSpec(memory_space=pltpu.VMEM)] * 4,
        out_specs=pl.BlockSpec(memory_space=pltpu.VMEM),
        compiler_params=pltpu.CompilerParams(vmem_limit_bytes=40 << 20),
    )(hits, most, mine, other)


def count_kernel(info_ref, assign_ref, out_ref):
    dp, slabs, _ = assign_ref.shape
    targets = iota((128, SEQ), 0) + info_ref[0]
    lane = iota(out_ref.shape, 1)

    def slab(f, out):
        acc = jnp.zeros((128, SEQ), F32)
        for d in range(dp):
            acc = acc + jnp.where(assign_ref[d, pl.ds(f, 1), :] == targets, 1.0, 0.0)
        return jnp.where(lane == f, jnp.sum(acc, axis=1, keepdims=True), out)

    out_ref[...] = lax.fori_loop(0, slabs, slab, jnp.zeros(out_ref.shape, F32))


def counted(info, assign):
    return pl.pallas_call(
        count_kernel,
        out_shape=jax.ShapeDtypeStruct((128, 128), F32),
        in_specs=[pl.BlockSpec(memory_space=pltpu.SMEM), pl.BlockSpec(memory_space=pltpu.VMEM)],
        out_specs=pl.BlockSpec(memory_space=pltpu.VMEM),
    )(info, assign)


def unpack_kernel(info_ref, counts_ref, got_ref, out_ref):
    slabs, _, width = got_ref.shape
    counts = counts_ref[...]
    present = jnp.where(counts > 0.5, 1.0, 0.0).astype(BF16)
    lower = jnp.where(iota((128, 128), 1) < iota((128, 128), 0), 1.0, 0.0).astype(BF16)
    rank = dot(lower, present).astype(jnp.int32) - info_ref[1] * SLOTS
    slot = iota((128, BLOCK), 1)
    parts = []
    for f in range(slabs):
        chosen = (slot == rank[:, f : f + 1]) & (slot < SLOTS) & (counts[:, f : f + 1] > 0.5)
        parts.append(jnp.where(chosen, 1.0, 0.0))
    hits = jnp.concatenate(parts, axis=1).astype(BF16)
    out_ref[...] = dot(hits, got_ref[...].reshape(slabs * BLOCK, width))


def unpacked_sums(info, counts, got):
    return pl.pallas_call(
        unpack_kernel,
        out_shape=jax.ShapeDtypeStruct((128, got.shape[2]), F32),
        in_specs=[pl.BlockSpec(memory_space=pltpu.SMEM)]
        + [pl.BlockSpec(memory_space=pltpu.VMEM)] * 2,
        out_specs=pl.BlockSpec(memory_space=pltpu.VMEM),
    )(info, counts, got)


def exchanged(blocks, axis):
    return lax.all_to_all(blocks, axis, 0, 0, tiled=True)


def gathered(shard, axis):
    devices = lax.axis_size(axis)
    return exchanged(jnp.broadcast_to(shard[None], (devices,) + shard.shape), axis)


def swapped(shard, axis):
    return lax.ppermute(shard, axis, [(0, 1), (1, 0)])


def turned(shard, axis, by):
    devices = lax.axis_size(axis)
    return lax.ppermute(shard, axis, [(i, (i + by) % devices) for i in range(devices)])


def neighbours(block, axis):
    return turned(block, axis, 1), turned(block, axis, lax.axis_size(axis) - 1)


def far_halves(back, ahead, axis):
    half = back.shape[0] // 2
    return turned(back[:half], axis, 1), turned(ahead[half:], axis, lax.axis_size(axis) - 1)


def backwards(values, here):
    for dim, at in enumerate(here):
        size = values.shape[dim]
        values = jnp.take(values, (at - jnp.arange(size)) % size, axis=dim)
    return values


def shards(token_ids, embed_table, w_qkv, w_out, ln_gain, ln_bias, centroids_t, assignments):
    core = lax.axis_index("core")
    dp_rank = lax.axis_index(DP)
    fs_rank = lax.axis_index(FS)
    fs_size = lax.axis_size(FS)
    dp_size = lax.axis_size(DP)
    x_size = lax.axis_size("x")
    vocab, width = embed_table.shape
    zero = jnp.int32(0)
    ids = token_ids.reshape(fs_size, SEQ)

    at_x = lax.axis_index("x")

    def info_of(*values):
        return jnp.stack(values).astype(jnp.int32)

    by_dev = assignments.reshape(2, x_size, 2, fs_size, SEQ)
    of_slab = lax.dynamic_index_in_dim(by_dev, fs_rank, 3, keepdims=False)
    of_slab = jnp.transpose(of_slab, (2, 1, 0, 3))
    here = (core, at_x, lax.axis_index("zh"))
    of_slab = backwards(of_slab, here)
    block = centroids_t.shape[1]
    local = of_slab.reshape(1, -1) - dp_rank * block
    chosen = choices(info_of(zero, zero), local, fs_size)
    counts = counted(
        info_of(dp_rank * block + fs_rank * (block // fs_size)),
        assignments.reshape(dp_size, fs_size, SEQ),
    )

    my_row = lax.dynamic_slice_in_dim(ids, fs_rank, 1, 0)
    my_column = core * x_size + at_x
    sent, most = listed_rows(info_of(fs_rank, zero, my_column), ids, embed_table, (w_qkv, w_out))
    got = exchanged(sent, FS)
    got, chosen, counts, my_row = lax.optimization_barrier((got, chosen, counts, my_row))
    ring = expanded(info_of(fs_rank, zero, vocab), my_row, got)

    def more_rows(state):
        turn, acc = state
        again, _ = listed_rows(info_of(fs_rank, turn, my_column), ids, embed_table)
        extra = expanded(info_of(fs_rank, turn, vocab), my_row, exchanged(again, FS))
        return turn + 1, acc.at[width:, :].add(extra)

    most = most[0, 0]
    _, ring = lax.while_loop(lambda state: state[0] * LIST < most, more_rows, (jnp.int32(1), ring))

    far = swapped(ring[width:], "zh")
    back, ahead = neighbours(ring, "x")
    rings = [ring, back, *far_halves(back, ahead, "x"), ahead]
    fars = [far] + [turned(far, "x", k) for k in range(1, x_size)]
    rings += [swapped(piece, "core") for piece in rings]

    shard, _ = lax.optimization_barrier((centroids_t, ring))
    near = gathered(shard, "zl").reshape(-1, block)
    fars[0], near = lax.optimization_barrier((fars[0], near))
    back, ahead = neighbours(near, "y")
    far_low, far_high = far_halves(back, ahead, "y")

    mine = encoded(info_of(core, at_x), rings, fars, ln_gain, ln_bias)
    mine, far_low, far_high = lax.optimization_barrier((mine, far_low, far_high))
    other = swapped(mine, "core")

    def one_turn(turn):
        info = info_of(zero, turn)
        got = exchanged(packed_sums(choices(info, local, fs_size), mine, other), FS)
        return unpacked_sums(info, counts, got)

    packed = packed_sums(chosen, mine, other)
    packed, mine, other = lax.optimization_barrier((packed, mine, other))
    got = exchanged(packed, FS)

    stats, previous = scored(
        info_of(lax.axis_index("y"), fs_rank),
        mine,
        other,
        local,
        [near, back, far_low, far_high, ahead],
    )
    stats = backwards(stats.reshape(2, x_size, 2, 8, SEQ), here)
    stats = jnp.transpose(stats, (2, 1, 0, 3, 4)).reshape(dp_size, 8, SEQ)
    stats, got = lax.optimization_barrier((stats, got))
    sums = unpacked_sums(info_of(zero, zero), counts, got)
    widest = jnp.max(got[:, SLOTS, 0:1].astype(F32)).astype(jnp.int32)
    _, sums = lax.while_loop(
        lambda state: state[0] * SLOTS < widest,
        lambda state: (state[0] + 1, state[1] + one_turn(state[0])),
        (jnp.int32(1), sums),
    )

    home = exchanged(stats, DP)
    lse = home[:, 0, :]
    peak = jnp.max(lse, axis=0)
    token_loss = (
        jnp.log(jnp.sum(jnp.exp(lse - peak[None, :]), axis=0)) + peak - jnp.sum(home[:, 1, :], axis=0)
    )

    total = jnp.sum(counts[:, 0:fs_size], axis=1, keepdims=True)
    new_centroids = jnp.where(total > 0, sums / jnp.maximum(total, 1.0), previous)
    return token_loss, new_centroids


def solution(mesh):
    finer = Mesh(mesh.devices.reshape(2, 4, 2, 4, 4), ALL)
    placed = (P(DP), P(FS, None), P(FS, None), P(FS, None), P(), P(), P(FS, DP), P())
    return jax.shard_map(
        shards, mesh=finer, in_specs=placed, out_specs=(P(ALL), P(ALL, None)), check_vma=False
    )
```

```python
import jax
import jax.numpy as jnp
from jax import lax
from jax.experimental import pallas as pl
from jax.experimental.pallas import tpu as pltpu
from jax.sharding import Mesh
from jax.sharding import PartitionSpec as P

HEADS = 12
HEAD = 64
SEQ = 128
DP = ("zh", "x", "core")
FS = ("y", "zl")
ALL = DP + FS
LIST = 16
SLOTS = 39
BLOCK = SLOTS + 1
ROOM = 48
F32 = jnp.float32
BF16 = jnp.bfloat16


RING = ((0, 0, 2), (1, 0, 2), (2, 0, 1), (2, 1, 1), (3, 0, 2))


def iota(shape, dim):
    return lax.broadcasted_iota(jnp.int32, shape, dim)


def dot(a, b, dims=((1,), (0,))):
    return lax.dot_general(a, b, (dims, ((), ())), preferred_element_type=F32)


def lists_kernel(info_ref, ids_ref, table_ref, rows_ref, count_ref, found_ref):
    vocab = table_ref.shape[0]
    passages = ids_ref.shape[0]
    base = info_ref[0] * vocab
    first_slot = info_ref[1] * LIST
    earlier = iota((SEQ, SEQ), 0) < iota((SEQ, SEQ), 1)
    later = iota((SEQ, SEQ), 0) > iota((SEQ, SEQ), 1)
    owners = iota((passages, SEQ), 0) * vocab

    def passage(p, most):
        row = ids_ref[pl.ds(p, 1), :]
        across = jnp.broadcast_to(row, (SEQ, SEQ))
        down = across.T
        same = across == down
        new_row = jnp.max(jnp.where(same & earlier, 1.0, 0.0), axis=0, keepdims=True) < 0.5
        new_down = jnp.max(jnp.where(same & later, 1.0, 0.0), axis=1, keepdims=True) < 0.5
        mine_down = (down >= base) & (down < base + vocab)
        before = jnp.where(new_down & mine_down & (down < across), 1.0, 0.0)
        slot = jnp.sum(before, axis=0, keepdims=True).astype(jnp.int32) - first_slot
        mine = (row >= base) & (row < base + vocab)
        chosen = (iota((LIST, SEQ), 0) == slot) & mine
        found = jnp.max(jnp.where(chosen, row - base, -1).astype(F32), axis=1, keepdims=True)
        found_ref[pl.ds(pl.multiple_of(p * LIST, LIST), LIST), :] = jnp.broadcast_to(found, (LIST, 128))
        held = (row >= owners) & (row < owners + vocab) & new_row
        return jnp.maximum(most, jnp.sum(jnp.where(held, 1.0, 0.0), axis=1, keepdims=True))

    most = lax.fori_loop(0, passages, passage, jnp.zeros((passages, 1), F32), unroll=4)
    wanted = found_ref[:, 0:1].astype(jnp.int32)
    whole = vocab // 16 * 16
    hits = jnp.where(wanted == iota((wanted.shape[0], whole), 1), 1.0, 0.0).astype(BF16)
    rows = dot(hits, table_ref[0:whole, :])
    if whole < vocab:
        tail = table_ref[whole:vocab, :].astype(F32)
        for k in range(vocab - whole):
            rows = rows + jnp.where(wanted == whole + k, tail[k : k + 1, :], 0.0)
    rows = rows.astype(BF16)
    half = rows_ref.shape[2]
    for side in range(2):
        rows_ref[:, side * LIST : (side + 1) * LIST, :] = rows[:, side * half : (side + 1) * half].reshape(
            passages, LIST, half
        )
    count_ref[...] = jnp.broadcast_to(jnp.max(most, axis=0, keepdims=True), count_ref.shape).astype(
        jnp.int32
    )


def listed_rows(info, ids, table):
    passages = ids.shape[0]
    half = table.shape[1] // 2
    rows = 2 * LIST
    return pl.pallas_call(
        lists_kernel,
        out_shape=(
            jax.ShapeDtypeStruct((passages, rows, half), BF16),
            jax.ShapeDtypeStruct((8, 128), jnp.int32),
        ),
        in_specs=[pl.BlockSpec(memory_space=pltpu.SMEM)]
        + [pl.BlockSpec(memory_space=pltpu.VMEM)] * 2,
        out_specs=(pl.BlockSpec(memory_space=pltpu.VMEM), pl.BlockSpec(memory_space=pltpu.VMEM)),
        scratch_shapes=[pltpu.VMEM((passages * LIST, 128), F32)],
        compiler_params=pltpu.CompilerParams(vmem_limit_bytes=40 << 20),
    )(info, ids, table)


def expand_kernel(info_ref, row_ref, got_ref, out_ref):
    owners, _, half = got_ref.shape
    vocab = info_ref[2]
    first_slot = info_ref[1] * LIST
    row = row_ref[...]
    across = jnp.broadcast_to(row, (SEQ, SEQ))
    down = across.T

    def owner_of(ids):
        owner = jnp.zeros(ids.shape, jnp.int32)
        for k in range(1, owners):
            owner = owner + jnp.where(ids >= k * vocab, 1, 0)
        return owner

    owner_across = jnp.broadcast_to(owner_of(row), (SEQ, SEQ))
    owner_down = owner_across.T
    earlier = iota((SEQ, SEQ), 0) < iota((SEQ, SEQ), 1)
    new_row = jnp.max(jnp.where((across == down) & earlier, 1.0, 0.0), axis=0, keepdims=True) < 0.5
    before = jnp.where(new_row & (owner_across == owner_down) & (across < down), 1.0, 0.0)
    slot = jnp.sum(before, axis=1, keepdims=True).astype(jnp.int32) - first_slot
    place = owner_down[:, 0:1] * LIST + slot
    place = jnp.where((slot >= 0) & (slot < LIST), place, -1)
    hits = jnp.where(place == iota((SEQ, owners * LIST), 1), 1.0, 0.0).astype(BF16)
    for side in range(2):
        rows = got_ref[:, side * LIST : (side + 1) * LIST, :].reshape(owners * LIST, half)
        out_ref[side * SEQ : (side + 1) * SEQ, :] = dot(hits, rows).astype(BF16)


def expanded(info, row, got):
    half = got.shape[2]
    return pl.pallas_call(
        expand_kernel,
        out_shape=jax.ShapeDtypeStruct((2 * SEQ, half), BF16),
        in_specs=[
            pl.BlockSpec(memory_space=pltpu.SMEM),
            pl.BlockSpec(memory_space=pltpu.VMEM),
            pl.BlockSpec(memory_space=pltpu.VMEM),
        ],
        out_specs=pl.BlockSpec(memory_space=pltpu.VMEM),
    )(info, row, got)


def put(sources, targets, sems):
    copies = [
        pltpu.make_async_copy(src, dst, sems.at[k])
        for k, (src, dst) in enumerate(zip(sources, targets, strict=True))
    ]
    for c in copies:
        c.start()
    for c in copies:
        c.wait()


def encode_kernel(info_ref, *refs):
    rings, pieces = refs[0:10], refs[10:18]
    gain_ref, bias_ref, out_ref = refs[18:21]
    x_ref, w_ref, packed_ref, scores_ref, probs_ref, context_ref, sems = refs[21:]
    x_size = 4
    core, at_x = info_ref[0], info_ref[1]
    depth, part = w_ref.shape[1:]
    sources, targets = [], []
    for ref, (core_at, (back, first, count)) in zip(
        rings, [(c, r) for c in (core, 1 - core) for r in RING], strict=True
    ):
        place = core_at * x_size + lax.rem(at_x - back + x_size, x_size)
        sources.append(ref)
        targets.append(w_ref.at[place, pl.ds(first * (depth // 2), count * (depth // 2)), :])
    for k, ref in enumerate(pieces):
        for side in range(2):
            sources.append(ref.at[pl.ds(side * SEQ, SEQ), :])
            rows = pl.ds(k // x_size * SEQ, SEQ)
            targets.append(x_ref.at[k % x_size, rows, pl.ds(side * part, part)])
    put(sources, targets, sems)
    tokens, width = x_ref.shape[1:]
    left = iota((SEQ, 2 * HEAD), 1) < HEAD
    zero = jnp.zeros((SEQ, 2 * HEAD), BF16)
    pairs = HEADS // 2
    passages = tokens // SEQ

    def stacked(values):
        return jnp.concatenate([jnp.where(left, values, zero), jnp.where(left, zero, values)], axis=0)

    def step(i, _):
        x = x_ref[i]
        for j in range(6):
            packed_ref[:, j * part : (j + 1) * part] = dot(x, w_ref[j]).astype(BF16)
        for b in range(passages):
            rows = slice(b * SEQ, (b + 1) * SEQ)
            for pair in range(pairs):
                at = pair * 2 * HEAD
                q = packed_ref[rows, at : at + 2 * HEAD] * jnp.asarray(HEAD**-0.5, BF16)
                k = packed_ref[rows, width + at : width + at + 2 * HEAD]
                scores_ref[b * pairs + pair] = dot(q, stacked(k), ((1,), (1,)))
        for n in range(passages * pairs):
            for h in range(2):
                s = scores_ref[n, :, h * SEQ : (h + 1) * SEQ]
                e = jnp.exp(s - jnp.max(s, axis=1, keepdims=True))
                probs = e * (1.0 / jnp.sum(e, axis=1, keepdims=True))
                probs_ref[n, :, h * SEQ : (h + 1) * SEQ] = probs.astype(BF16)
        for b in range(passages):
            rows = slice(b * SEQ, (b + 1) * SEQ)
            for pair in range(pairs):
                at = pair * 2 * HEAD
                v = packed_ref[rows, 2 * width + at : 2 * width + at + 2 * HEAD]
                context_ref[rows, at : at + 2 * HEAD] = dot(
                    probs_ref[b * pairs + pair], stacked(v)
                ).astype(BF16)
        context = context_ref[...]
        half = width // 2
        mixed = [
            dot(context, w_ref[6 + k]) + x[:, k * half : (k + 1) * half].astype(F32) for k in range(2)
        ]
        mean = sum(jnp.sum(m, axis=1, keepdims=True) for m in mixed) * (1.0 / width)
        center = [m - mean for m in mixed]
        spread = sum(jnp.sum(c * c, axis=1, keepdims=True) for c in center) * (1.0 / width)
        scale = lax.rsqrt(spread + 1e-05)
        for k in range(2):
            cols = slice(k * half, (k + 1) * half)
            out_ref[pl.ds(i * tokens, tokens), cols] = (
                center[k] * scale * gain_ref[:, cols] + bias_ref[:, cols]
            ).astype(BF16)
        return 0

    lax.fori_loop(0, x_size, step, 0)


def encoded(info, rings, pieces, gain, bias):
    part = pieces[0].shape[1]
    tokens, width, chunks = 2 * SEQ, 2 * part, len(pieces) // 2
    pairs = tokens // SEQ * HEADS // 2
    return pl.pallas_call(
        encode_kernel,
        out_shape=jax.ShapeDtypeStruct((chunks * tokens, width), BF16),
        in_specs=[pl.BlockSpec(memory_space=pltpu.SMEM)]
        + [pl.BlockSpec(memory_space=pl.ANY)] * (len(rings) + len(pieces))
        + [pl.BlockSpec(memory_space=pltpu.VMEM)] * 2,
        out_specs=pl.BlockSpec(memory_space=pltpu.VMEM),
        scratch_shapes=[
            pltpu.VMEM((chunks, tokens, width), BF16),
            pltpu.VMEM((chunks * 2, width, part), BF16),
            pltpu.VMEM((tokens, 3 * width), BF16),
            pltpu.VMEM((pairs, SEQ, 2 * SEQ), F32),
            pltpu.VMEM((pairs, SEQ, 2 * SEQ), BF16),
            pltpu.VMEM((tokens, width), BF16),
            pltpu.SemaphoreType.DMA((len(rings) + 2 * len(pieces),)),
        ],
        compiler_params=pltpu.CompilerParams(vmem_limit_bytes=40 << 20),
    )(info, *rings, *pieces, gain.reshape(1, width), bias.reshape(1, width))


def score_kernel(info_ref, mine_ref, other_ref, local_ref, *refs):
    parts = refs[0:5]
    out_ref, old_ref, cent_ref, sems = refs[5:]
    step = pl.program_id(0)
    half = pl.num_programs(0) // 2

    @pl.when(step == 0)
    def _():
        rows_of = parts[0].shape[0]
        targets = []
        for back, first, count in RING:
            start = lax.rem(info_ref[0] - back + 4, 4) * rows_of + first * (rows_of // 2)
            start = pl.multiple_of(start, rows_of // 2)
            targets.append(cent_ref.at[pl.ds(start, count * (rows_of // 2)), :])
        put(parts, targets, sems)

    block = cent_ref.shape[1]
    span = 2 * SEQ
    for n in range(mine_ref.shape[0] // span):
        rows = slice(n * span, (n + 1) * span)
        s = dot(jnp.where(step < half, mine_ref[rows, :], other_ref[rows, :]), cent_ref[...])
        peak = jnp.max(s, axis=1, keepdims=True)
        mass = jnp.sum(jnp.exp(s - peak), axis=1, keepdims=True)
        local = jnp.concatenate(
            [jnp.broadcast_to(local_ref[2 * n + z], (SEQ, SEQ)).T[:, 0:1] for z in range(2)], axis=0
        )
        picked = jnp.sum(jnp.where(local == iota((span, block), 1), s, 0.0), axis=1, keepdims=True)
        both = jnp.where(iota((span, 128), 1) == 0, peak + jnp.log(mass), picked)
        x_size = info_ref[5]
        per_step = mine_ref.shape[0] // span
        back = lax.rem(step, half) * per_step + n
        x = lax.rem(info_ref[3] - back + x_size, x_size)
        core = jnp.where(step < half, info_ref[2], 1 - info_ref[2])
        for z in range(2):
            zh = info_ref[4] if z == 0 else 1 - info_ref[4]
            out_ref[zh * (2 * x_size) + x * 2 + core] = both[z * SEQ : (z + 1) * SEQ, :].T[0:8, :]

    @pl.when(step == pl.num_programs(0) - 1)
    def _():
        per = old_ref.shape[0]
        old = cent_ref[:, pl.ds(pl.multiple_of(info_ref[1] * per, per), per)]
        old_ref[...] = old.astype(F32).T


def scored(info, mine, other, local, parts):
    tokens, width = mine.shape
    block = parts[0].shape[1]
    step = 4 * SEQ
    per = step // SEQ
    half = tokens // step
    return pl.pallas_call(
        score_kernel,
        grid=(2 * half,),
        out_shape=(
            jax.ShapeDtypeStruct((2 * tokens // SEQ, 8, SEQ), F32),
            jax.ShapeDtypeStruct((SEQ, width), F32),
        ),
        in_specs=[
            pl.BlockSpec(memory_space=pltpu.SMEM),
            pl.BlockSpec((step, width), lambda i: (jnp.minimum(i, half - 1), 0)),
            pl.BlockSpec((step, width), lambda i: (jnp.maximum(i - half, 0), 0)),
            pl.BlockSpec((per, 1, SEQ), lambda i: (i, 0, 0)),
        ]
        + [pl.BlockSpec(memory_space=pl.ANY)] * len(parts),
        out_specs=(
            pl.BlockSpec((2 * tokens // SEQ, 8, SEQ), lambda i: (0, 0, 0)),
            pl.BlockSpec((SEQ, width), lambda i: (0, 0)),
        ),
        scratch_shapes=[
            pltpu.VMEM((width, block), BF16),
            pltpu.SemaphoreType.DMA((len(parts),)),
        ],
        compiler_params=pltpu.CompilerParams(vmem_limit_bytes=48 << 20),
    )(info, mine, other, local.reshape(2 * tokens // SEQ, 1, SEQ), *parts)


def choose_kernel(info_ref, local_ref, out_ref, most_ref):
    tokens = local_ref.shape[1]
    per = 128
    dests = out_ref.shape[0] // ROOM
    first_slot = info_ref[1] * SLOTS
    local = local_ref[...]
    upper = iota((per, per), 0) < iota((per, per), 1)
    diagonal = iota((per, per), 0) == iota((per, per), 1)

    def group(g, most):
        match = jnp.where(local - g * per == iota((per, tokens), 0), 1.0, 0.0)
        hits = match.astype(BF16)
        present = jnp.broadcast_to(jnp.max(match, axis=1, keepdims=True), (per, per))
        rank = jnp.sum(jnp.where(upper, present, 0.0), axis=0, keepdims=True).astype(jnp.int32)
        here = jnp.sum(jnp.where(diagonal, present, 0.0), axis=0, keepdims=True)
        slot = iota((ROOM, per), 0)
        chosen = (slot < SLOTS) & (slot == rank - first_slot) & (here > 0.5)
        packing = jnp.where(chosen, 1.0, 0.0).astype(BF16)
        out_ref[pl.ds(pl.multiple_of(g * ROOM, ROOM), ROOM), :] = dot(packing, hits).astype(BF16)
        return jnp.maximum(most, jnp.sum(here, axis=1, keepdims=True))

    most = lax.fori_loop(0, dests, group, jnp.zeros((1, 1), F32), unroll=4)
    most_ref[...] = jnp.broadcast_to(most, most_ref.shape)


def choices(info, local, dests):
    return pl.pallas_call(
        choose_kernel,
        out_shape=(
            jax.ShapeDtypeStruct((dests * ROOM, local.shape[1]), BF16),
            jax.ShapeDtypeStruct((8, 128), F32),
        ),
        in_specs=[pl.BlockSpec(memory_space=pltpu.SMEM), pl.BlockSpec(memory_space=pltpu.VMEM)],
        out_specs=(pl.BlockSpec(memory_space=pltpu.VMEM), pl.BlockSpec(memory_space=pltpu.VMEM)),
        compiler_params=pltpu.CompilerParams(vmem_limit_bytes=40 << 20),
    )(info, local)


def pack_kernel(hits_ref, most_ref, mine_ref, other_ref, out_ref):
    dests, _, width = out_ref.shape
    half = mine_ref.shape[0]
    sums = dot(hits_ref[:, 0:half], mine_ref[...]) + dot(hits_ref[:, half:], other_ref[...])
    sums = sums.reshape(dests, ROOM, width)[:, 0:BLOCK, :]
    last = iota((dests, BLOCK, width), 1) == SLOTS
    out_ref[...] = jnp.where(last, most_ref[0:1, 0:1].reshape(1, 1, 1), sums).astype(BF16)


def packed_sums(chosen, mine, other):
    hits, most = chosen
    width = mine.shape[1]
    return pl.pallas_call(
        pack_kernel,
        out_shape=jax.ShapeDtypeStruct((hits.shape[0] // ROOM, BLOCK, width), BF16),
        in_specs=[pl.BlockSpec(memory_space=pltpu.VMEM)] * 4,
        out_specs=pl.BlockSpec(memory_space=pltpu.VMEM),
        compiler_params=pltpu.CompilerParams(vmem_limit_bytes=40 << 20),
    )(hits, most, mine, other)


def count_kernel(info_ref, assign_ref, out_ref):
    dp, slabs, _ = assign_ref.shape
    targets = iota((128, SEQ), 0) + info_ref[0]
    lane = iota(out_ref.shape, 1)

    def slab(f, out):
        acc = jnp.zeros((128, SEQ), F32)
        for d in range(dp):
            acc = acc + jnp.where(assign_ref[d, pl.ds(f, 1), :] == targets, 1.0, 0.0)
        return jnp.where(lane == f, jnp.sum(acc, axis=1, keepdims=True), out)

    out_ref[...] = lax.fori_loop(0, slabs, slab, jnp.zeros(out_ref.shape, F32))


def counted(info, assign):
    return pl.pallas_call(
        count_kernel,
        out_shape=jax.ShapeDtypeStruct((128, 128), F32),
        in_specs=[pl.BlockSpec(memory_space=pltpu.SMEM), pl.BlockSpec(memory_space=pltpu.VMEM)],
        out_specs=pl.BlockSpec(memory_space=pltpu.VMEM),
    )(info, assign)


def unpack_kernel(info_ref, counts_ref, got_ref, out_ref, most_ref):
    slabs, _, width = got_ref.shape
    counts = counts_ref[...]
    present = jnp.where(counts > 0.5, 1.0, 0.0).astype(BF16)
    lower = jnp.where(iota((128, 128), 1) < iota((128, 128), 0), 1.0, 0.0).astype(BF16)
    rank = dot(lower, present).astype(jnp.int32) - info_ref[1] * SLOTS
    slot = iota((128, BLOCK), 1)
    parts = []
    for f in range(slabs):
        chosen = (slot == rank[:, f : f + 1]) & (slot < SLOTS) & (counts[:, f : f + 1] > 0.5)
        parts.append(jnp.where(chosen, 1.0, 0.0))
    hits = jnp.concatenate(parts, axis=1).astype(BF16)
    out_ref[...] = dot(hits, got_ref[...].reshape(slabs * BLOCK, width))
    most = jnp.max(got_ref[:, SLOTS, 0:128].astype(F32), axis=0, keepdims=True)
    most_ref[...] = jnp.broadcast_to(most, most_ref.shape).astype(jnp.int32)


def unpacked_sums(info, counts, got):
    return pl.pallas_call(
        unpack_kernel,
        out_shape=(
            jax.ShapeDtypeStruct((128, got.shape[2]), F32),
            jax.ShapeDtypeStruct((8, 128), jnp.int32),
        ),
        in_specs=[pl.BlockSpec(memory_space=pltpu.SMEM)]
        + [pl.BlockSpec(memory_space=pltpu.VMEM)] * 2,
        out_specs=(pl.BlockSpec(memory_space=pltpu.VMEM), pl.BlockSpec(memory_space=pltpu.VMEM)),
    )(info, counts, got)


def exchanged(blocks, axis):
    return lax.all_to_all(blocks, axis, 0, 0, tiled=True)


def gathered(shard, axis):
    devices = lax.axis_size(axis)
    return exchanged(jnp.broadcast_to(shard[None], (devices,) + shard.shape), axis)


def swapped(shard, axis):
    return lax.ppermute(shard, axis, [(0, 1), (1, 0)])


def turned(shard, axis, by):
    devices = lax.axis_size(axis)
    return lax.ppermute(shard, axis, [(i, (i + by) % devices) for i in range(devices)])


def neighbours(block, axis):
    return turned(block, axis, 1), turned(block, axis, lax.axis_size(axis) - 1)


def far_halves(back, ahead, axis):
    half = back.shape[0] // 2
    return turned(back[:half], axis, 1), turned(ahead[half:], axis, lax.axis_size(axis) - 1)


def backwards(values, here):
    for dim, at in enumerate(here):
        size = values.shape[dim]
        values = jnp.take(values, (at - jnp.arange(size)) % size, axis=dim)
    return values


def shards(token_ids, embed_table, w_qkv, w_out, ln_gain, ln_bias, centroids_t, assignments):
    core = lax.axis_index("core")
    dp_rank = lax.axis_index(DP)
    fs_rank = lax.axis_index(FS)
    fs_size = lax.axis_size(FS)
    dp_size = lax.axis_size(DP)
    x_size = lax.axis_size("x")
    vocab, width = embed_table.shape
    zero = jnp.int32(0)
    ids = token_ids.reshape(fs_size, SEQ)

    at_x = lax.axis_index("x")

    def info_of(*values):
        return jnp.stack([jnp.asarray(v, jnp.int32) for v in values])

    by_dev = assignments.reshape(2, x_size, 2, fs_size, SEQ)
    of_slab = lax.dynamic_index_in_dim(by_dev, fs_rank, 3, keepdims=False)
    of_slab = jnp.transpose(of_slab, (2, 1, 0, 3))
    here = (core, at_x, lax.axis_index("zh"))
    of_slab = backwards(of_slab, here)
    block = centroids_t.shape[1]
    local = of_slab.reshape(1, -1) - dp_rank * block
    chosen = choices(info_of(zero, zero), local, fs_size)
    counts = counted(
        info_of(dp_rank * block + fs_rank * (block // fs_size)),
        assignments.reshape(dp_size, fs_size, SEQ),
    )

    part = (w_qkv.shape[1] + w_out.shape[1]) // (2 * x_size)
    both = jnp.concatenate([w_qkv, w_out], axis=1)
    piece = lax.dynamic_slice_in_dim(both, (core * x_size + at_x) * part, part, 1)
    column = gathered(piece, FS).reshape(width, part)

    my_row = lax.dynamic_slice_in_dim(ids, fs_rank, 1, 0)
    sent, most = listed_rows(info_of(fs_rank, zero), ids, embed_table)
    sent, column = lax.optimization_barrier((sent, column))
    w_back, w_ahead = neighbours(column, "x")
    rings = [column, w_back, *far_halves(w_back, w_ahead, "x"), w_ahead]
    got = exchanged(sent, FS)
    got, chosen, counts, my_row = lax.optimization_barrier((got, chosen, counts, my_row))
    inputs = expanded(info_of(fs_rank, zero, vocab), my_row, got)

    def more_rows(state):
        turn, acc = state
        again, _ = listed_rows(info_of(fs_rank, turn), ids, embed_table)
        return turn + 1, acc + expanded(info_of(fs_rank, turn, vocab), my_row, exchanged(again, FS))

    most = most[0, 0]
    _, inputs = lax.while_loop(lambda state: state[0] * LIST < most, more_rows, (jnp.int32(1), inputs))

    inputs, *rings = lax.optimization_barrier((inputs, *rings))
    far = swapped(inputs, "zh")
    pieces = [inputs] + [turned(inputs, "x", k) for k in range(1, x_size)]
    far, *pieces = lax.optimization_barrier((far, *pieces))
    pieces += [far] + [turned(far, "x", k) for k in range(1, x_size)]
    rings += [swapped(w, "core") for w in rings]

    shard, _ = lax.optimization_barrier((centroids_t, far))
    near = gathered(shard, "zl").reshape(-1, block)
    pieces[0], near = lax.optimization_barrier((pieces[0], near))
    back, ahead = neighbours(near, "y")
    far_low, far_high = far_halves(back, ahead, "y")

    mine = encoded(info_of(core, at_x), rings, pieces, ln_gain, ln_bias)
    mine, back, ahead = lax.optimization_barrier((mine, back, ahead))
    other = swapped(mine, "core")

    def one_turn(turn):
        info = info_of(zero, turn)
        got = exchanged(packed_sums(choices(info, local, fs_size), mine, other), FS)
        return unpacked_sums(info, counts, got)[0]

    packed = packed_sums(chosen, mine, other)
    packed, mine, other = lax.optimization_barrier((packed, mine, other))
    got = exchanged(packed, FS)

    stats, previous = scored(
        info_of(lax.axis_index("y"), fs_rank, *here, x_size),
        mine,
        other,
        local,
        [near, back, far_low, far_high, ahead],
    )
    stats, got = lax.optimization_barrier((stats, got))
    sums, widest = unpacked_sums(info_of(zero, zero), counts, got)
    widest = widest[0, 0]
    _, sums = lax.while_loop(
        lambda state: state[0] * SLOTS < widest,
        lambda state: (state[0] + 1, state[1] + one_turn(state[0])),
        (jnp.int32(1), sums),
    )

    home = exchanged(stats, DP)
    lse = home[:, 0, :]
    peak = jnp.max(lse, axis=0)
    token_loss = (
        jnp.log(jnp.sum(jnp.exp(lse - peak[None, :]), axis=0)) + peak - jnp.sum(home[:, 1, :], axis=0)
    )

    total = jnp.sum(counts[:, 0:fs_size], axis=1, keepdims=True)
    new_centroids = jnp.where(total > 0, sums / jnp.maximum(total, 1.0), previous)
    return token_loss, new_centroids


def solution(mesh):
    finer = Mesh(mesh.devices.reshape(2, 4, 2, 4, 4), ALL)
    placed = (P(DP), P(FS, None), P(FS, None), P(FS, None), P(), P(), P(FS, DP), P())
    return jax.shard_map(
        shards, mesh=finer, in_specs=placed, out_specs=(P(ALL), P(ALL, None)), check_vma=False
    )
```

```python
import jax
import jax.numpy as jnp
from jax import lax
from jax.experimental import pallas as pl
from jax.experimental.pallas import tpu as pltpu
from jax.sharding import Mesh
from jax.sharding import PartitionSpec as P

HEADS = 12
HEAD = 64
SEQ = 128
DP = ("zh", "x", "core")
FS = ("y", "zl")
ALL = DP + FS
LIST = 47
SLOTS = 39
BLOCK = SLOTS + 1
ROOM = 48
F32 = jnp.float32
BF16 = jnp.bfloat16


RING = ((0, 0, 2), (1, 0, 2), (2, 0, 1), (2, 1, 1), (3, 0, 2))


def iota(shape, dim):
    return lax.broadcasted_iota(jnp.int32, shape, dim)


def dot(a, b, dims=((1,), (0,))):
    return lax.dot_general(a, b, (dims, ((), ())), preferred_element_type=F32)


def ranked(present, groups):
    rows = present.shape[0]
    per = rows // groups
    upper = jnp.where(iota((128, 128), 0) < iota((128, 128), 1), 1.0, 0.0).astype(BF16)
    at, of = iota((rows, rows), 0), iota((rows, rows), 1)
    above = jnp.where((at // per == of // per) & (of < at), 1.0, 0.0).astype(BF16)
    ones = present.astype(BF16)
    return dot(ones, upper) + jnp.sum(dot(above, ones), axis=1, keepdims=True)


def lists_kernel(info_ref, ids_ref, table_ref, rows_ref, present_ref, rank_ref, hits_ref):
    vocab = table_ref.shape[0]
    dests, tokens = ids_ref.shape
    base = info_ref[0] * vocab
    first_slot = info_ref[1] * LIST
    high = 16

    def find(p, _):
        local = ids_ref[pl.ds(p, 1), :] - base
        inside = (local >= 0) & (local < vocab)
        block = jnp.where((iota((high, tokens), 0) == (local >> 7)) & inside, 1.0, 0.0).astype(BF16)
        lane = jnp.where(iota((128, tokens), 0) == (local & 127), 1.0, 0.0).astype(BF16)
        seen = dot(block, lane, ((1,), (1,)))
        present_ref[pl.ds(pl.multiple_of(p * high, high), high), :] = jnp.where(seen > 0.5, 1.0, 0.0)
        return 0

    lax.fori_loop(0, dests, find, 0, unroll=4)
    present = present_ref[...]
    rank_ref[...] = jnp.where(present > 0.5, ranked(present, dests) - first_slot.astype(F32), -1.0)
    blocks = -(-vocab // 128)

    def choose(p, most):
        ranks = rank_ref[pl.ds(pl.multiple_of(p * high, high), high), :]
        slot = iota((ROOM, 128), 0)
        for h in range(blocks):
            chosen = (slot == ranks[h : h + 1, :].astype(jnp.int32)) & (slot < LIST)
            hits_ref[pl.ds(pl.multiple_of(p * ROOM, ROOM), ROOM), h * 128 : (h + 1) * 128] = jnp.where(
                chosen, 1.0, 0.0
            ).astype(BF16)
        return jnp.maximum(most, jnp.max(ranks))

    most = lax.fori_loop(0, dests, choose, jnp.float32(-1.0), unroll=2) + first_slot.astype(F32)
    whole = vocab // 16 * 16
    rows = dot(hits_ref[:, 0:whole], table_ref[0:whole, :])
    if whole < vocab:
        tail = table_ref[whole:vocab, :].astype(F32)
        for k in range(vocab - whole):
            rows = rows + hits_ref[:, whole + k : whole + k + 1].astype(F32) * tail[k : k + 1, :]
    rounds = jnp.floor(most * (1.0 / LIST) + 1e-3) + 1.0
    rows = rows.reshape(rows_ref.shape)
    rows_ref[...] = jnp.where(iota(rows.shape, 1) == LIST, rounds, rows).astype(BF16)


def listed_rows(info, ids, table):
    dests = ids.shape[0]
    width = table.shape[1]
    return pl.pallas_call(
        lists_kernel,
        out_shape=jax.ShapeDtypeStruct((dests, ROOM, width), BF16),
        in_specs=[pl.BlockSpec(memory_space=pltpu.SMEM)] + [pl.BlockSpec(memory_space=pltpu.VMEM)] * 2,
        out_specs=pl.BlockSpec(memory_space=pltpu.VMEM),
        scratch_shapes=[
            pltpu.VMEM((dests * 16, 128), F32),
            pltpu.VMEM((dests * 16, 128), F32),
            pltpu.VMEM((dests * ROOM, 16 * 128), BF16),
        ],
        compiler_params=pltpu.CompilerParams(vmem_limit_bytes=40 << 20),
    )(info, ids, table)


def place_kernel(info_ref, row_ref, out_ref):
    tokens = row_ref.shape[1]
    owners = out_ref.shape[1] // ROOM
    first_slot = info_ref[1] * LIST
    vocab = info_ref[2]
    row = row_ref[...]
    owner = jnp.zeros(row.shape, jnp.int32)
    for k in range(1, owners):
        owner = owner + jnp.where(row >= k * vocab, 1, 0)
    local = row - owner * vocab
    group = owner * 16 + (local >> 7)
    block = jnp.where(iota((owners * 16, tokens), 0) == group, 1.0, 0.0).astype(BF16)
    lane = jnp.where(iota((128, tokens), 0) == (local & 127), 1.0, 0.0).astype(BF16)
    present = jnp.where(dot(block, lane, ((1,), (1,))) > 0.5, 1.0, 0.0)
    rank = ranked(present, owners) - first_slot.astype(F32)
    rank = jnp.where((rank >= 0) & (rank < LIST), rank, 255.0).astype(BF16)
    owner = owner.astype(F32)
    low = (local & 127).astype(F32)
    for t in range(tokens // 128):
        cols = slice(t * 128, (t + 1) * 128)
        found = lax.dot_general(
            block[:, cols], rank, (((0,), (0,)), ((), ())), preferred_element_type=F32
        )
        down = jnp.broadcast_to(low[:, cols], (128, 128)).T
        slot = jnp.sum(jnp.where(iota((128, 128), 1).astype(F32) == down, found, 0.0), axis=1, keepdims=True)
        of = jnp.broadcast_to(owner[:, cols], (128, 128)).T[:, 0:1]
        place = jnp.where(slot < LIST, of * ROOM + slot, -1.0).astype(jnp.int32)
        out_ref[cols, :] = jnp.where(place == iota((128, owners * ROOM), 1), 1.0, 0.0).astype(BF16)


def placed_rows(info, row, owners):
    return pl.pallas_call(
        place_kernel,
        out_shape=jax.ShapeDtypeStruct((row.shape[1], owners * ROOM), BF16),
        in_specs=[pl.BlockSpec(memory_space=pltpu.SMEM), pl.BlockSpec(memory_space=pltpu.VMEM)],
        out_specs=pl.BlockSpec(memory_space=pltpu.VMEM),
        compiler_params=pltpu.CompilerParams(vmem_limit_bytes=40 << 20),
    )(info, row)


def expand_kernel(places_ref, got_ref, out_ref, rounds_ref):
    owners, room, width = got_ref.shape
    out_ref[...] = dot(places_ref[...], got_ref[...].reshape(owners * room, width)).astype(BF16)
    most = jnp.max(got_ref[:, LIST, 0:128].astype(F32), axis=0, keepdims=True)
    rounds_ref[...] = jnp.broadcast_to(most, rounds_ref.shape).astype(jnp.int32)


def expanded(places, got):
    return pl.pallas_call(
        expand_kernel,
        out_shape=(
            jax.ShapeDtypeStruct((places.shape[0], got.shape[2]), BF16),
            jax.ShapeDtypeStruct((8, 128), jnp.int32),
        ),
        in_specs=[pl.BlockSpec(memory_space=pltpu.VMEM)] * 2,
        out_specs=(pl.BlockSpec(memory_space=pltpu.VMEM), pl.BlockSpec(memory_space=pltpu.VMEM)),
        compiler_params=pltpu.CompilerParams(vmem_limit_bytes=40 << 20),
    )(places, got)


def put(sources, targets, sems):
    copies = [
        pltpu.make_async_copy(src, dst, sems.at[k])
        for k, (src, dst) in enumerate(zip(sources, targets, strict=True))
    ]
    for c in copies:
        c.start()
    for c in copies:
        c.wait()


def encode_kernel(info_ref, *refs):
    rings = refs[0:10]
    slab_ref, gain_ref, bias_ref, out_ref, w_ref, packed_ref, scores_ref, probs_ref, context_ref, sems = (
        refs[10:]
    )
    x_size = 4
    core, at_x = info_ref[0], info_ref[1]
    depth, part = w_ref.shape[1:]
    targets = []
    for core_at in (core, 1 - core):
        for back, first, count in RING:
            place = core_at * x_size + lax.rem(at_x - back + x_size, x_size)
            targets.append(w_ref.at[place, pl.ds(first * (depth // 2), count * (depth // 2)), :])
    put(rings, targets, sems)
    tokens, width = packed_ref.shape[0], slab_ref.shape[1]
    left = iota((SEQ, 2 * HEAD), 1) < HEAD
    zero = jnp.zeros((SEQ, 2 * HEAD), BF16)
    pairs = HEADS // 2
    passages = tokens // SEQ

    def stacked(values):
        return jnp.concatenate([jnp.where(left, values, zero), jnp.where(left, zero, values)], axis=0)

    def step(i, _):
        x = slab_ref[pl.ds(i * tokens, tokens), :]
        for j in range(6):
            packed_ref[:, j * part : (j + 1) * part] = dot(x, w_ref[j]).astype(BF16)
        for b in range(passages):
            rows = slice(b * SEQ, (b + 1) * SEQ)
            for pair in range(pairs):
                at = pair * 2 * HEAD
                q = packed_ref[rows, at : at + 2 * HEAD] * jnp.asarray(HEAD**-0.5, BF16)
                k = packed_ref[rows, width + at : width + at + 2 * HEAD]
                scores_ref[b * pairs + pair] = dot(q, stacked(k), ((1,), (1,)))
        for n in range(passages * pairs):
            for h in range(2):
                s = scores_ref[n, :, h * SEQ : (h + 1) * SEQ]
                e = jnp.exp(s - jnp.max(s, axis=1, keepdims=True))
                probs = e * (1.0 / jnp.sum(e, axis=1, keepdims=True))
                probs_ref[n, :, h * SEQ : (h + 1) * SEQ] = probs.astype(BF16)
        for b in range(passages):
            rows = slice(b * SEQ, (b + 1) * SEQ)
            for pair in range(pairs):
                at = pair * 2 * HEAD
                v = packed_ref[rows, 2 * width + at : 2 * width + at + 2 * HEAD]
                context_ref[rows, at : at + 2 * HEAD] = dot(
                    probs_ref[b * pairs + pair], stacked(v)
                ).astype(BF16)
        context = context_ref[...]
        half = width // 2
        mixed = [
            dot(context, w_ref[6 + k]) + x[:, k * half : (k + 1) * half].astype(F32) for k in range(2)
        ]
        mean = sum(jnp.sum(m, axis=1, keepdims=True) for m in mixed) * (1.0 / width)
        center = [m - mean for m in mixed]
        spread = sum(jnp.sum(c * c, axis=1, keepdims=True) for c in center) * (1.0 / width)
        scale = lax.rsqrt(spread + 1e-05)
        for k in range(2):
            cols = slice(k * half, (k + 1) * half)
            out_ref[pl.ds(i * tokens, tokens), cols] = (
                center[k] * scale * gain_ref[:, cols] + bias_ref[:, cols]
            ).astype(BF16)
        return 0

    lax.fori_loop(0, slab_ref.shape[0] // tokens, step, 0)


def encoded(info, rings, slab, gain, bias):
    part = rings[0].shape[1]
    tokens, width = 2 * SEQ, slab.shape[1]
    pairs = tokens // SEQ * HEADS // 2
    return pl.pallas_call(
        encode_kernel,
        out_shape=jax.ShapeDtypeStruct(slab.shape, BF16),
        in_specs=[pl.BlockSpec(memory_space=pltpu.SMEM)]
        + [pl.BlockSpec(memory_space=pltpu.HBM)] * len(rings)
        + [pl.BlockSpec(memory_space=pltpu.VMEM)] * 3,
        out_specs=pl.BlockSpec(memory_space=pltpu.VMEM),
        scratch_shapes=[
            pltpu.VMEM((8, width, part), BF16),
            pltpu.VMEM((tokens, 3 * width), BF16),
            pltpu.VMEM((pairs, SEQ, 2 * SEQ), F32),
            pltpu.VMEM((pairs, SEQ, 2 * SEQ), BF16),
            pltpu.VMEM((tokens, width), BF16),
            pltpu.SemaphoreType.DMA((len(rings),)),
        ],
        compiler_params=pltpu.CompilerParams(vmem_limit_bytes=40 << 20),
    )(info, *rings, slab, gain.reshape(1, width), bias.reshape(1, width))


def score_kernel(info_ref, mine_ref, other_ref, local_ref, *refs):
    parts = refs[0:5]
    out_ref, old_ref, cent_ref, sems = refs[5:]
    step = pl.program_id(0)
    half = pl.num_programs(0) // 2

    @pl.when(step == 0)
    def _():
        rows_of = parts[0].shape[0]
        targets = []
        for back, first, count in RING:
            start = lax.rem(info_ref[0] - back + 4, 4) * rows_of + first * (rows_of // 2)
            start = pl.multiple_of(start, rows_of // 2)
            targets.append(cent_ref.at[pl.ds(start, count * (rows_of // 2)), :])
        put(parts, targets, sems)

    block = cent_ref.shape[1]
    span = 2 * SEQ
    for n in range(mine_ref.shape[0] // span):
        rows = slice(n * span, (n + 1) * span)
        s = dot(jnp.where(step < half, mine_ref[rows, :], other_ref[rows, :]), cent_ref[...])
        peak = jnp.max(s, axis=1, keepdims=True)
        mass = jnp.sum(jnp.exp(s - peak), axis=1, keepdims=True)
        local = jnp.concatenate(
            [jnp.broadcast_to(local_ref[2 * n + z], (SEQ, SEQ)).T[:, 0:1] for z in range(2)], axis=0
        )
        picked = jnp.sum(jnp.where(local == iota((span, block), 1), s, 0.0), axis=1, keepdims=True)
        both = jnp.where(iota((span, 128), 1) == 0, peak + jnp.log(mass), picked)
        x_size = info_ref[5]
        per_step = mine_ref.shape[0] // span
        back = lax.rem(step, half) * per_step + n
        x = lax.rem(info_ref[3] - back + x_size, x_size)
        core = jnp.where(step < half, info_ref[2], 1 - info_ref[2])
        for z in range(2):
            zh = info_ref[4] if z == 0 else 1 - info_ref[4]
            out_ref[zh * (2 * x_size) + x * 2 + core] = both[z * SEQ : (z + 1) * SEQ, :].T[0:8, :]

    @pl.when(step == pl.num_programs(0) - 1)
    def _():
        per = old_ref.shape[0]
        old = cent_ref[:, pl.ds(pl.multiple_of(info_ref[1] * per, per), per)]
        old_ref[...] = old.astype(F32).T


def scored(info, mine, other, local, parts):
    tokens, width = mine.shape
    block = parts[0].shape[1]
    step = 4 * SEQ
    per = step // SEQ
    half = tokens // step
    return pl.pallas_call(
        score_kernel,
        grid=(2 * half,),
        out_shape=(
            jax.ShapeDtypeStruct((2 * tokens // SEQ, 8, SEQ), F32),
            jax.ShapeDtypeStruct((SEQ, width), F32),
        ),
        in_specs=[
            pl.BlockSpec(memory_space=pltpu.SMEM),
            pl.BlockSpec((step, width), lambda i: (jnp.minimum(i, half - 1), 0)),
            pl.BlockSpec((step, width), lambda i: (jnp.maximum(i - half, 0), 0)),
            pl.BlockSpec((per, 1, SEQ), lambda i: (i, 0, 0)),
        ]
        + [pl.BlockSpec(memory_space=pltpu.HBM)] * len(parts),
        out_specs=(
            pl.BlockSpec((2 * tokens // SEQ, 8, SEQ), lambda i: (0, 0, 0)),
            pl.BlockSpec((SEQ, width), lambda i: (0, 0)),
        ),
        scratch_shapes=[
            pltpu.VMEM((width, block), BF16),
            pltpu.SemaphoreType.DMA((len(parts),)),
        ],
        compiler_params=pltpu.CompilerParams(vmem_limit_bytes=48 << 20),
    )(info, mine, other, local.reshape(2 * tokens // SEQ, 1, SEQ), *parts)


def choose_kernel(info_ref, local_ref, out_ref, most_ref):
    tokens = local_ref.shape[1]
    per = 128
    dests = out_ref.shape[0] // ROOM
    first_slot = info_ref[1] * SLOTS
    local = local_ref[...]
    upper = iota((per, per), 0) < iota((per, per), 1)
    diagonal = iota((per, per), 0) == iota((per, per), 1)

    def group(g, most):
        match = jnp.where(local - g * per == iota((per, tokens), 0), 1.0, 0.0)
        hits = match.astype(BF16)
        present = jnp.broadcast_to(jnp.max(match, axis=1, keepdims=True), (per, per))
        rank = jnp.sum(jnp.where(upper, present, 0.0), axis=0, keepdims=True).astype(jnp.int32)
        here = jnp.sum(jnp.where(diagonal, present, 0.0), axis=0, keepdims=True)
        slot = iota((ROOM, per), 0)
        chosen = (slot < SLOTS) & (slot == rank - first_slot) & (here > 0.5)
        packing = jnp.where(chosen, 1.0, 0.0).astype(BF16)
        out_ref[pl.ds(pl.multiple_of(g * ROOM, ROOM), ROOM), :] = dot(packing, hits).astype(BF16)
        return jnp.maximum(most, jnp.sum(here, axis=1, keepdims=True))

    most = lax.fori_loop(0, dests, group, jnp.zeros((1, 1), F32), unroll=4)
    most_ref[...] = jnp.broadcast_to(most, most_ref.shape)


def choices(info, local, dests):
    return pl.pallas_call(
        choose_kernel,
        out_shape=(
            jax.ShapeDtypeStruct((dests * ROOM, local.shape[1]), BF16),
            jax.ShapeDtypeStruct((8, 128), F32),
        ),
        in_specs=[pl.BlockSpec(memory_space=pltpu.SMEM), pl.BlockSpec(memory_space=pltpu.VMEM)],
        out_specs=(pl.BlockSpec(memory_space=pltpu.VMEM), pl.BlockSpec(memory_space=pltpu.VMEM)),
        compiler_params=pltpu.CompilerParams(vmem_limit_bytes=40 << 20),
    )(info, local)


def pack_kernel(hits_ref, most_ref, mine_ref, other_ref, out_ref):
    dests, _, width = out_ref.shape
    half = mine_ref.shape[0]
    sums = dot(hits_ref[:, 0:half], mine_ref[...]) + dot(hits_ref[:, half:], other_ref[...])
    sums = sums.reshape(dests, ROOM, width)[:, 0:BLOCK, :]
    last = iota((dests, BLOCK, width), 1) == SLOTS
    out_ref[...] = jnp.where(last, most_ref[0:1, 0:1].reshape(1, 1, 1), sums).astype(BF16)


def packed_sums(chosen, mine, other):
    hits, most = chosen
    width = mine.shape[1]
    return pl.pallas_call(
        pack_kernel,
        out_shape=jax.ShapeDtypeStruct((hits.shape[0] // ROOM, BLOCK, width), BF16),
        in_specs=[pl.BlockSpec(memory_space=pltpu.VMEM)] * 4,
        out_specs=pl.BlockSpec(memory_space=pltpu.VMEM),
        compiler_params=pltpu.CompilerParams(vmem_limit_bytes=40 << 20),
    )(hits, most, mine, other)


def count_kernel(info_ref, assign_ref, out_ref):
    dp, slabs, _ = assign_ref.shape
    targets = iota((128, SEQ), 0) + info_ref[0]
    lane = iota(out_ref.shape, 1)

    def slab(f, out):
        acc = jnp.zeros((128, SEQ), F32)
        for d in range(dp):
            acc = acc + jnp.where(assign_ref[d, pl.ds(f, 1), :] == targets, 1.0, 0.0)
        return jnp.where(lane == f, jnp.sum(acc, axis=1, keepdims=True), out)

    out_ref[...] = lax.fori_loop(0, slabs, slab, jnp.zeros(out_ref.shape, F32))


def counted(info, assign):
    return pl.pallas_call(
        count_kernel,
        out_shape=jax.ShapeDtypeStruct((128, 128), F32),
        in_specs=[pl.BlockSpec(memory_space=pltpu.SMEM), pl.BlockSpec(memory_space=pltpu.VMEM)],
        out_specs=pl.BlockSpec(memory_space=pltpu.VMEM),
    )(info, assign)


def unpack_kernel(info_ref, counts_ref, got_ref, out_ref, most_ref):
    slabs, _, width = got_ref.shape
    counts = counts_ref[...]
    present = jnp.where(counts > 0.5, 1.0, 0.0).astype(BF16)
    lower = jnp.where(iota((128, 128), 1) < iota((128, 128), 0), 1.0, 0.0).astype(BF16)
    rank = dot(lower, present).astype(jnp.int32) - info_ref[1] * SLOTS
    slot = iota((128, BLOCK), 1)
    parts = []
    for f in range(slabs):
        chosen = (slot == rank[:, f : f + 1]) & (slot < SLOTS) & (counts[:, f : f + 1] > 0.5)
        parts.append(jnp.where(chosen, 1.0, 0.0))
    hits = jnp.concatenate(parts, axis=1).astype(BF16)
    out_ref[...] = dot(hits, got_ref[...].reshape(slabs * BLOCK, width))
    most = jnp.max(got_ref[:, SLOTS, 0:128].astype(F32), axis=0, keepdims=True)
    most_ref[...] = jnp.broadcast_to(most, most_ref.shape).astype(jnp.int32)


def unpacked_sums(info, counts, got):
    return pl.pallas_call(
        unpack_kernel,
        out_shape=(
            jax.ShapeDtypeStruct((128, got.shape[2]), F32),
            jax.ShapeDtypeStruct((8, 128), jnp.int32),
        ),
        in_specs=[pl.BlockSpec(memory_space=pltpu.SMEM)]
        + [pl.BlockSpec(memory_space=pltpu.VMEM)] * 2,
        out_specs=(pl.BlockSpec(memory_space=pltpu.VMEM), pl.BlockSpec(memory_space=pltpu.VMEM)),
    )(info, counts, got)


def exchanged(blocks, axis):
    return lax.all_to_all(blocks, axis, 0, 0, tiled=True)


def gathered(shard, axis):
    devices = lax.axis_size(axis)
    return exchanged(jnp.broadcast_to(shard[None], (devices,) + shard.shape), axis)


def swapped(shard, axis):
    return lax.ppermute(shard, axis, [(0, 1), (1, 0)])


def turned(shard, axis, by):
    devices = lax.axis_size(axis)
    return lax.ppermute(shard, axis, [(i, (i + by) % devices) for i in range(devices)])


def neighbours(block, axis):
    return turned(block, axis, 1), turned(block, axis, lax.axis_size(axis) - 1)


def far_halves(back, ahead, axis):
    half = back.shape[0] // 2
    return turned(back[:half], axis, 1), turned(ahead[half:], axis, lax.axis_size(axis) - 1)


def backwards(values, here):
    for dim, at in enumerate(here):
        size = values.shape[dim]
        values = jnp.take(values, (at - jnp.arange(size)) % size, axis=dim)
    return values


def shards(token_ids, embed_table, w_qkv, w_out, ln_gain, ln_bias, centroids_t, assignments):
    core = lax.axis_index("core")
    dp_rank = lax.axis_index(DP)
    fs_rank = lax.axis_index(FS)
    fs_size = lax.axis_size(FS)
    dp_size = lax.axis_size(DP)
    x_size = lax.axis_size("x")
    vocab, width = embed_table.shape
    zero = jnp.int32(0)
    ids = token_ids.reshape(fs_size, SEQ)

    at_x = lax.axis_index("x")

    def info_of(*values):
        return jnp.stack([jnp.asarray(v, jnp.int32) for v in values])

    by_dev = assignments.reshape(2, x_size, 2, fs_size, SEQ)
    of_slab = lax.dynamic_index_in_dim(by_dev, fs_rank, 3, keepdims=False)
    of_slab = jnp.transpose(of_slab, (2, 1, 0, 3))
    here = (core, at_x, lax.axis_index("zh"))
    of_slab = backwards(of_slab, here)
    block = centroids_t.shape[1]
    local = of_slab.reshape(1, -1) - dp_rank * block
    chosen = choices(info_of(zero, zero), local, fs_size)
    counts = counted(
        info_of(dp_rank * block + fs_rank * (block // fs_size)),
        assignments.reshape(dp_size, fs_size, SEQ),
    )

    part = (w_qkv.shape[1] + w_out.shape[1]) // (2 * x_size)
    both = jnp.concatenate([w_qkv, w_out], axis=1)
    piece = lax.dynamic_slice_in_dim(both, (core * x_size + at_x) * part, part, 1)
    column = gathered(piece, FS).reshape(width, part)

    two = jnp.stack([ids, swapped(ids, "zh")])
    ids = jnp.stack([two] + [turned(two, "x", k) for k in range(1, x_size)])
    ids = jnp.transpose(ids, (2, 0, 1, 3)).reshape(fs_size, -1)

    my_row = lax.dynamic_slice_in_dim(ids, fs_rank, 1, 0)
    sent = listed_rows(info_of(fs_rank, zero), ids, embed_table)
    sent, column, chosen, counts, local = lax.optimization_barrier((sent, column, chosen, counts, local))
    w_back, w_ahead = neighbours(column, "x")
    rings = [column, w_back, *far_halves(w_back, w_ahead, "x"), w_ahead]
    places = placed_rows(info_of(fs_rank, zero, vocab), my_row, fs_size)
    rings += [swapped(w, "core") for w in rings]
    got = exchanged(sent, FS)
    got, places, *rings = lax.optimization_barrier((got, places, *rings))
    slab, rounds = expanded(places, got)

    def more_rows(state):
        turn, acc = state
        again = exchanged(listed_rows(info_of(fs_rank, turn), ids, embed_table), FS)
        extra, _ = expanded(placed_rows(info_of(fs_rank, turn, vocab), my_row, fs_size), again)
        return turn + 1, acc + extra

    rounds = rounds[0, 0]
    _, slab = lax.while_loop(lambda state: state[0] < rounds, more_rows, (jnp.int32(1), slab))

    shard, _ = lax.optimization_barrier((centroids_t, got))
    near = gathered(shard, "zl").reshape(-1, block)
    back, ahead = neighbours(near, "y")
    far_low, far_high = far_halves(back, ahead, "y")

    mine = encoded(info_of(core, at_x), rings, slab, ln_gain, ln_bias)
    mine, near = lax.optimization_barrier((mine, near))
    other = swapped(mine, "core")

    def one_turn(turn):
        info = info_of(zero, turn)
        got = exchanged(packed_sums(choices(info, local, fs_size), mine, other), FS)
        return unpacked_sums(info, counts, got)[0]

    packed = packed_sums(chosen, mine, other)
    packed, mine, other = lax.optimization_barrier((packed, mine, other))
    got = exchanged(packed, FS)

    stats, previous = scored(
        info_of(lax.axis_index("y"), fs_rank, *here, x_size),
        mine,
        other,
        local,
        [near, back, far_low, far_high, ahead],
    )
    stats, got = lax.optimization_barrier((stats, got))
    sums, widest = unpacked_sums(info_of(zero, zero), counts, got)
    widest = widest[0, 0]
    _, sums = lax.while_loop(
        lambda state: state[0] * SLOTS < widest,
        lambda state: (state[0] + 1, state[1] + one_turn(state[0])),
        (jnp.int32(1), sums),
    )

    home = exchanged(stats, DP)
    lse = home[:, 0, :]
    peak = jnp.max(lse, axis=0)
    token_loss = (
        jnp.log(jnp.sum(jnp.exp(lse - peak[None, :]), axis=0)) + peak - jnp.sum(home[:, 1, :], axis=0)
    )

    total = jnp.sum(counts[:, 0:fs_size], axis=1, keepdims=True)
    new_centroids = jnp.where(total > 0, sums / jnp.maximum(total, 1.0), previous)
    return token_loss, new_centroids


def solution(mesh):
    finer = Mesh(mesh.devices.reshape(2, 4, 2, 4, 4), ALL)
    placed = (P(DP), P(FS, None), P(FS, None), P(FS, None), P(), P(), P(FS, DP), P())
    return jax.shard_map(
        shards, mesh=finer, in_specs=placed, out_specs=(P(ALL), P(ALL, None)), check_vma=False
    )
```

```python
import jax
import jax.numpy as jnp
from jax import lax
from jax.experimental import pallas as pl
from jax.experimental.pallas import tpu as pltpu
from jax.sharding import Mesh
from jax.sharding import PartitionSpec as P

HEADS = 12
HEAD = 64
SEQ = 128
DP = ("zh", "x", "core")
FS = ("y", "zl")
ALL = DP + FS
LIST = 47
SLOTS = 39
BLOCK = SLOTS + 1
ROOM = 48
F32 = jnp.float32
BF16 = jnp.bfloat16


RING = ((0, 0, 2), (1, 0, 2), (2, 0, 1), (2, 1, 1), (3, 0, 2))


def iota(shape, dim):
    return lax.broadcasted_iota(jnp.int32, shape, dim)


def dot(a, b, dims=((1,), (0,))):
    return lax.dot_general(a, b, (dims, ((), ())), preferred_element_type=F32)


def ranked(present, groups):
    rows = present.shape[0]
    per = rows // groups
    upper = jnp.where(iota((128, 128), 0) < iota((128, 128), 1), 1.0, 0.0).astype(BF16)
    at, of = iota((rows, rows), 0), iota((rows, rows), 1)
    above = jnp.where((at // per == of // per) & (of < at), 1.0, 0.0).astype(BF16)
    ones = present.astype(BF16)
    return dot(ones, upper) + jnp.sum(dot(above, ones), axis=1, keepdims=True)


def tokens_of(ids_refs, dest):
    dests = ids_refs[0].shape[0] // 2
    return jnp.concatenate(
        [ref[pl.ds(z * dests + dest, 1), :] for ref in ids_refs for z in range(2)], axis=1
    )


def lists_kernel(info_ref, *refs):
    ids_refs, table_ref, rows_ref, present_ref, rank_ref, hits_ref = refs[0:4], *refs[4:]
    vocab = table_ref.shape[0]
    dests, tokens = rows_ref.shape[0], 8 * SEQ
    base = info_ref[0] * vocab
    first_slot = info_ref[1] * LIST
    high = 16

    def find(p, _):
        local = tokens_of(ids_refs, p) - base
        inside = (local >= 0) & (local < vocab)
        block = jnp.where((iota((high, tokens), 0) == (local >> 7)) & inside, 1.0, 0.0).astype(BF16)
        lane = jnp.where(iota((128, tokens), 0) == (local & 127), 1.0, 0.0).astype(BF16)
        seen = dot(block, lane, ((1,), (1,)))
        present_ref[pl.ds(pl.multiple_of(p * high, high), high), :] = jnp.where(seen > 0.5, 1.0, 0.0)
        return 0

    lax.fori_loop(0, dests, find, 0, unroll=4)
    present = present_ref[...]
    rank_ref[...] = jnp.where(present > 0.5, ranked(present, dests) - first_slot.astype(F32), -1.0)
    blocks = -(-vocab // 128)

    def choose(p, most):
        ranks = rank_ref[pl.ds(pl.multiple_of(p * high, high), high), :]
        slot = iota((ROOM, 128), 0)
        for h in range(blocks):
            chosen = (slot == ranks[h : h + 1, :].astype(jnp.int32)) & (slot < LIST)
            hits_ref[pl.ds(pl.multiple_of(p * ROOM, ROOM), ROOM), h * 128 : (h + 1) * 128] = jnp.where(
                chosen, 1.0, 0.0
            ).astype(BF16)
        return jnp.maximum(most, jnp.max(ranks))

    most = lax.fori_loop(0, dests, choose, jnp.float32(-1.0), unroll=2) + first_slot.astype(F32)
    whole = vocab // 16 * 16
    rows = dot(hits_ref[:, 0:whole], table_ref[0:whole, :])
    if whole < vocab:
        tail = table_ref[whole:vocab, :].astype(F32)
        for k in range(vocab - whole):
            rows = rows + hits_ref[:, whole + k : whole + k + 1].astype(F32) * tail[k : k + 1, :]
    rounds = jnp.floor(most * (1.0 / LIST) + 1e-3) + 1.0
    rows = rows.reshape(rows_ref.shape)
    rows_ref[...] = jnp.where(iota(rows.shape, 1) == LIST, rounds, rows).astype(BF16)


def listed_rows(info, ids, table):
    dests = ids[0].shape[0] // 2
    width = table.shape[1]
    return pl.pallas_call(
        lists_kernel,
        out_shape=jax.ShapeDtypeStruct((dests, ROOM, width), BF16),
        in_specs=[pl.BlockSpec(memory_space=pltpu.SMEM)]
        + [pl.BlockSpec(memory_space=pltpu.VMEM)] * (len(ids) + 1),
        out_specs=pl.BlockSpec(memory_space=pltpu.VMEM),
        scratch_shapes=[
            pltpu.VMEM((dests * 16, 128), F32),
            pltpu.VMEM((dests * 16, 128), F32),
            pltpu.VMEM((dests * ROOM, 16 * 128), BF16),
        ],
        compiler_params=pltpu.CompilerParams(vmem_limit_bytes=40 << 20),
    )(info, *ids, table)


def place_kernel(info_ref, *refs):
    ids_refs, out_ref = refs[0:4], refs[4]
    tokens = 8 * SEQ
    owners = out_ref.shape[1] // ROOM
    first_slot = info_ref[1] * LIST
    vocab = info_ref[2]
    row = tokens_of(ids_refs, info_ref[0])
    owner = jnp.zeros(row.shape, jnp.int32)
    for k in range(1, owners):
        owner = owner + jnp.where(row >= k * vocab, 1, 0)
    local = row - owner * vocab
    group = owner * 16 + (local >> 7)
    block = jnp.where(iota((owners * 16, tokens), 0) == group, 1.0, 0.0).astype(BF16)
    lane = jnp.where(iota((128, tokens), 0) == (local & 127), 1.0, 0.0).astype(BF16)
    present = jnp.where(dot(block, lane, ((1,), (1,))) > 0.5, 1.0, 0.0)
    rank = ranked(present, owners) - first_slot.astype(F32)
    rank = jnp.where((rank >= 0) & (rank < LIST), rank, 255.0).astype(BF16)
    owner = owner.astype(F32)
    low = (local & 127).astype(F32)
    for t in range(tokens // 128):
        cols = slice(t * 128, (t + 1) * 128)
        found = lax.dot_general(
            block[:, cols], rank, (((0,), (0,)), ((), ())), preferred_element_type=F32
        )
        down = jnp.broadcast_to(low[:, cols], (128, 128)).T
        slot = jnp.sum(jnp.where(iota((128, 128), 1).astype(F32) == down, found, 0.0), axis=1, keepdims=True)
        of = jnp.broadcast_to(owner[:, cols], (128, 128)).T[:, 0:1]
        place = jnp.where(slot < LIST, of * ROOM + slot, -1.0).astype(jnp.int32)
        out_ref[cols, :] = jnp.where(place == iota((128, owners * ROOM), 1), 1.0, 0.0).astype(BF16)


def placed_rows(info, ids, owners):
    return pl.pallas_call(
        place_kernel,
        out_shape=jax.ShapeDtypeStruct((8 * SEQ, owners * ROOM), BF16),
        in_specs=[pl.BlockSpec(memory_space=pltpu.SMEM)]
        + [pl.BlockSpec(memory_space=pltpu.VMEM)] * len(ids),
        out_specs=pl.BlockSpec(memory_space=pltpu.VMEM),
        compiler_params=pltpu.CompilerParams(vmem_limit_bytes=40 << 20),
    )(info, *ids)


def expand_kernel(places_ref, got_ref, out_ref, rounds_ref):
    owners, room, width = got_ref.shape
    out_ref[...] = dot(places_ref[...], got_ref[...].reshape(owners * room, width)).astype(BF16)
    most = jnp.max(got_ref[:, LIST, 0:128].astype(F32), axis=0, keepdims=True)
    rounds_ref[...] = jnp.broadcast_to(most, rounds_ref.shape).astype(jnp.int32)


def expanded(places, got):
    return pl.pallas_call(
        expand_kernel,
        out_shape=(
            jax.ShapeDtypeStruct((places.shape[0], got.shape[2]), BF16),
            jax.ShapeDtypeStruct((8, 128), jnp.int32),
        ),
        in_specs=[pl.BlockSpec(memory_space=pltpu.VMEM)] * 2,
        out_specs=(pl.BlockSpec(memory_space=pltpu.VMEM), pl.BlockSpec(memory_space=pltpu.VMEM)),
        compiler_params=pltpu.CompilerParams(vmem_limit_bytes=40 << 20),
    )(places, got)


def put(sources, targets, sems):
    copies = [
        pltpu.make_async_copy(src, dst, sems.at[k])
        for k, (src, dst) in enumerate(zip(sources, targets, strict=True))
    ]
    for c in copies:
        c.start()
    for c in copies:
        c.wait()


def encode_kernel(info_ref, *refs):
    rings = refs[0:10]
    slab_ref, gain_ref, bias_ref, out_ref, w_ref, packed_ref, scores_ref, probs_ref, context_ref, sems = (
        refs[10:]
    )
    x_size = 4
    core, at_x = info_ref[0], info_ref[1]
    depth, part = w_ref.shape[1:]
    targets = []
    for core_at in (core, 1 - core):
        for back, first, count in RING:
            place = core_at * x_size + lax.rem(at_x - back + x_size, x_size)
            targets.append(w_ref.at[place, pl.ds(first * (depth // 2), count * (depth // 2)), :])
    put(rings, targets, sems)
    tokens, width = packed_ref.shape[0], slab_ref.shape[1]
    left = iota((SEQ, 2 * HEAD), 1) < HEAD
    zero = jnp.zeros((SEQ, 2 * HEAD), BF16)
    pairs = HEADS // 2
    passages = tokens // SEQ

    def stacked(values):
        return jnp.concatenate([jnp.where(left, values, zero), jnp.where(left, zero, values)], axis=0)

    def step(i, _):
        x = slab_ref[pl.ds(i * tokens, tokens), :]
        for j in range(6):
            packed_ref[:, j * part : (j + 1) * part] = dot(x, w_ref[j]).astype(BF16)
        for b in range(passages):
            rows = slice(b * SEQ, (b + 1) * SEQ)
            for pair in range(pairs):
                at = pair * 2 * HEAD
                q = packed_ref[rows, at : at + 2 * HEAD] * jnp.asarray(HEAD**-0.5, BF16)
                k = packed_ref[rows, width + at : width + at + 2 * HEAD]
                scores_ref[b * pairs + pair] = dot(q, stacked(k), ((1,), (1,)))
        for n in range(passages * pairs):
            for h in range(2):
                s = scores_ref[n, :, h * SEQ : (h + 1) * SEQ]
                e = jnp.exp(s - jnp.max(s, axis=1, keepdims=True))
                probs = e * (1.0 / jnp.sum(e, axis=1, keepdims=True))
                probs_ref[n, :, h * SEQ : (h + 1) * SEQ] = probs.astype(BF16)
        for b in range(passages):
            rows = slice(b * SEQ, (b + 1) * SEQ)
            for pair in range(pairs):
                at = pair * 2 * HEAD
                v = packed_ref[rows, 2 * width + at : 2 * width + at + 2 * HEAD]
                context_ref[rows, at : at + 2 * HEAD] = dot(
                    probs_ref[b * pairs + pair], stacked(v)
                ).astype(BF16)
        context = context_ref[...]
        half = width // 2
        mixed = [
            dot(context, w_ref[6 + k]) + x[:, k * half : (k + 1) * half].astype(F32) for k in range(2)
        ]
        mean = sum(jnp.sum(m, axis=1, keepdims=True) for m in mixed) * (1.0 / width)
        center = [m - mean for m in mixed]
        spread = sum(jnp.sum(c * c, axis=1, keepdims=True) for c in center) * (1.0 / width)
        scale = lax.rsqrt(spread + 1e-05)
        for k in range(2):
            cols = slice(k * half, (k + 1) * half)
            out_ref[pl.ds(i * tokens, tokens), cols] = (
                center[k] * scale * gain_ref[:, cols] + bias_ref[:, cols]
            ).astype(BF16)
        return 0

    lax.fori_loop(0, slab_ref.shape[0] // tokens, step, 0)


def encoded(info, rings, slab, gain, bias):
    part = rings[0].shape[1]
    tokens, width = 2 * SEQ, slab.shape[1]
    pairs = tokens // SEQ * HEADS // 2
    return pl.pallas_call(
        encode_kernel,
        out_shape=jax.ShapeDtypeStruct(slab.shape, BF16),
        in_specs=[pl.BlockSpec(memory_space=pltpu.SMEM)]
        + [pl.BlockSpec(memory_space=pltpu.HBM)] * len(rings)
        + [pl.BlockSpec(memory_space=pltpu.VMEM)] * 3,
        out_specs=pl.BlockSpec(memory_space=pltpu.VMEM),
        scratch_shapes=[
            pltpu.VMEM((8, width, part), BF16),
            pltpu.VMEM((tokens, 3 * width), BF16),
            pltpu.VMEM((pairs, SEQ, 2 * SEQ), F32),
            pltpu.VMEM((pairs, SEQ, 2 * SEQ), BF16),
            pltpu.VMEM((tokens, width), BF16),
            pltpu.SemaphoreType.DMA((len(rings),)),
        ],
        compiler_params=pltpu.CompilerParams(vmem_limit_bytes=40 << 20),
    )(info, *rings, slab, gain.reshape(1, width), bias.reshape(1, width))


def score_kernel(info_ref, mine_ref, other_ref, local_ref, *refs):
    parts = refs[0:5]
    out_ref, old_ref, cent_ref, sems = refs[5:]
    step = pl.program_id(0)
    half = pl.num_programs(0) // 2

    @pl.when(step == 0)
    def _():
        rows_of = parts[0].shape[0]
        targets = []
        for back, first, count in RING:
            start = lax.rem(info_ref[0] - back + 4, 4) * rows_of + first * (rows_of // 2)
            start = pl.multiple_of(start, rows_of // 2)
            targets.append(cent_ref.at[pl.ds(start, count * (rows_of // 2)), :])
        put(parts, targets, sems)

    block = cent_ref.shape[1]
    span = 2 * SEQ
    for n in range(mine_ref.shape[0] // span):
        rows = slice(n * span, (n + 1) * span)
        s = dot(jnp.where(step < half, mine_ref[rows, :], other_ref[rows, :]), cent_ref[...])
        peak = jnp.max(s, axis=1, keepdims=True)
        mass = jnp.sum(jnp.exp(s - peak), axis=1, keepdims=True)
        local = jnp.concatenate(
            [jnp.broadcast_to(local_ref[2 * n + z], (SEQ, SEQ)).T[:, 0:1] for z in range(2)], axis=0
        )
        picked = jnp.sum(jnp.where(local == iota((span, block), 1), s, 0.0), axis=1, keepdims=True)
        both = jnp.where(iota((span, 128), 1) == 0, peak + jnp.log(mass), picked)
        x_size = info_ref[5]
        per_step = mine_ref.shape[0] // span
        back = lax.rem(step, half) * per_step + n
        x = lax.rem(info_ref[3] - back + x_size, x_size)
        core = jnp.where(step < half, info_ref[2], 1 - info_ref[2])
        for z in range(2):
            zh = info_ref[4] if z == 0 else 1 - info_ref[4]
            out_ref[zh * (2 * x_size) + x * 2 + core] = both[z * SEQ : (z + 1) * SEQ, :].T[0:8, :]

    @pl.when(step == pl.num_programs(0) - 1)
    def _():
        per = old_ref.shape[0]
        old = cent_ref[:, pl.ds(pl.multiple_of(info_ref[1] * per, per), per)]
        old_ref[...] = old.astype(F32).T


def scored(info, mine, other, local, parts):
    tokens, width = mine.shape
    block = parts[0].shape[1]
    step = 4 * SEQ
    per = step // SEQ
    half = tokens // step
    return pl.pallas_call(
        score_kernel,
        grid=(2 * half,),
        out_shape=(
            jax.ShapeDtypeStruct((2 * tokens // SEQ, 8, SEQ), F32),
            jax.ShapeDtypeStruct((SEQ, width), F32),
        ),
        in_specs=[
            pl.BlockSpec(memory_space=pltpu.SMEM),
            pl.BlockSpec((step, width), lambda i: (jnp.minimum(i, half - 1), 0)),
            pl.BlockSpec((step, width), lambda i: (jnp.maximum(i - half, 0), 0)),
            pl.BlockSpec((per, 1, SEQ), lambda i: (i, 0, 0)),
        ]
        + [pl.BlockSpec(memory_space=pltpu.HBM)] * len(parts),
        out_specs=(
            pl.BlockSpec((2 * tokens // SEQ, 8, SEQ), lambda i: (0, 0, 0)),
            pl.BlockSpec((SEQ, width), lambda i: (0, 0)),
        ),
        scratch_shapes=[
            pltpu.VMEM((width, block), BF16),
            pltpu.SemaphoreType.DMA((len(parts),)),
        ],
        compiler_params=pltpu.CompilerParams(vmem_limit_bytes=48 << 20),
    )(info, mine, other, local.reshape(2 * tokens // SEQ, 1, SEQ), *parts)


def choose_kernel(info_ref, local_ref, out_ref, most_ref):
    tokens = local_ref.shape[1]
    per = 128
    dests = out_ref.shape[0] // ROOM
    first_slot = info_ref[1] * SLOTS
    local = local_ref[...]
    upper = iota((per, per), 0) < iota((per, per), 1)
    diagonal = iota((per, per), 0) == iota((per, per), 1)

    def group(g, most):
        match = jnp.where(local - g * per == iota((per, tokens), 0), 1.0, 0.0)
        hits = match.astype(BF16)
        present = jnp.broadcast_to(jnp.max(match, axis=1, keepdims=True), (per, per))
        rank = jnp.sum(jnp.where(upper, present, 0.0), axis=0, keepdims=True).astype(jnp.int32)
        here = jnp.sum(jnp.where(diagonal, present, 0.0), axis=0, keepdims=True)
        slot = iota((ROOM, per), 0)
        chosen = (slot < SLOTS) & (slot == rank - first_slot) & (here > 0.5)
        packing = jnp.where(chosen, 1.0, 0.0).astype(BF16)
        out_ref[pl.ds(pl.multiple_of(g * ROOM, ROOM), ROOM), :] = dot(packing, hits).astype(BF16)
        return jnp.maximum(most, jnp.sum(here, axis=1, keepdims=True))

    most = lax.fori_loop(0, dests, group, jnp.zeros((1, 1), F32), unroll=4)
    most_ref[...] = jnp.broadcast_to(most, most_ref.shape)


def choices(info, local, dests):
    return pl.pallas_call(
        choose_kernel,
        out_shape=(
            jax.ShapeDtypeStruct((dests * ROOM, local.shape[1]), BF16),
            jax.ShapeDtypeStruct((8, 128), F32),
        ),
        in_specs=[pl.BlockSpec(memory_space=pltpu.SMEM), pl.BlockSpec(memory_space=pltpu.VMEM)],
        out_specs=(pl.BlockSpec(memory_space=pltpu.VMEM), pl.BlockSpec(memory_space=pltpu.VMEM)),
        compiler_params=pltpu.CompilerParams(vmem_limit_bytes=40 << 20),
    )(info, local)


def pack_kernel(hits_ref, most_ref, mine_ref, other_ref, out_ref):
    dests, _, width = out_ref.shape
    half = mine_ref.shape[0]
    sums = dot(hits_ref[:, 0:half], mine_ref[...]) + dot(hits_ref[:, half:], other_ref[...])
    sums = sums.reshape(dests, ROOM, width)[:, 0:BLOCK, :]
    last = iota((dests, BLOCK, width), 1) == SLOTS
    out_ref[...] = jnp.where(last, most_ref[0:1, 0:1].reshape(1, 1, 1), sums).astype(BF16)


def packed_sums(chosen, mine, other):
    hits, most = chosen
    width = mine.shape[1]
    return pl.pallas_call(
        pack_kernel,
        out_shape=jax.ShapeDtypeStruct((hits.shape[0] // ROOM, BLOCK, width), BF16),
        in_specs=[pl.BlockSpec(memory_space=pltpu.VMEM)] * 4,
        out_specs=pl.BlockSpec(memory_space=pltpu.VMEM),
        compiler_params=pltpu.CompilerParams(vmem_limit_bytes=40 << 20),
    )(hits, most, mine, other)


def count_kernel(info_ref, assign_ref, out_ref):
    dp, slabs, _ = assign_ref.shape
    targets = iota((128, SEQ), 0) + info_ref[0]
    lane = iota(out_ref.shape, 1)

    def slab(f, out):
        acc = jnp.zeros((128, SEQ), F32)
        for d in range(dp):
            acc = acc + jnp.where(assign_ref[d, pl.ds(f, 1), :] == targets, 1.0, 0.0)
        return jnp.where(lane == f, jnp.sum(acc, axis=1, keepdims=True), out)

    out_ref[...] = lax.fori_loop(0, slabs, slab, jnp.zeros(out_ref.shape, F32))


def counted(info, assign):
    return pl.pallas_call(
        count_kernel,
        out_shape=jax.ShapeDtypeStruct((128, 128), F32),
        in_specs=[pl.BlockSpec(memory_space=pltpu.SMEM), pl.BlockSpec(memory_space=pltpu.VMEM)],
        out_specs=pl.BlockSpec(memory_space=pltpu.VMEM),
    )(info, assign)


def unpack_kernel(info_ref, counts_ref, got_ref, out_ref, most_ref):
    slabs, _, width = got_ref.shape
    counts = counts_ref[...]
    present = jnp.where(counts > 0.5, 1.0, 0.0).astype(BF16)
    lower = jnp.where(iota((128, 128), 1) < iota((128, 128), 0), 1.0, 0.0).astype(BF16)
    rank = dot(lower, present).astype(jnp.int32) - info_ref[1] * SLOTS
    slot = iota((128, BLOCK), 1)
    parts = []
    for f in range(slabs):
        chosen = (slot == rank[:, f : f + 1]) & (slot < SLOTS) & (counts[:, f : f + 1] > 0.5)
        parts.append(jnp.where(chosen, 1.0, 0.0))
    hits = jnp.concatenate(parts, axis=1).astype(BF16)
    out_ref[...] = dot(hits, got_ref[...].reshape(slabs * BLOCK, width))
    most = jnp.max(got_ref[:, SLOTS, 0:128].astype(F32), axis=0, keepdims=True)
    most_ref[...] = jnp.broadcast_to(most, most_ref.shape).astype(jnp.int32)


def unpacked_sums(info, counts, got):
    return pl.pallas_call(
        unpack_kernel,
        out_shape=(
            jax.ShapeDtypeStruct((128, got.shape[2]), F32),
            jax.ShapeDtypeStruct((8, 128), jnp.int32),
        ),
        in_specs=[pl.BlockSpec(memory_space=pltpu.SMEM)]
        + [pl.BlockSpec(memory_space=pltpu.VMEM)] * 2,
        out_specs=(pl.BlockSpec(memory_space=pltpu.VMEM), pl.BlockSpec(memory_space=pltpu.VMEM)),
    )(info, counts, got)


def exchanged(blocks, axis):
    return lax.all_to_all(blocks, axis, 0, 0, tiled=True)


def gathered(shard, axis):
    devices = lax.axis_size(axis)
    return exchanged(jnp.broadcast_to(shard[None], (devices,) + shard.shape), axis)


def swapped(shard, axis):
    return lax.ppermute(shard, axis, [(0, 1), (1, 0)])


def turned(shard, axis, by):
    devices = lax.axis_size(axis)
    return lax.ppermute(shard, axis, [(i, (i + by) % devices) for i in range(devices)])


def neighbours(block, axis):
    return turned(block, axis, 1), turned(block, axis, lax.axis_size(axis) - 1)


def far_halves(back, ahead, axis):
    half = back.shape[0] // 2
    return turned(back[:half], axis, 1), turned(ahead[half:], axis, lax.axis_size(axis) - 1)


def backwards(values, here):
    for dim, at in enumerate(here):
        size = values.shape[dim]
        values = jnp.take(values, (at - jnp.arange(size)) % size, axis=dim)
    return values


def shards(token_ids, embed_table, w_qkv, w_out, ln_gain, ln_bias, centroids_t, assignments):
    core = lax.axis_index("core")
    dp_rank = lax.axis_index(DP)
    fs_rank = lax.axis_index(FS)
    fs_size = lax.axis_size(FS)
    dp_size = lax.axis_size(DP)
    x_size = lax.axis_size("x")
    vocab, width = embed_table.shape
    zero = jnp.int32(0)
    ids = token_ids.reshape(fs_size, SEQ)

    at_x = lax.axis_index("x")

    def info_of(*values):
        return jnp.stack([jnp.asarray(v, jnp.int32) for v in values])

    by_dev = assignments.reshape(2, x_size, 2, fs_size, SEQ)
    of_slab = lax.dynamic_index_in_dim(by_dev, fs_rank, 3, keepdims=False)
    of_slab = jnp.transpose(of_slab, (2, 1, 0, 3))
    here = (core, at_x, lax.axis_index("zh"))
    of_slab = backwards(of_slab, here)
    block = centroids_t.shape[1]
    local = of_slab.reshape(1, -1) - dp_rank * block
    chosen = choices(info_of(zero, zero), local, fs_size)
    counts = counted(
        info_of(dp_rank * block + fs_rank * (block // fs_size)),
        assignments.reshape(dp_size, fs_size, SEQ),
    )

    near = gathered(centroids_t, "zl").reshape(-1, block)
    back, ahead = neighbours(near, "y")
    far_low, far_high = far_halves(back, ahead, "y")

    part = (w_qkv.shape[1] + w_out.shape[1]) // (2 * x_size)
    both = jnp.concatenate([w_qkv, w_out], axis=1)
    piece = lax.dynamic_slice_in_dim(both, (core * x_size + at_x) * part, part, 1)
    piece, near = lax.optimization_barrier((piece, near))
    column = gathered(piece, FS).reshape(width, part)

    two = jnp.concatenate([ids, swapped(ids, "zh")], axis=0)
    ids = [two] + [turned(two, "x", k) for k in range(1, x_size)]

    sent = listed_rows(info_of(fs_rank, zero), ids, embed_table)
    sent, column, chosen, local = lax.optimization_barrier((sent, column, chosen, local))
    w_back, w_ahead = neighbours(column, "x")
    rings = [column, w_back, *far_halves(w_back, w_ahead, "x"), w_ahead]
    places = placed_rows(info_of(fs_rank, zero, vocab), ids, fs_size)
    rings += [swapped(w, "core") for w in rings]
    got = exchanged(sent, FS)
    got, places, counts, back, ahead, *rings = lax.optimization_barrier(
        (got, places, counts, back, ahead, *rings)
    )
    slab, rounds = expanded(places, got)

    def more_rows(state):
        turn, acc = state
        again = exchanged(listed_rows(info_of(fs_rank, turn), ids, embed_table), FS)
        extra, _ = expanded(placed_rows(info_of(fs_rank, turn, vocab), ids, fs_size), again)
        return turn + 1, acc + extra

    rounds = rounds[0, 0]
    _, slab = lax.while_loop(lambda state: state[0] < rounds, more_rows, (jnp.int32(1), slab))

    mine = encoded(info_of(core, at_x), rings, slab, ln_gain, ln_bias)
    mine, far_low, far_high = lax.optimization_barrier((mine, far_low, far_high))
    other = swapped(mine, "core")

    def one_turn(turn):
        info = info_of(zero, turn)
        got = exchanged(packed_sums(choices(info, local, fs_size), mine, other), FS)
        return unpacked_sums(info, counts, got)[0]

    packed = packed_sums(chosen, mine, other)
    packed, mine, other = lax.optimization_barrier((packed, mine, other))
    got = exchanged(packed, FS)

    stats, previous = scored(
        info_of(lax.axis_index("y"), fs_rank, *here, x_size),
        mine,
        other,
        local,
        [near, back, far_low, far_high, ahead],
    )
    stats, got = lax.optimization_barrier((stats, got))
    sums, widest = unpacked_sums(info_of(zero, zero), counts, got)
    widest = widest[0, 0]
    _, sums = lax.while_loop(
        lambda state: state[0] * SLOTS < widest,
        lambda state: (state[0] + 1, state[1] + one_turn(state[0])),
        (jnp.int32(1), sums),
    )

    home = exchanged(stats, DP)
    lse = home[:, 0, :]
    peak = jnp.max(lse, axis=0)
    token_loss = (
        jnp.log(jnp.sum(jnp.exp(lse - peak[None, :]), axis=0)) + peak - jnp.sum(home[:, 1, :], axis=0)
    )

    total = jnp.sum(counts[:, 0:fs_size], axis=1, keepdims=True)
    new_centroids = jnp.where(total > 0, sums / jnp.maximum(total, 1.0), previous)
    return token_loss, new_centroids


def solution(mesh):
    finer = Mesh(mesh.devices.reshape(2, 4, 2, 4, 4), ALL)
    placed = (P(DP), P(FS, None), P(FS, None), P(FS, None), P(), P(), P(FS, DP), P())
    return jax.shard_map(
        shards, mesh=finer, in_specs=placed, out_specs=(P(ALL), P(ALL, None)), check_vma=False
    )
```

```python
import jax
import jax.numpy as jnp
from jax import lax
from jax.experimental import pallas as pl
from jax.experimental.pallas import tpu as pltpu
from jax.sharding import Mesh
from jax.sharding import PartitionSpec as P

HEADS = 12
HEAD = 64
SEQ = 128
DP = ("zh", "x", "core")
FS = ("y", "zl")
ALL = DP + FS
LIST = 47
SLOTS = 39
BLOCK = SLOTS + 1
ROOM = 48
F32 = jnp.float32
BF16 = jnp.bfloat16


RING = ((0, 0, 2), (1, 0, 2), (2, 0, 1), (2, 1, 1), (3, 0, 2))


def iota(shape, dim):
    return lax.broadcasted_iota(jnp.int32, shape, dim)


def dot(a, b, dims=((1,), (0,))):
    return lax.dot_general(a, b, (dims, ((), ())), preferred_element_type=F32)


def ranked(present, groups):
    rows = present.shape[0]
    per = rows // groups
    upper = jnp.where(iota((128, 128), 0) < iota((128, 128), 1), 1.0, 0.0).astype(BF16)
    at, of = iota((rows, rows), 0), iota((rows, rows), 1)
    above = jnp.where((at // per == of // per) & (of < at), 1.0, 0.0).astype(BF16)
    ones = present.astype(BF16)
    return dot(ones, upper) + jnp.sum(dot(above, ones), axis=1, keepdims=True)


def tokens_of(ids_refs, dest):
    dests = ids_refs[0].shape[0] // 2
    return jnp.concatenate(
        [ref[pl.ds(z * dests + dest, 1), :] for ref in ids_refs for z in range(2)], axis=1
    )


def lists_kernel(info_ref, *refs):
    ids_refs, table_ref, rows_ref, present_ref, rank_ref, hits_ref = refs[0:4], *refs[4:]
    vocab = table_ref.shape[0]
    dests, tokens = rows_ref.shape[0], 8 * SEQ
    base = info_ref[0] * vocab
    first_slot = info_ref[1] * LIST
    high = 16

    def find(p, _):
        local = tokens_of(ids_refs, p) - base
        inside = (local >= 0) & (local < vocab)
        block = jnp.where((iota((high, tokens), 0) == (local >> 7)) & inside, 1.0, 0.0).astype(BF16)
        lane = jnp.where(iota((128, tokens), 0) == (local & 127), 1.0, 0.0).astype(BF16)
        seen = dot(block, lane, ((1,), (1,)))
        present_ref[pl.ds(pl.multiple_of(p * high, high), high), :] = jnp.where(seen > 0.5, 1.0, 0.0)
        return 0

    lax.fori_loop(0, dests, find, 0, unroll=2)
    present = present_ref[...]
    rank_ref[...] = jnp.where(present > 0.5, ranked(present, dests) - first_slot.astype(F32), -1.0)
    blocks = -(-vocab // 128)

    def choose(p, most):
        ranks = rank_ref[pl.ds(pl.multiple_of(p * high, high), high), :]
        slot = iota((ROOM, 128), 0)
        for h in range(blocks):
            chosen = (slot == ranks[h : h + 1, :].astype(jnp.int32)) & (slot < LIST)
            hits_ref[pl.ds(pl.multiple_of(p * ROOM, ROOM), ROOM), h * 128 : (h + 1) * 128] = jnp.where(
                chosen, 1.0, 0.0
            ).astype(BF16)
        return jnp.maximum(most, jnp.max(ranks))

    most = lax.fori_loop(0, dests, choose, jnp.float32(-1.0)) + first_slot.astype(F32)
    whole = vocab // 16 * 16
    rows = dot(hits_ref[:, 0:whole], table_ref[0:whole, :])
    if whole < vocab:
        tail = table_ref[whole:vocab, :].astype(F32)
        for k in range(vocab - whole):
            rows = rows + hits_ref[:, whole + k : whole + k + 1].astype(F32) * tail[k : k + 1, :]
    rounds = jnp.floor(most * (1.0 / LIST) + 1e-3) + 1.0
    rows = rows.reshape(rows_ref.shape)
    rows_ref[...] = jnp.where(iota(rows.shape, 1) == LIST, rounds, rows).astype(BF16)


def listed_rows(info, ids, table):
    dests = ids[0].shape[0] // 2
    width = table.shape[1]
    return pl.pallas_call(
        lists_kernel,
        out_shape=jax.ShapeDtypeStruct((dests, ROOM, width), BF16),
        in_specs=[pl.BlockSpec(memory_space=pltpu.SMEM)]
        + [pl.BlockSpec(memory_space=pltpu.VMEM)] * (len(ids) + 1),
        out_specs=pl.BlockSpec(memory_space=pltpu.VMEM),
        scratch_shapes=[
            pltpu.VMEM((dests * 16, 128), F32),
            pltpu.VMEM((dests * 16, 128), F32),
            pltpu.VMEM((dests * ROOM, 16 * 128), BF16),
        ],
        compiler_params=pltpu.CompilerParams(vmem_limit_bytes=40 << 20),
    )(info, *ids, table)


def place_kernel(info_ref, *refs):
    ids_refs, out_ref = refs[0:4], refs[4]
    tokens = 8 * SEQ
    owners = out_ref.shape[1] // ROOM
    first_slot = info_ref[1] * LIST
    vocab = info_ref[2]
    row = tokens_of(ids_refs, info_ref[0])
    owner = jnp.zeros(row.shape, jnp.int32)
    for k in range(1, owners):
        owner = owner + jnp.where(row >= k * vocab, 1, 0)
    local = row - owner * vocab
    group = owner * 16 + (local >> 7)
    block = jnp.where(iota((owners * 16, tokens), 0) == group, 1.0, 0.0).astype(BF16)
    lane = jnp.where(iota((128, tokens), 0) == (local & 127), 1.0, 0.0).astype(BF16)
    present = jnp.where(dot(block, lane, ((1,), (1,))) > 0.5, 1.0, 0.0)
    rank = ranked(present, owners) - first_slot.astype(F32)
    rank = jnp.where((rank >= 0) & (rank < LIST), rank, 255.0).astype(BF16)
    owner = owner.astype(F32)
    low = (local & 127).astype(F32)
    for t in range(tokens // 128):
        cols = slice(t * 128, (t + 1) * 128)
        found = lax.dot_general(
            block[:, cols], rank, (((0,), (0,)), ((), ())), preferred_element_type=F32
        )
        down = jnp.broadcast_to(low[:, cols], (128, 128)).T
        slot = jnp.sum(jnp.where(iota((128, 128), 1).astype(F32) == down, found, 0.0), axis=1, keepdims=True)
        of = jnp.broadcast_to(owner[:, cols], (128, 128)).T[:, 0:1]
        place = jnp.where(slot < LIST, of * ROOM + slot, -1.0).astype(jnp.int32)
        out_ref[cols, :] = jnp.where(place == iota((128, owners * ROOM), 1), 1.0, 0.0).astype(BF16)


def placed_rows(info, ids, owners):
    return pl.pallas_call(
        place_kernel,
        out_shape=jax.ShapeDtypeStruct((8 * SEQ, owners * ROOM), BF16),
        in_specs=[pl.BlockSpec(memory_space=pltpu.SMEM)]
        + [pl.BlockSpec(memory_space=pltpu.VMEM)] * len(ids),
        out_specs=pl.BlockSpec(memory_space=pltpu.VMEM),
        compiler_params=pltpu.CompilerParams(vmem_limit_bytes=40 << 20),
    )(info, *ids)


def expand_kernel(places_ref, got_ref, out_ref, rounds_ref):
    owners, room, width = got_ref.shape
    out_ref[...] = dot(places_ref[...], got_ref[...].reshape(owners * room, width)).astype(BF16)
    most = jnp.max(got_ref[:, LIST, 0:128].astype(F32), axis=0, keepdims=True)
    rounds_ref[...] = jnp.broadcast_to(most, rounds_ref.shape).astype(jnp.int32)


def expanded(places, got):
    return pl.pallas_call(
        expand_kernel,
        out_shape=(
            jax.ShapeDtypeStruct((places.shape[0], got.shape[2]), BF16),
            jax.ShapeDtypeStruct((8, 128), jnp.int32),
        ),
        in_specs=[pl.BlockSpec(memory_space=pltpu.VMEM)] * 2,
        out_specs=(pl.BlockSpec(memory_space=pltpu.VMEM), pl.BlockSpec(memory_space=pltpu.VMEM)),
        compiler_params=pltpu.CompilerParams(vmem_limit_bytes=40 << 20),
    )(places, got)


def put(sources, targets, sems):
    copies = [
        pltpu.make_async_copy(src, dst, sems.at[k])
        for k, (src, dst) in enumerate(zip(sources, targets, strict=True))
    ]
    for c in copies:
        c.start()
    for c in copies:
        c.wait()


def encode_kernel(info_ref, *refs):
    rings = refs[0:10]
    slab_ref, gain_ref, bias_ref, out_ref, w_ref, packed_ref, scores_ref, probs_ref, context_ref, sems = (
        refs[10:]
    )
    x_size = 4
    core, at_x = info_ref[0], info_ref[1]
    depth, part = w_ref.shape[1:]
    targets = []
    for core_at in (core, 1 - core):
        for back, first, count in RING:
            place = core_at * x_size + lax.rem(at_x - back + x_size, x_size)
            targets.append(w_ref.at[place, pl.ds(first * (depth // 2), count * (depth // 2)), :])
    put(rings, targets, sems)
    tokens, width = packed_ref.shape[0], slab_ref.shape[1]
    left = iota((SEQ, 2 * HEAD), 1) < HEAD
    zero = jnp.zeros((SEQ, 2 * HEAD), BF16)
    pairs = HEADS // 2
    passages = tokens // SEQ

    def stacked(values):
        return jnp.concatenate([jnp.where(left, values, zero), jnp.where(left, zero, values)], axis=0)

    def step(i, _):
        x = slab_ref[pl.ds(i * tokens, tokens), :]
        for j in range(6):
            packed_ref[:, j * part : (j + 1) * part] = dot(x, w_ref[j]).astype(BF16)
        for b in range(passages):
            rows = slice(b * SEQ, (b + 1) * SEQ)
            for pair in range(pairs):
                at = pair * 2 * HEAD
                q = packed_ref[rows, at : at + 2 * HEAD] * jnp.asarray(HEAD**-0.5, BF16)
                k = packed_ref[rows, width + at : width + at + 2 * HEAD]
                scores_ref[b * pairs + pair] = dot(q, stacked(k), ((1,), (1,)))

        def softmax(n, _):
            for h in range(2):
                s = scores_ref[n, :, h * SEQ : (h + 1) * SEQ]
                e = jnp.exp(s - jnp.max(s, axis=1, keepdims=True))
                probs = e * (1.0 / jnp.sum(e, axis=1, keepdims=True))
                probs_ref[n, :, h * SEQ : (h + 1) * SEQ] = probs.astype(BF16)
            return 0

        lax.fori_loop(0, passages * pairs, softmax, 0, unroll=4)
        for b in range(passages):
            rows = slice(b * SEQ, (b + 1) * SEQ)
            for pair in range(pairs):
                at = pair * 2 * HEAD
                v = packed_ref[rows, 2 * width + at : 2 * width + at + 2 * HEAD]
                context_ref[rows, at : at + 2 * HEAD] = dot(
                    probs_ref[b * pairs + pair], stacked(v)
                ).astype(BF16)
        context = context_ref[...]
        half = width // 2
        mixed = [
            dot(context, w_ref[6 + k]) + x[:, k * half : (k + 1) * half].astype(F32) for k in range(2)
        ]
        mean = sum(jnp.sum(m, axis=1, keepdims=True) for m in mixed) * (1.0 / width)
        center = [m - mean for m in mixed]
        spread = sum(jnp.sum(c * c, axis=1, keepdims=True) for c in center) * (1.0 / width)
        scale = lax.rsqrt(spread + 1e-05)
        for k in range(2):
            cols = slice(k * half, (k + 1) * half)
            out_ref[pl.ds(i * tokens, tokens), cols] = (
                center[k] * scale * gain_ref[:, cols] + bias_ref[:, cols]
            ).astype(BF16)
        return 0

    lax.fori_loop(0, slab_ref.shape[0] // tokens, step, 0)


def encoded(info, rings, slab, gain, bias):
    part = rings[0].shape[1]
    tokens, width = 2 * SEQ, slab.shape[1]
    pairs = tokens // SEQ * HEADS // 2
    return pl.pallas_call(
        encode_kernel,
        out_shape=jax.ShapeDtypeStruct(slab.shape, BF16),
        in_specs=[pl.BlockSpec(memory_space=pltpu.SMEM)]
        + [pl.BlockSpec(memory_space=pltpu.HBM)] * len(rings)
        + [pl.BlockSpec(memory_space=pltpu.VMEM)] * 3,
        out_specs=pl.BlockSpec(memory_space=pltpu.VMEM),
        scratch_shapes=[
            pltpu.VMEM((8, width, part), BF16),
            pltpu.VMEM((tokens, 3 * width), BF16),
            pltpu.VMEM((pairs, SEQ, 2 * SEQ), F32),
            pltpu.VMEM((pairs, SEQ, 2 * SEQ), BF16),
            pltpu.VMEM((tokens, width), BF16),
            pltpu.SemaphoreType.DMA((len(rings),)),
        ],
        compiler_params=pltpu.CompilerParams(vmem_limit_bytes=40 << 20),
    )(info, *rings, slab, gain.reshape(1, width), bias.reshape(1, width))


def score_kernel(info_ref, mine_ref, other_ref, local_ref, *refs):
    parts = refs[0:5]
    out_ref, old_ref, cent_ref, sems = refs[5:]
    step = pl.program_id(0)
    half = pl.num_programs(0) // 2

    @pl.when(step == 0)
    def _():
        rows_of = parts[0].shape[0]
        targets = []
        for back, first, count in RING:
            start = lax.rem(info_ref[0] - back + 4, 4) * rows_of + first * (rows_of // 2)
            start = pl.multiple_of(start, rows_of // 2)
            targets.append(cent_ref.at[pl.ds(start, count * (rows_of // 2)), :])
        put(parts, targets, sems)

    block = cent_ref.shape[1]
    span = 2 * SEQ
    for n in range(mine_ref.shape[0] // span):
        rows = slice(n * span, (n + 1) * span)
        s = dot(jnp.where(step < half, mine_ref[rows, :], other_ref[rows, :]), cent_ref[...])
        peak = jnp.max(s, axis=1, keepdims=True)
        mass = jnp.sum(jnp.exp(s - peak), axis=1, keepdims=True)
        local = jnp.concatenate(
            [jnp.broadcast_to(local_ref[2 * n + z], (SEQ, SEQ)).T[:, 0:1] for z in range(2)], axis=0
        )
        picked = jnp.sum(jnp.where(local == iota((span, block), 1), s, 0.0), axis=1, keepdims=True)
        both = jnp.where(iota((span, 128), 1) == 0, peak + jnp.log(mass), picked)
        x_size = info_ref[5]
        per_step = mine_ref.shape[0] // span
        back = lax.rem(step, half) * per_step + n
        x = lax.rem(info_ref[3] - back + x_size, x_size)
        core = jnp.where(step < half, info_ref[2], 1 - info_ref[2])
        for z in range(2):
            zh = info_ref[4] if z == 0 else 1 - info_ref[4]
            out_ref[zh * (2 * x_size) + x * 2 + core] = both[z * SEQ : (z + 1) * SEQ, :].T[0:8, :]

    @pl.when(step == pl.num_programs(0) - 1)
    def _():
        per = old_ref.shape[0]
        old = cent_ref[:, pl.ds(pl.multiple_of(info_ref[1] * per, per), per)]
        old_ref[...] = old.astype(F32).T


def scored(info, mine, other, local, parts):
    tokens, width = mine.shape
    block = parts[0].shape[1]
    step = 4 * SEQ
    per = step // SEQ
    half = tokens // step
    return pl.pallas_call(
        score_kernel,
        grid=(2 * half,),
        out_shape=(
            jax.ShapeDtypeStruct((2 * tokens // SEQ, 8, SEQ), F32),
            jax.ShapeDtypeStruct((SEQ, width), F32),
        ),
        in_specs=[
            pl.BlockSpec(memory_space=pltpu.SMEM),
            pl.BlockSpec((step, width), lambda i: (jnp.minimum(i, half - 1), 0)),
            pl.BlockSpec((step, width), lambda i: (jnp.maximum(i - half, 0), 0)),
            pl.BlockSpec((per, 1, SEQ), lambda i: (i, 0, 0)),
        ]
        + [pl.BlockSpec(memory_space=pltpu.HBM)] * len(parts),
        out_specs=(
            pl.BlockSpec((2 * tokens // SEQ, 8, SEQ), lambda i: (0, 0, 0)),
            pl.BlockSpec((SEQ, width), lambda i: (0, 0)),
        ),
        scratch_shapes=[
            pltpu.VMEM((width, block), BF16),
            pltpu.SemaphoreType.DMA((len(parts),)),
        ],
        compiler_params=pltpu.CompilerParams(vmem_limit_bytes=48 << 20),
    )(info, mine, other, local.reshape(2 * tokens // SEQ, 1, SEQ), *parts)


def choose_kernel(info_ref, local_ref, out_ref, most_ref):
    tokens = local_ref.shape[1]
    per = 128
    dests = out_ref.shape[0] // ROOM
    first_slot = info_ref[1] * SLOTS
    local = local_ref[...]
    upper = iota((per, per), 0) < iota((per, per), 1)
    diagonal = iota((per, per), 0) == iota((per, per), 1)

    def group(g, most):
        match = jnp.where(local - g * per == iota((per, tokens), 0), 1.0, 0.0)
        hits = match.astype(BF16)
        present = jnp.broadcast_to(jnp.max(match, axis=1, keepdims=True), (per, per))
        rank = jnp.sum(jnp.where(upper, present, 0.0), axis=0, keepdims=True).astype(jnp.int32)
        here = jnp.sum(jnp.where(diagonal, present, 0.0), axis=0, keepdims=True)
        slot = iota((ROOM, per), 0)
        chosen = (slot < SLOTS) & (slot == rank - first_slot) & (here > 0.5)
        packing = jnp.where(chosen, 1.0, 0.0).astype(BF16)
        out_ref[pl.ds(pl.multiple_of(g * ROOM, ROOM), ROOM), :] = dot(packing, hits).astype(BF16)
        return jnp.maximum(most, jnp.sum(here, axis=1, keepdims=True))

    most = lax.fori_loop(0, dests, group, jnp.zeros((1, 1), F32), unroll=2)
    most_ref[...] = jnp.broadcast_to(most, most_ref.shape)


def choices(info, local, dests):
    return pl.pallas_call(
        choose_kernel,
        out_shape=(
            jax.ShapeDtypeStruct((dests * ROOM, local.shape[1]), BF16),
            jax.ShapeDtypeStruct((8, 128), F32),
        ),
        in_specs=[pl.BlockSpec(memory_space=pltpu.SMEM), pl.BlockSpec(memory_space=pltpu.VMEM)],
        out_specs=(pl.BlockSpec(memory_space=pltpu.VMEM), pl.BlockSpec(memory_space=pltpu.VMEM)),
        compiler_params=pltpu.CompilerParams(vmem_limit_bytes=40 << 20),
    )(info, local)


def pack_kernel(hits_ref, most_ref, mine_ref, other_ref, out_ref):
    dests, _, width = out_ref.shape
    half = mine_ref.shape[0]
    sums = dot(hits_ref[:, 0:half], mine_ref[...]) + dot(hits_ref[:, half:], other_ref[...])
    sums = sums.reshape(dests, ROOM, width)[:, 0:BLOCK, :]
    last = iota((dests, BLOCK, width), 1) == SLOTS
    out_ref[...] = jnp.where(last, most_ref[0:1, 0:1].reshape(1, 1, 1), sums).astype(BF16)


def packed_sums(chosen, mine, other):
    hits, most = chosen
    width = mine.shape[1]
    return pl.pallas_call(
        pack_kernel,
        out_shape=jax.ShapeDtypeStruct((hits.shape[0] // ROOM, BLOCK, width), BF16),
        in_specs=[pl.BlockSpec(memory_space=pltpu.VMEM)] * 4,
        out_specs=pl.BlockSpec(memory_space=pltpu.VMEM),
        compiler_params=pltpu.CompilerParams(vmem_limit_bytes=40 << 20),
    )(hits, most, mine, other)


def count_kernel(info_ref, assign_ref, out_ref):
    dp, slabs, _ = assign_ref.shape
    targets = iota((128, SEQ), 0) + info_ref[0]
    lane = iota(out_ref.shape, 1)

    def slab(f, out):
        acc = jnp.zeros((128, SEQ), F32)
        for d in range(dp):
            acc = acc + jnp.where(assign_ref[d, pl.ds(f, 1), :] == targets, 1.0, 0.0)
        return jnp.where(lane == f, jnp.sum(acc, axis=1, keepdims=True), out)

    out_ref[...] = lax.fori_loop(0, slabs, slab, jnp.zeros(out_ref.shape, F32))


def counted(info, assign):
    return pl.pallas_call(
        count_kernel,
        out_shape=jax.ShapeDtypeStruct((128, 128), F32),
        in_specs=[pl.BlockSpec(memory_space=pltpu.SMEM), pl.BlockSpec(memory_space=pltpu.VMEM)],
        out_specs=pl.BlockSpec(memory_space=pltpu.VMEM),
    )(info, assign)


def unpack_kernel(info_ref, counts_ref, got_ref, out_ref, most_ref):
    slabs, _, width = got_ref.shape
    counts = counts_ref[...]
    present = jnp.where(counts > 0.5, 1.0, 0.0).astype(BF16)
    lower = jnp.where(iota((128, 128), 1) < iota((128, 128), 0), 1.0, 0.0).astype(BF16)
    rank = dot(lower, present).astype(jnp.int32) - info_ref[1] * SLOTS
    slot = iota((128, BLOCK), 1)
    parts = []
    for f in range(slabs):
        chosen = (slot == rank[:, f : f + 1]) & (slot < SLOTS) & (counts[:, f : f + 1] > 0.5)
        parts.append(jnp.where(chosen, 1.0, 0.0))
    hits = jnp.concatenate(parts, axis=1).astype(BF16)
    out_ref[...] = dot(hits, got_ref[...].reshape(slabs * BLOCK, width))
    most = jnp.max(got_ref[:, SLOTS, 0:128].astype(F32), axis=0, keepdims=True)
    most_ref[...] = jnp.broadcast_to(most, most_ref.shape).astype(jnp.int32)


def unpacked_sums(info, counts, got):
    return pl.pallas_call(
        unpack_kernel,
        out_shape=(
            jax.ShapeDtypeStruct((128, got.shape[2]), F32),
            jax.ShapeDtypeStruct((8, 128), jnp.int32),
        ),
        in_specs=[pl.BlockSpec(memory_space=pltpu.SMEM)]
        + [pl.BlockSpec(memory_space=pltpu.VMEM)] * 2,
        out_specs=(pl.BlockSpec(memory_space=pltpu.VMEM), pl.BlockSpec(memory_space=pltpu.VMEM)),
    )(info, counts, got)


def exchanged(blocks, axis):
    return lax.all_to_all(blocks, axis, 0, 0, tiled=True)


def gathered(shard, axis):
    devices = lax.axis_size(axis)
    return exchanged(jnp.broadcast_to(shard[None], (devices,) + shard.shape), axis)


def swapped(shard, axis):
    return lax.ppermute(shard, axis, [(0, 1), (1, 0)])


def turned(shard, axis, by):
    devices = lax.axis_size(axis)
    return lax.ppermute(shard, axis, [(i, (i + by) % devices) for i in range(devices)])


def neighbours(block, axis):
    return turned(block, axis, 1), turned(block, axis, lax.axis_size(axis) - 1)


def far_halves(back, ahead, axis):
    half = back.shape[0] // 2
    return turned(back[:half], axis, 1), turned(ahead[half:], axis, lax.axis_size(axis) - 1)


def backwards(values, here):
    for dim, at in enumerate(here):
        size = values.shape[dim]
        values = jnp.take(values, (at - jnp.arange(size)) % size, axis=dim)
    return values


def shards(token_ids, embed_table, w_qkv, w_out, ln_gain, ln_bias, centroids_t, assignments):
    core = lax.axis_index("core")
    dp_rank = lax.axis_index(DP)
    fs_rank = lax.axis_index(FS)
    fs_size = lax.axis_size(FS)
    dp_size = lax.axis_size(DP)
    x_size = lax.axis_size("x")
    vocab, width = embed_table.shape
    zero = jnp.int32(0)
    ids = token_ids.reshape(fs_size, SEQ)

    at_x = lax.axis_index("x")

    def info_of(*values):
        return jnp.stack([jnp.asarray(v, jnp.int32) for v in values])

    by_dev = assignments.reshape(2, x_size, 2, fs_size, SEQ)
    of_slab = lax.dynamic_index_in_dim(by_dev, fs_rank, 3, keepdims=False)
    of_slab = jnp.transpose(of_slab, (2, 1, 0, 3))
    here = (core, at_x, lax.axis_index("zh"))
    of_slab = backwards(of_slab, here)
    block = centroids_t.shape[1]
    local = of_slab.reshape(1, -1) - dp_rank * block
    chosen = choices(info_of(zero, zero), local, fs_size)
    counts = counted(
        info_of(dp_rank * block + fs_rank * (block // fs_size)),
        assignments.reshape(dp_size, fs_size, SEQ),
    )

    blocks = jnp.broadcast_to(centroids_t[None], (lax.axis_size("zl"),) + centroids_t.shape)

    part = (w_qkv.shape[1] + w_out.shape[1]) // (2 * x_size)
    both = jnp.concatenate([w_qkv, w_out], axis=1)
    piece = lax.dynamic_slice_in_dim(both, (core * x_size + at_x) * part, part, 1)
    column = gathered(piece, FS).reshape(width, part)

    two = jnp.concatenate([ids, swapped(ids, "zh")], axis=0)
    ids = [two] + [turned(two, "x", k) for k in range(1, x_size)]

    sent = listed_rows(info_of(fs_rank, zero), ids, embed_table)
    sent, column, local = lax.optimization_barrier((sent, column, local))
    w_back, w_ahead = neighbours(column, "x")
    rings = [column, w_back, *far_halves(w_back, w_ahead, "x"), w_ahead]
    places = placed_rows(info_of(fs_rank, zero, vocab), ids, fs_size)
    rings += [swapped(w, "core") for w in rings]
    got = exchanged(sent, FS)
    got, places, chosen, blocks, *rings = lax.optimization_barrier((got, places, chosen, blocks, *rings))
    slab, rounds = expanded(places, got)

    def more_rows(state):
        turn, acc = state
        again = exchanged(listed_rows(info_of(fs_rank, turn), ids, embed_table), FS)
        extra, _ = expanded(placed_rows(info_of(fs_rank, turn, vocab), ids, fs_size), again)
        return turn + 1, acc + extra

    rounds = rounds[0, 0]
    _, slab = lax.while_loop(lambda state: state[0] < rounds, more_rows, (jnp.int32(1), slab))

    near = exchanged(blocks, "zl").reshape(-1, block)
    back, ahead = neighbours(near, "y")
    far_low, far_high = far_halves(back, ahead, "y")

    mine = encoded(info_of(core, at_x), rings, slab, ln_gain, ln_bias)
    mine, near = lax.optimization_barrier((mine, near))
    other = swapped(mine, "core")

    def one_turn(turn):
        info = info_of(zero, turn)
        got = exchanged(packed_sums(choices(info, local, fs_size), mine, other), FS)
        return unpacked_sums(info, counts, got)[0]

    packed = packed_sums(chosen, mine, other)
    packed, mine, other, back, ahead = lax.optimization_barrier((packed, mine, other, back, ahead))
    got = exchanged(packed, FS)

    stats, previous = scored(
        info_of(lax.axis_index("y"), fs_rank, *here, x_size),
        mine,
        other,
        local,
        [near, back, far_low, far_high, ahead],
    )
    stats, got = lax.optimization_barrier((stats, got))
    sums, widest = unpacked_sums(info_of(zero, zero), counts, got)
    widest = widest[0, 0]
    _, sums = lax.while_loop(
        lambda state: state[0] * SLOTS < widest,
        lambda state: (state[0] + 1, state[1] + one_turn(state[0])),
        (jnp.int32(1), sums),
    )

    home = exchanged(stats, DP)
    lse = home[:, 0, :]
    peak = jnp.max(lse, axis=0)
    token_loss = (
        jnp.log(jnp.sum(jnp.exp(lse - peak[None, :]), axis=0)) + peak - jnp.sum(home[:, 1, :], axis=0)
    )

    total = jnp.sum(counts[:, 0:fs_size], axis=1, keepdims=True)
    new_centroids = jnp.where(total > 0, sums / jnp.maximum(total, 1.0), previous)
    return token_loss, new_centroids


def solution(mesh):
    finer = Mesh(mesh.devices.reshape(2, 4, 2, 4, 4), ALL)
    placed = (P(DP), P(FS, None), P(FS, None), P(FS, None), P(), P(), P(FS, DP), P())
    return jax.shard_map(
        shards, mesh=finer, in_specs=placed, out_specs=(P(ALL), P(ALL, None)), check_vma=False
    )
```

```python
import jax
import jax.numpy as jnp
from jax import lax
from jax.experimental import pallas as pl
from jax.experimental.pallas import tpu as pltpu
from jax.sharding import Mesh
from jax.sharding import PartitionSpec as P

HEADS = 12
HEAD = 64
SEQ = 128
DP = ("zh", "x", "core")
FS = ("y", "zl")
ALL = DP + FS
LIST = 47
SLOTS = 39
BLOCK = SLOTS + 1
ROOM = 48
F32 = jnp.float32
BF16 = jnp.bfloat16


RING = ((0, 0, 2), (1, 0, 2), (2, 0, 1), (2, 1, 1), (3, 0, 2))


def iota(shape, dim):
    return lax.broadcasted_iota(jnp.int32, shape, dim)


def dot(a, b, dims=((1,), (0,))):
    return lax.dot_general(a, b, (dims, ((), ())), preferred_element_type=F32)


def ranked(present, groups):
    rows = present.shape[0]
    per = rows // groups
    upper = jnp.where(iota((128, 128), 0) < iota((128, 128), 1), 1.0, 0.0).astype(BF16)
    at, of = iota((rows, rows), 0), iota((rows, rows), 1)
    above = jnp.where((at // per == of // per) & (of < at), 1.0, 0.0).astype(BF16)
    ones = present.astype(BF16)
    return dot(ones, upper) + jnp.sum(dot(above, ones), axis=1, keepdims=True)


def tokens_of(ids_refs, dest):
    dests = ids_refs[0].shape[0] // 2
    return jnp.concatenate(
        [ref[pl.ds(z * dests + dest, 1), :] for ref in ids_refs for z in range(2)], axis=1
    )


def lists_kernel(info_ref, *refs):
    ids_refs, table_ref, rows_ref, present_ref, rank_ref, hits_ref = refs[0:4], *refs[4:]
    vocab = table_ref.shape[0]
    dests, tokens = rows_ref.shape[0], 8 * SEQ
    base = info_ref[0] * vocab
    first_slot = info_ref[1] * LIST
    high = 16

    def find(p, _):
        local = tokens_of(ids_refs, p) - base
        inside = (local >= 0) & (local < vocab)
        block = jnp.where((iota((high, tokens), 0) == (local >> 7)) & inside, 1.0, 0.0).astype(BF16)
        lane = jnp.where(iota((128, tokens), 0) == (local & 127), 1.0, 0.0).astype(BF16)
        seen = dot(block, lane, ((1,), (1,)))
        present_ref[pl.ds(pl.multiple_of(p * high, high), high), :] = jnp.where(seen > 0.5, 1.0, 0.0)
        return 0

    lax.fori_loop(0, dests, find, 0, unroll=2)
    present = present_ref[...]
    rank_ref[...] = jnp.where(present > 0.5, ranked(present, dests) - first_slot.astype(F32), -1.0)
    blocks = -(-vocab // 128)

    def choose(p, most):
        ranks = rank_ref[pl.ds(pl.multiple_of(p * high, high), high), :]
        slot = iota((ROOM, 128), 0)
        for h in range(blocks):
            chosen = (slot == ranks[h : h + 1, :].astype(jnp.int32)) & (slot < LIST)
            hits_ref[pl.ds(pl.multiple_of(p * ROOM, ROOM), ROOM), h * 128 : (h + 1) * 128] = jnp.where(
                chosen, 1.0, 0.0
            ).astype(BF16)
        return jnp.maximum(most, jnp.max(ranks))

    most = lax.fori_loop(0, dests, choose, jnp.float32(-1.0)) + first_slot.astype(F32)
    whole = vocab // 16 * 16
    rounds = jnp.floor(most * (1.0 / LIST) + 1e-3) + 1.0
    some = 4

    def fetch(i, _):
        hits = hits_ref[pl.ds(pl.multiple_of(i * some * ROOM, some * ROOM), some * ROOM), :]
        rows = dot(hits[:, 0:whole], table_ref[0:whole, :])
        if whole < vocab:
            tail = table_ref[whole:vocab, :].astype(F32)
            for k in range(vocab - whole):
                rows = rows + hits[:, whole + k : whole + k + 1].astype(F32) * tail[k : k + 1, :]
        rows = rows.reshape(some, ROOM, rows.shape[1])
        rows_ref[pl.ds(i * some, some)] = jnp.where(iota(rows.shape, 1) == LIST, rounds, rows).astype(BF16)
        return 0

    lax.fori_loop(0, dests // some, fetch, 0)


def listed_rows(info, ids, table):
    dests = ids[0].shape[0] // 2
    width = table.shape[1]
    return pl.pallas_call(
        lists_kernel,
        out_shape=jax.ShapeDtypeStruct((dests, ROOM, width), BF16),
        in_specs=[pl.BlockSpec(memory_space=pltpu.SMEM)]
        + [pl.BlockSpec(memory_space=pltpu.VMEM)] * (len(ids) + 1),
        out_specs=pl.BlockSpec(memory_space=pltpu.VMEM),
        scratch_shapes=[
            pltpu.VMEM((dests * 16, 128), F32),
            pltpu.VMEM((dests * 16, 128), F32),
            pltpu.VMEM((dests * ROOM, 16 * 128), BF16),
        ],
        compiler_params=pltpu.CompilerParams(vmem_limit_bytes=40 << 20),
    )(info, *ids, table)


def place_kernel(info_ref, *refs):
    ids_refs, out_ref = refs[0:4], refs[4]
    tokens = 8 * SEQ
    owners = out_ref.shape[1] // ROOM
    first_slot = info_ref[1] * LIST
    vocab = info_ref[2]
    row = tokens_of(ids_refs, info_ref[0])
    owner = jnp.zeros(row.shape, jnp.int32)
    for k in range(1, owners):
        owner = owner + jnp.where(row >= k * vocab, 1, 0)
    local = row - owner * vocab
    group = owner * 16 + (local >> 7)
    block = jnp.where(iota((owners * 16, tokens), 0) == group, 1.0, 0.0).astype(BF16)
    lane = jnp.where(iota((128, tokens), 0) == (local & 127), 1.0, 0.0).astype(BF16)
    present = jnp.where(dot(block, lane, ((1,), (1,))) > 0.5, 1.0, 0.0)
    rank = ranked(present, owners) - first_slot.astype(F32)
    rank = jnp.where((rank >= 0) & (rank < LIST), rank, 255.0).astype(BF16)
    owner = owner.astype(F32)
    low = (local & 127).astype(F32)
    for t in range(tokens // 128):
        cols = slice(t * 128, (t + 1) * 128)
        found = lax.dot_general(
            block[:, cols], rank, (((0,), (0,)), ((), ())), preferred_element_type=F32
        )
        down = jnp.broadcast_to(low[:, cols], (128, 128)).T
        slot = jnp.sum(jnp.where(iota((128, 128), 1).astype(F32) == down, found, 0.0), axis=1, keepdims=True)
        of = jnp.broadcast_to(owner[:, cols], (128, 128)).T[:, 0:1]
        place = jnp.where(slot < LIST, of * ROOM + slot, -1.0).astype(jnp.int32)
        out_ref[cols, :] = jnp.where(place == iota((128, owners * ROOM), 1), 1.0, 0.0).astype(BF16)


def placed_rows(info, ids, owners):
    return pl.pallas_call(
        place_kernel,
        out_shape=jax.ShapeDtypeStruct((8 * SEQ, owners * ROOM), BF16),
        in_specs=[pl.BlockSpec(memory_space=pltpu.SMEM)]
        + [pl.BlockSpec(memory_space=pltpu.VMEM)] * len(ids),
        out_specs=pl.BlockSpec(memory_space=pltpu.VMEM),
        compiler_params=pltpu.CompilerParams(vmem_limit_bytes=40 << 20),
    )(info, *ids)


def expand_kernel(places_ref, got_ref, out_ref, rounds_ref):
    owners, room, width = got_ref.shape
    got = got_ref[...].reshape(owners * room, width)

    def fill(i, _):
        rows = pl.ds(pl.multiple_of(i * 2 * SEQ, 2 * SEQ), 2 * SEQ)
        out_ref[rows, :] = dot(places_ref[rows, :], got).astype(BF16)
        return 0

    lax.fori_loop(0, out_ref.shape[0] // (2 * SEQ), fill, 0)
    most = jnp.max(got_ref[:, LIST, 0:128].astype(F32), axis=0, keepdims=True)
    rounds_ref[...] = jnp.broadcast_to(most, rounds_ref.shape).astype(jnp.int32)


def expanded(places, got):
    return pl.pallas_call(
        expand_kernel,
        out_shape=(
            jax.ShapeDtypeStruct((places.shape[0], got.shape[2]), BF16),
            jax.ShapeDtypeStruct((8, 128), jnp.int32),
        ),
        in_specs=[pl.BlockSpec(memory_space=pltpu.VMEM)] * 2,
        out_specs=(pl.BlockSpec(memory_space=pltpu.VMEM), pl.BlockSpec(memory_space=pltpu.VMEM)),
        compiler_params=pltpu.CompilerParams(vmem_limit_bytes=40 << 20),
    )(places, got)


def join_kernel(*refs):
    parts, out_ref, sems = refs[:-2], refs[-2], refs[-1]
    rows = parts[0].shape[0]
    put(parts, [out_ref.at[pl.ds(k * rows, rows), :] for k in range(len(parts))], sems)


def joined(parts):
    rows, cols = parts[0].shape
    return pl.pallas_call(
        join_kernel,
        out_shape=jax.ShapeDtypeStruct((len(parts) * rows, cols), parts[0].dtype),
        in_specs=[pl.BlockSpec(memory_space=pltpu.HBM)] * len(parts),
        out_specs=pl.BlockSpec(memory_space=pltpu.HBM),
        scratch_shapes=[pltpu.SemaphoreType.DMA((len(parts),))],
    )(*parts)


def put(sources, targets, sems):
    copies = [
        pltpu.make_async_copy(src, dst, sems.at[k])
        for k, (src, dst) in enumerate(zip(sources, targets, strict=True))
    ]
    for c in copies:
        c.start()
    for c in copies:
        c.wait()


def encode_kernel(info_ref, *refs):
    rings = refs[0:10]
    slab_ref, gain_ref, bias_ref, out_ref, w_ref, packed_ref, scores_ref, probs_ref, context_ref, sems = (
        refs[10:]
    )
    x_size = 4
    core, at_x = info_ref[0], info_ref[1]
    depth, part = w_ref.shape[1:]
    targets = []
    for core_at in (core, 1 - core):
        for back, first, count in RING:
            place = core_at * x_size + lax.rem(at_x - back + x_size, x_size)
            targets.append(w_ref.at[place, pl.ds(first * (depth // 2), count * (depth // 2)), :])
    put(rings, targets, sems)
    tokens, width = packed_ref.shape[0], slab_ref.shape[1]
    left = iota((SEQ, 2 * HEAD), 1) < HEAD
    zero = jnp.zeros((SEQ, 2 * HEAD), BF16)
    pairs = HEADS // 2
    passages = tokens // SEQ

    def stacked(values):
        return jnp.concatenate([jnp.where(left, values, zero), jnp.where(left, zero, values)], axis=0)

    def step(i, _):
        x = slab_ref[pl.ds(i * tokens, tokens), :]
        for j in range(6):
            packed_ref[:, j * part : (j + 1) * part] = dot(x, w_ref[j]).astype(BF16)
        for b in range(passages):
            rows = slice(b * SEQ, (b + 1) * SEQ)
            for pair in range(pairs):
                at = pair * 2 * HEAD
                q = packed_ref[rows, at : at + 2 * HEAD] * jnp.asarray(HEAD**-0.5, BF16)
                k = packed_ref[rows, width + at : width + at + 2 * HEAD]
                scores_ref[b * pairs + pair] = dot(q, stacked(k), ((1,), (1,)))
        for n in range(passages * pairs):
            for h in range(2):
                s = scores_ref[n, :, h * SEQ : (h + 1) * SEQ]
                e = jnp.exp(s - jnp.max(s, axis=1, keepdims=True))
                probs = e * (1.0 / jnp.sum(e, axis=1, keepdims=True))
                probs_ref[n, :, h * SEQ : (h + 1) * SEQ] = probs.astype(BF16)
        for b in range(passages):
            rows = slice(b * SEQ, (b + 1) * SEQ)
            for pair in range(pairs):
                at = pair * 2 * HEAD
                v = packed_ref[rows, 2 * width + at : 2 * width + at + 2 * HEAD]
                context_ref[rows, at : at + 2 * HEAD] = dot(
                    probs_ref[b * pairs + pair], stacked(v)
                ).astype(BF16)
        context = context_ref[...]
        half = width // 2
        mixed = [
            dot(context, w_ref[6 + k]) + x[:, k * half : (k + 1) * half].astype(F32) for k in range(2)
        ]
        mean = sum(jnp.sum(m, axis=1, keepdims=True) for m in mixed) * (1.0 / width)
        center = [m - mean for m in mixed]
        spread = sum(jnp.sum(c * c, axis=1, keepdims=True) for c in center) * (1.0 / width)
        scale = lax.rsqrt(spread + 1e-05)
        for k in range(2):
            cols = slice(k * half, (k + 1) * half)
            out_ref[pl.ds(i * tokens, tokens), cols] = (
                center[k] * scale * gain_ref[:, cols] + bias_ref[:, cols]
            ).astype(BF16)
        return 0

    lax.fori_loop(0, slab_ref.shape[0] // tokens, step, 0)


def encoded(info, rings, slab, gain, bias):
    part = rings[0].shape[1]
    tokens, width = 2 * SEQ, slab.shape[1]
    pairs = tokens // SEQ * HEADS // 2
    return pl.pallas_call(
        encode_kernel,
        out_shape=jax.ShapeDtypeStruct(slab.shape, BF16),
        in_specs=[pl.BlockSpec(memory_space=pltpu.SMEM)]
        + [pl.BlockSpec(memory_space=pltpu.HBM)] * len(rings)
        + [pl.BlockSpec(memory_space=pltpu.VMEM)] * 3,
        out_specs=pl.BlockSpec(memory_space=pltpu.VMEM),
        scratch_shapes=[
            pltpu.VMEM((8, width, part), BF16),
            pltpu.VMEM((tokens, 3 * width), BF16),
            pltpu.VMEM((pairs, SEQ, 2 * SEQ), F32),
            pltpu.VMEM((pairs, SEQ, 2 * SEQ), BF16),
            pltpu.VMEM((tokens, width), BF16),
            pltpu.SemaphoreType.DMA((len(rings),)),
        ],
        compiler_params=pltpu.CompilerParams(vmem_limit_bytes=40 << 20),
    )(info, *rings, slab, gain.reshape(1, width), bias.reshape(1, width))


def score_kernel(info_ref, mine_ref, other_ref, local_ref, *refs):
    parts = refs[0:5]
    out_ref, old_ref, cent_ref, sems = refs[5:]
    step = pl.program_id(0)
    half = pl.num_programs(0) // 2

    @pl.when(step == 0)
    def _():
        shard = parts[0].shape[0] // 4
        sources, targets = [], []
        for ref, (back, first, count) in zip(parts, RING, strict=True):
            owner = lax.rem(info_ref[0] - back + 4, 4) * 4
            for k in range(2 * count):
                start = (owner + lax.rem(info_ref[6] - 2 * first - k + 4, 4)) * shard
                sources.append(ref.at[pl.ds(k * shard, shard), :])
                targets.append(cent_ref.at[pl.ds(pl.multiple_of(start, shard), shard), :])
        put(sources, targets, sems)

    block = cent_ref.shape[1]
    span = 2 * SEQ
    for n in range(mine_ref.shape[0] // span):
        rows = slice(n * span, (n + 1) * span)
        s = dot(jnp.where(step < half, mine_ref[rows, :], other_ref[rows, :]), cent_ref[...])
        peak = jnp.max(s, axis=1, keepdims=True)
        mass = jnp.sum(jnp.exp(s - peak), axis=1, keepdims=True)
        local = jnp.concatenate(
            [jnp.broadcast_to(local_ref[2 * n + z], (SEQ, SEQ)).T[:, 0:1] for z in range(2)], axis=0
        )
        picked = jnp.sum(jnp.where(local == iota((span, block), 1), s, 0.0), axis=1, keepdims=True)
        both = jnp.where(iota((span, 128), 1) == 0, peak + jnp.log(mass), picked)
        x_size = info_ref[5]
        per_step = mine_ref.shape[0] // span
        back = lax.rem(step, half) * per_step + n
        x = lax.rem(info_ref[3] - back + x_size, x_size)
        core = jnp.where(step < half, info_ref[2], 1 - info_ref[2])
        for z in range(2):
            zh = info_ref[4] if z == 0 else 1 - info_ref[4]
            out_ref[zh * (2 * x_size) + x * 2 + core] = both[z * SEQ : (z + 1) * SEQ, :].T[0:8, :]

    @pl.when(step == pl.num_programs(0) - 1)
    def _():
        per = old_ref.shape[0]
        old = cent_ref[:, pl.ds(pl.multiple_of(info_ref[1] * per, per), per)]
        old_ref[...] = old.astype(F32).T


def scored(info, mine, other, local, parts):
    tokens, width = mine.shape
    block = parts[0].shape[1]
    step = 4 * SEQ
    per = step // SEQ
    half = tokens // step
    return pl.pallas_call(
        score_kernel,
        grid=(2 * half,),
        out_shape=(
            jax.ShapeDtypeStruct((2 * tokens // SEQ, 8, SEQ), F32),
            jax.ShapeDtypeStruct((SEQ, width), F32),
        ),
        in_specs=[
            pl.BlockSpec(memory_space=pltpu.SMEM),
            pl.BlockSpec((step, width), lambda i: (jnp.minimum(i, half - 1), 0)),
            pl.BlockSpec((step, width), lambda i: (jnp.maximum(i - half, 0), 0)),
            pl.BlockSpec((per, 1, SEQ), lambda i: (i, 0, 0)),
        ]
        + [pl.BlockSpec(memory_space=pltpu.HBM)] * len(parts),
        out_specs=(
            pl.BlockSpec((2 * tokens // SEQ, 8, SEQ), lambda i: (0, 0, 0)),
            pl.BlockSpec((SEQ, width), lambda i: (0, 0)),
        ),
        scratch_shapes=[
            pltpu.VMEM((width, block), BF16),
            pltpu.SemaphoreType.DMA((16,)),
        ],
        compiler_params=pltpu.CompilerParams(vmem_limit_bytes=48 << 20),
    )(info, mine, other, local.reshape(2 * tokens // SEQ, 1, SEQ), *parts)


def choose_kernel(info_ref, local_ref, out_ref, most_ref):
    tokens = local_ref.shape[1]
    per = 128
    dests = out_ref.shape[0] // ROOM
    first_slot = info_ref[1] * SLOTS
    local = local_ref[...]
    upper = iota((per, per), 0) < iota((per, per), 1)
    diagonal = iota((per, per), 0) == iota((per, per), 1)

    def group(g, most):
        match = jnp.where(local - g * per == iota((per, tokens), 0), 1.0, 0.0)
        hits = match.astype(BF16)
        present = jnp.broadcast_to(jnp.max(match, axis=1, keepdims=True), (per, per))
        rank = jnp.sum(jnp.where(upper, present, 0.0), axis=0, keepdims=True).astype(jnp.int32)
        here = jnp.sum(jnp.where(diagonal, present, 0.0), axis=0, keepdims=True)
        slot = iota((ROOM, per), 0)
        chosen = (slot < SLOTS) & (slot == rank - first_slot) & (here > 0.5)
        packing = jnp.where(chosen, 1.0, 0.0).astype(BF16)
        out_ref[pl.ds(pl.multiple_of(g * ROOM, ROOM), ROOM), :] = dot(packing, hits).astype(BF16)
        return jnp.maximum(most, jnp.sum(here, axis=1, keepdims=True))

    most = lax.fori_loop(0, dests, group, jnp.zeros((1, 1), F32), unroll=2)
    most_ref[...] = jnp.broadcast_to(most, most_ref.shape)


def choices(info, local, dests):
    return pl.pallas_call(
        choose_kernel,
        out_shape=(
            jax.ShapeDtypeStruct((dests * ROOM, local.shape[1]), BF16),
            jax.ShapeDtypeStruct((8, 128), F32),
        ),
        in_specs=[pl.BlockSpec(memory_space=pltpu.SMEM), pl.BlockSpec(memory_space=pltpu.VMEM)],
        out_specs=(pl.BlockSpec(memory_space=pltpu.VMEM), pl.BlockSpec(memory_space=pltpu.VMEM)),
        compiler_params=pltpu.CompilerParams(vmem_limit_bytes=40 << 20),
    )(info, local)


def pack_kernel(hits_ref, most_ref, mine_ref, other_ref, out_ref):
    dests, _, width = out_ref.shape
    half = mine_ref.shape[0]
    some = dests // 2

    def pack(i, _):
        hits = hits_ref[pl.ds(pl.multiple_of(i * some * ROOM, some * ROOM), some * ROOM), :]
        sums = dot(hits[:, 0:half], mine_ref[...]) + dot(hits[:, half:], other_ref[...])
        sums = sums.reshape(some, ROOM, width)[:, 0:BLOCK, :]
        last = iota(sums.shape, 1) == SLOTS
        out_ref[pl.ds(i * some, some)] = jnp.where(
            last, most_ref[0:1, 0:1].reshape(1, 1, 1), sums
        ).astype(BF16)
        return 0

    lax.fori_loop(0, 2, pack, 0)


def packed_sums(chosen, mine, other):
    hits, most = chosen
    width = mine.shape[1]
    return pl.pallas_call(
        pack_kernel,
        out_shape=jax.ShapeDtypeStruct((hits.shape[0] // ROOM, BLOCK, width), BF16),
        in_specs=[pl.BlockSpec(memory_space=pltpu.VMEM)] * 4,
        out_specs=pl.BlockSpec(memory_space=pltpu.VMEM),
        compiler_params=pltpu.CompilerParams(vmem_limit_bytes=40 << 20),
    )(hits, most, mine, other)


def count_kernel(info_ref, assign_ref, out_ref):
    dp, slabs, _ = assign_ref.shape
    targets = iota((128, SEQ), 0) + info_ref[0]
    lane = iota(out_ref.shape, 1)

    def slab(f, out):
        acc = jnp.zeros((128, SEQ), F32)
        for d in range(dp):
            acc = acc + jnp.where(assign_ref[d, pl.ds(f, 1), :] == targets, 1.0, 0.0)
        return jnp.where(lane == f, jnp.sum(acc, axis=1, keepdims=True), out)

    out_ref[...] = lax.fori_loop(0, slabs, slab, jnp.zeros(out_ref.shape, F32))


def counted(info, assign):
    return pl.pallas_call(
        count_kernel,
        out_shape=jax.ShapeDtypeStruct((128, 128), F32),
        in_specs=[pl.BlockSpec(memory_space=pltpu.SMEM), pl.BlockSpec(memory_space=pltpu.VMEM)],
        out_specs=pl.BlockSpec(memory_space=pltpu.VMEM),
    )(info, assign)


def unpack_kernel(info_ref, counts_ref, got_ref, out_ref, most_ref):
    slabs, _, width = got_ref.shape
    counts = counts_ref[...]
    present = jnp.where(counts > 0.5, 1.0, 0.0).astype(BF16)
    lower = jnp.where(iota((128, 128), 1) < iota((128, 128), 0), 1.0, 0.0).astype(BF16)
    rank = dot(lower, present).astype(jnp.int32) - info_ref[1] * SLOTS
    slot = iota((128, BLOCK), 1)
    parts = []
    for f in range(slabs):
        chosen = (slot == rank[:, f : f + 1]) & (slot < SLOTS) & (counts[:, f : f + 1] > 0.5)
        parts.append(jnp.where(chosen, 1.0, 0.0))
    hits = jnp.concatenate(parts, axis=1).astype(BF16)
    out_ref[...] = dot(hits, got_ref[...].reshape(slabs * BLOCK, width))
    most = jnp.max(got_ref[:, SLOTS, 0:128].astype(F32), axis=0, keepdims=True)
    most_ref[...] = jnp.broadcast_to(most, most_ref.shape).astype(jnp.int32)


def unpacked_sums(info, counts, got):
    return pl.pallas_call(
        unpack_kernel,
        out_shape=(
            jax.ShapeDtypeStruct((128, got.shape[2]), F32),
            jax.ShapeDtypeStruct((8, 128), jnp.int32),
        ),
        in_specs=[pl.BlockSpec(memory_space=pltpu.SMEM)]
        + [pl.BlockSpec(memory_space=pltpu.VMEM)] * 2,
        out_specs=(pl.BlockSpec(memory_space=pltpu.VMEM), pl.BlockSpec(memory_space=pltpu.VMEM)),
    )(info, counts, got)


def exchanged(blocks, axis):
    return lax.all_to_all(blocks, axis, 0, 0, tiled=True)


def gathered(shard, axis):
    devices = lax.axis_size(axis)
    return exchanged(jnp.broadcast_to(shard[None], (devices,) + shard.shape), axis)


def swapped(shard, axis):
    return lax.ppermute(shard, axis, [(0, 1), (1, 0)])


def turned(shard, axis, by):
    devices = lax.axis_size(axis)
    return lax.ppermute(shard, axis, [(i, (i + by) % devices) for i in range(devices)])


def neighbours(block, axis):
    return turned(block, axis, 1), turned(block, axis, lax.axis_size(axis) - 1)


def far_halves(back, ahead, axis):
    half = back.shape[0] // 2
    return turned(back[:half], axis, 1), turned(ahead[half:], axis, lax.axis_size(axis) - 1)


def backwards(values, here):
    for dim, at in enumerate(here):
        size = values.shape[dim]
        values = jnp.take(values, (at - jnp.arange(size)) % size, axis=dim)
    return values


def shards(token_ids, embed_table, w_qkv, w_out, ln_gain, ln_bias, centroids_t, assignments):
    core = lax.axis_index("core")
    dp_rank = lax.axis_index(DP)
    fs_rank = lax.axis_index(FS)
    fs_size = lax.axis_size(FS)
    dp_size = lax.axis_size(DP)
    x_size = lax.axis_size("x")
    vocab, width = embed_table.shape
    zero = jnp.int32(0)
    ids = token_ids.reshape(fs_size, SEQ)

    at_x = lax.axis_index("x")

    def info_of(*values):
        return jnp.stack([jnp.asarray(v, jnp.int32) for v in values])

    by_dev = assignments.reshape(2, x_size, 2, fs_size, SEQ)
    of_slab = lax.dynamic_index_in_dim(by_dev, fs_rank, 3, keepdims=False)
    of_slab = jnp.transpose(of_slab, (2, 1, 0, 3))
    here = (core, at_x, lax.axis_index("zh"))
    of_slab = backwards(of_slab, here)
    block = centroids_t.shape[1]
    local = of_slab.reshape(1, -1) - dp_rank * block
    chosen = choices(info_of(zero, zero), local, fs_size)
    counts = counted(
        info_of(dp_rank * block + fs_rank * (block // fs_size)),
        assignments.reshape(dp_size, fs_size, SEQ),
    )

    part = (w_qkv.shape[1] + w_out.shape[1]) // (2 * x_size)
    both = jnp.concatenate([w_qkv, w_out], axis=1)
    piece = lax.dynamic_slice_in_dim(both, (core * x_size + at_x) * part, part, 1)
    column = gathered(piece, FS).reshape(width, part)

    two = jnp.concatenate([ids, swapped(ids, "zh")], axis=0)
    ids = [two] + [turned(two, "x", k) for k in range(1, x_size)]

    sent = listed_rows(info_of(fs_rank, zero), ids, embed_table)
    sent, column, local, shard = lax.optimization_barrier((sent, column, local, centroids_t))
    w_back, w_ahead = neighbours(column, "x")
    near = joined([shard] + [turned(shard, "zl", k) for k in range(1, 4)])
    places = placed_rows(info_of(fs_rank, zero, vocab), ids, fs_size)
    w_back, w_ahead, chosen, places = lax.optimization_barrier((w_back, w_ahead, chosen, places))
    rings = [column, w_back, *far_halves(w_back, w_ahead, "x"), w_ahead]
    rings += [swapped(w, "core") for w in rings]
    got = exchanged(sent, FS)
    got, near, *rings = lax.optimization_barrier((got, near, *rings))
    slab, rounds = expanded(places, got)

    def more_rows(state):
        turn, acc = state
        again = exchanged(listed_rows(info_of(fs_rank, turn), ids, embed_table), FS)
        extra, _ = expanded(placed_rows(info_of(fs_rank, turn, vocab), ids, fs_size), again)
        return turn + 1, acc + extra

    rounds = rounds[0, 0]
    _, slab = lax.while_loop(lambda state: state[0] < rounds, more_rows, (jnp.int32(1), slab))

    back, ahead = neighbours(near, "y")

    mine = encoded(info_of(core, at_x), rings, slab, ln_gain, ln_bias)
    mine, back, ahead = lax.optimization_barrier((mine, back, ahead))
    far_low, far_high = far_halves(back, ahead, "y")
    other = swapped(mine, "core")

    def one_turn(turn):
        info = info_of(zero, turn)
        got = exchanged(packed_sums(choices(info, local, fs_size), mine, other), FS)
        return unpacked_sums(info, counts, got)[0]

    packed = packed_sums(chosen, mine, other)
    packed, mine, other, far_low, far_high = lax.optimization_barrier(
        (packed, mine, other, far_low, far_high)
    )
    got = exchanged(packed, FS)

    stats, previous = scored(
        info_of(lax.axis_index("y"), fs_rank, *here, x_size, lax.axis_index("zl")),
        mine,
        other,
        local,
        [near, back, far_low, far_high, ahead],
    )
    stats, got = lax.optimization_barrier((stats, got))
    sums, widest = unpacked_sums(info_of(zero, zero), counts, got)
    widest = widest[0, 0]
    _, sums = lax.while_loop(
        lambda state: state[0] * SLOTS < widest,
        lambda state: (state[0] + 1, state[1] + one_turn(state[0])),
        (jnp.int32(1), sums),
    )

    home = exchanged(stats, DP)
    lse = home[:, 0, :]
    peak = jnp.max(lse, axis=0)
    token_loss = (
        jnp.log(jnp.sum(jnp.exp(lse - peak[None, :]), axis=0)) + peak - jnp.sum(home[:, 1, :], axis=0)
    )

    total = jnp.sum(counts[:, 0:fs_size], axis=1, keepdims=True)
    new_centroids = jnp.where(total > 0, sums / jnp.maximum(total, 1.0), previous)
    return token_loss, new_centroids


def solution(mesh):
    finer = Mesh(mesh.devices.reshape(2, 4, 2, 4, 4), ALL)
    placed = (P(DP), P(FS, None), P(FS, None), P(FS, None), P(), P(), P(FS, DP), P())
    return jax.shard_map(
        shards, mesh=finer, in_specs=placed, out_specs=(P(ALL), P(ALL, None)), check_vma=False
    )
```

```python
import jax
import jax.numpy as jnp
from jax import lax
from jax.experimental import pallas as pl
from jax.experimental.pallas import tpu as pltpu
from jax.sharding import Mesh
from jax.sharding import PartitionSpec as P

HEADS = 12
HEAD = 64
SEQ = 128
DP = ("zh", "x", "core")
FS = ("y", "zl")
ALL = DP + FS
LIST = 47
SLOTS = 39
BLOCK = SLOTS + 1
ROOM = 48
F32 = jnp.float32
BF16 = jnp.bfloat16


RING = ((0, 0, 2), (1, 0, 2), (2, 0, 1), (2, 1, 1), (3, 0, 2))


def iota(shape, dim):
    return lax.broadcasted_iota(jnp.int32, shape, dim)


def dot(a, b, dims=((1,), (0,))):
    return lax.dot_general(a, b, (dims, ((), ())), preferred_element_type=F32)


def ranked(present, groups):
    rows = present.shape[0]
    per = rows // groups
    upper = jnp.where(iota((128, 128), 0) < iota((128, 128), 1), 1.0, 0.0).astype(BF16)
    at, of = iota((rows, rows), 0), iota((rows, rows), 1)
    above = jnp.where((at // per == of // per) & (of < at), 1.0, 0.0).astype(BF16)
    ones = present.astype(BF16)
    return dot(ones, upper) + jnp.sum(dot(above, ones), axis=1, keepdims=True)


def tokens_of(ids_refs, dest):
    dests = ids_refs[0].shape[0] // 2
    return jnp.concatenate(
        [ref[pl.ds(z * dests + dest, 1), :] for ref in ids_refs for z in range(2)], axis=1
    )


def lists_kernel(info_ref, *refs):
    ids_refs, table_ref, rows_ref, present_ref, rank_ref, hits_ref = refs[0:4], *refs[4:]
    vocab = table_ref.shape[0]
    dests, tokens = rows_ref.shape[0], 8 * SEQ
    base = info_ref[0] * vocab
    first_slot = info_ref[1] * LIST
    high = 16

    def find(p, _):
        local = tokens_of(ids_refs, p) - base
        inside = (local >= 0) & (local < vocab)
        block = jnp.where((iota((high, tokens), 0) == (local >> 7)) & inside, 1.0, 0.0).astype(BF16)
        lane = jnp.where(iota((128, tokens), 0) == (local & 127), 1.0, 0.0).astype(BF16)
        seen = dot(block, lane, ((1,), (1,)))
        present_ref[pl.ds(pl.multiple_of(p * high, high), high), :] = jnp.where(seen > 0.5, 1.0, 0.0)
        return 0

    lax.fori_loop(0, dests, find, 0, unroll=4)
    present = present_ref[...]
    rank_ref[...] = jnp.where(present > 0.5, ranked(present, dests) - first_slot.astype(F32), -1.0)
    blocks = -(-vocab // 128)

    def choose(p, most):
        ranks = rank_ref[pl.ds(pl.multiple_of(p * high, high), high), :]
        slot = iota((ROOM, 128), 0)
        for h in range(blocks):
            chosen = (slot == ranks[h : h + 1, :].astype(jnp.int32)) & (slot < LIST)
            hits_ref[pl.ds(pl.multiple_of(p * ROOM, ROOM), ROOM), h * 128 : (h + 1) * 128] = jnp.where(
                chosen, 1.0, 0.0
            ).astype(BF16)
        return jnp.maximum(most, jnp.max(ranks))

    most = lax.fori_loop(0, dests, choose, jnp.float32(-1.0), unroll=2) + first_slot.astype(F32)
    whole = vocab // 16 * 16
    rounds = jnp.floor(most * (1.0 / LIST) + 1e-3) + 1.0
    some = 4

    def fetch(i, _):
        hits = hits_ref[pl.ds(pl.multiple_of(i * some * ROOM, some * ROOM), some * ROOM), :]
        rows = dot(hits[:, 0:whole], table_ref[0:whole, :])
        if whole < vocab:
            tail = table_ref[whole:vocab, :].astype(F32)
            for k in range(vocab - whole):
                rows = rows + hits[:, whole + k : whole + k + 1].astype(F32) * tail[k : k + 1, :]
        rows = rows.reshape(some, ROOM, rows.shape[1])
        rows_ref[pl.ds(i * some, some)] = jnp.where(iota(rows.shape, 1) == LIST, rounds, rows).astype(BF16)
        return 0

    lax.fori_loop(0, dests // some, fetch, 0)


def listed_rows(info, ids, table):
    dests = ids[0].shape[0] // 2
    width = table.shape[1]
    return pl.pallas_call(
        lists_kernel,
        out_shape=jax.ShapeDtypeStruct((dests, ROOM, width), BF16),
        in_specs=[pl.BlockSpec(memory_space=pltpu.SMEM)]
        + [pl.BlockSpec(memory_space=pltpu.VMEM)] * (len(ids) + 1),
        out_specs=pl.BlockSpec(memory_space=pltpu.VMEM),
        scratch_shapes=[
            pltpu.VMEM((dests * 16, 128), F32),
            pltpu.VMEM((dests * 16, 128), F32),
            pltpu.VMEM((dests * ROOM, 16 * 128), BF16),
        ],
        compiler_params=pltpu.CompilerParams(vmem_limit_bytes=40 << 20),
    )(info, *ids, table)


def place_kernel(info_ref, *refs):
    ids_refs, out_ref = refs[0:4], refs[4]
    tokens = 8 * SEQ
    owners = out_ref.shape[1] // ROOM
    first_slot = info_ref[1] * LIST
    vocab = info_ref[2]
    row = tokens_of(ids_refs, info_ref[0])
    owner = jnp.zeros(row.shape, jnp.int32)
    for k in range(1, owners):
        owner = owner + jnp.where(row >= k * vocab, 1, 0)
    local = row - owner * vocab
    group = owner * 16 + (local >> 7)
    block = jnp.where(iota((owners * 16, tokens), 0) == group, 1.0, 0.0).astype(BF16)
    lane = jnp.where(iota((128, tokens), 0) == (local & 127), 1.0, 0.0).astype(BF16)
    present = jnp.where(dot(block, lane, ((1,), (1,))) > 0.5, 1.0, 0.0)
    rank = ranked(present, owners) - first_slot.astype(F32)
    rank = jnp.where((rank >= 0) & (rank < LIST), rank, 255.0).astype(BF16)
    owner = owner.astype(F32)
    low = (local & 127).astype(F32)
    for t in range(tokens // 128):
        cols = slice(t * 128, (t + 1) * 128)
        found = lax.dot_general(
            block[:, cols], rank, (((0,), (0,)), ((), ())), preferred_element_type=F32
        )
        down = jnp.broadcast_to(low[:, cols], (128, 128)).T
        slot = jnp.sum(jnp.where(iota((128, 128), 1).astype(F32) == down, found, 0.0), axis=1, keepdims=True)
        of = jnp.broadcast_to(owner[:, cols], (128, 128)).T[:, 0:1]
        place = jnp.where(slot < LIST, of * ROOM + slot, -1.0).astype(jnp.int32)
        out_ref[cols, :] = jnp.where(place == iota((128, owners * ROOM), 1), 1.0, 0.0).astype(BF16)


def placed_rows(info, ids, owners):
    return pl.pallas_call(
        place_kernel,
        out_shape=jax.ShapeDtypeStruct((8 * SEQ, owners * ROOM), BF16),
        in_specs=[pl.BlockSpec(memory_space=pltpu.SMEM)]
        + [pl.BlockSpec(memory_space=pltpu.VMEM)] * len(ids),
        out_specs=pl.BlockSpec(memory_space=pltpu.VMEM),
        compiler_params=pltpu.CompilerParams(vmem_limit_bytes=40 << 20),
    )(info, *ids)


def expand_kernel(places_ref, got_ref, out_ref, rounds_ref):
    owners, room, width = got_ref.shape
    got = got_ref[...].reshape(owners * room, width)

    def fill(i, _):
        rows = pl.ds(pl.multiple_of(i * 2 * SEQ, 2 * SEQ), 2 * SEQ)
        out_ref[rows, :] = dot(places_ref[rows, :], got).astype(BF16)
        return 0

    lax.fori_loop(0, out_ref.shape[0] // (2 * SEQ), fill, 0)
    most = jnp.max(got_ref[:, LIST, 0:128].astype(F32), axis=0, keepdims=True)
    rounds_ref[...] = jnp.broadcast_to(most, rounds_ref.shape).astype(jnp.int32)


def expanded(places, got):
    return pl.pallas_call(
        expand_kernel,
        out_shape=(
            jax.ShapeDtypeStruct((places.shape[0], got.shape[2]), BF16),
            jax.ShapeDtypeStruct((8, 128), jnp.int32),
        ),
        in_specs=[pl.BlockSpec(memory_space=pltpu.VMEM)] * 2,
        out_specs=(pl.BlockSpec(memory_space=pltpu.VMEM), pl.BlockSpec(memory_space=pltpu.VMEM)),
        compiler_params=pltpu.CompilerParams(vmem_limit_bytes=40 << 20),
    )(places, got)


def join_kernel(*refs):
    parts, out_ref = refs[:-1], refs[-1]
    rows = parts[0].shape[0]
    for k, ref in enumerate(parts):
        out_ref[k * rows : (k + 1) * rows, :] = ref[...]


def joined(parts):
    rows, cols = parts[0].shape
    return pl.pallas_call(
        join_kernel,
        out_shape=jax.ShapeDtypeStruct((len(parts) * rows, cols), parts[0].dtype),
        in_specs=[pl.BlockSpec(memory_space=pltpu.VMEM)] * len(parts),
        out_specs=pl.BlockSpec(memory_space=pltpu.VMEM),
    )(*parts)


def put(sources, targets, sems):
    copies = [
        pltpu.make_async_copy(src, dst, sems.at[k])
        for k, (src, dst) in enumerate(zip(sources, targets, strict=True))
    ]
    for c in copies:
        c.start()
    for c in copies:
        c.wait()


def encode_kernel(info_ref, *refs):
    rings = refs[0:10]
    slab_ref, gain_ref, bias_ref, out_ref, w_ref, packed_ref, scores_ref, probs_ref, context_ref, sems = (
        refs[10:]
    )
    x_size = 4
    core, at_x = info_ref[0], info_ref[1]
    depth, part = w_ref.shape[1:]
    targets = []
    for core_at in (core, 1 - core):
        for back, first, count in RING:
            place = core_at * x_size + lax.rem(at_x - back + x_size, x_size)
            targets.append(w_ref.at[place, pl.ds(first * (depth // 2), count * (depth // 2)), :])
    put(rings, targets, sems)
    tokens, width = packed_ref.shape[0], slab_ref.shape[1]
    left = iota((SEQ, 2 * HEAD), 1) < HEAD
    zero = jnp.zeros((SEQ, 2 * HEAD), BF16)
    pairs = HEADS // 2
    passages = tokens // SEQ

    def stacked(values):
        return jnp.concatenate([jnp.where(left, values, zero), jnp.where(left, zero, values)], axis=0)

    def step(i, _):
        x = slab_ref[pl.ds(i * tokens, tokens), :]
        for j in range(6):
            packed_ref[:, j * part : (j + 1) * part] = dot(x, w_ref[j]).astype(BF16)
        for b in range(passages):
            rows = slice(b * SEQ, (b + 1) * SEQ)
            for pair in range(pairs):
                at = pair * 2 * HEAD
                q = packed_ref[rows, at : at + 2 * HEAD] * jnp.asarray(HEAD**-0.5, BF16)
                k = packed_ref[rows, width + at : width + at + 2 * HEAD]
                scores_ref[b * pairs + pair] = dot(q, stacked(k), ((1,), (1,)))
        for n in range(passages * pairs):
            for h in range(2):
                s = scores_ref[n, :, h * SEQ : (h + 1) * SEQ]
                e = jnp.exp(s - jnp.max(s, axis=1, keepdims=True))
                probs = e * (1.0 / jnp.sum(e, axis=1, keepdims=True))
                probs_ref[n, :, h * SEQ : (h + 1) * SEQ] = probs.astype(BF16)
        for b in range(passages):
            rows = slice(b * SEQ, (b + 1) * SEQ)
            for pair in range(pairs):
                at = pair * 2 * HEAD
                v = packed_ref[rows, 2 * width + at : 2 * width + at + 2 * HEAD]
                context_ref[rows, at : at + 2 * HEAD] = dot(
                    probs_ref[b * pairs + pair], stacked(v)
                ).astype(BF16)
        context = context_ref[...]
        half = width // 2
        mixed = [
            dot(context, w_ref[6 + k]) + x[:, k * half : (k + 1) * half].astype(F32) for k in range(2)
        ]
        mean = sum(jnp.sum(m, axis=1, keepdims=True) for m in mixed) * (1.0 / width)
        center = [m - mean for m in mixed]
        spread = sum(jnp.sum(c * c, axis=1, keepdims=True) for c in center) * (1.0 / width)
        scale = lax.rsqrt(spread + 1e-05)
        for k in range(2):
            cols = slice(k * half, (k + 1) * half)
            out_ref[pl.ds(i * tokens, tokens), cols] = (
                center[k] * scale * gain_ref[:, cols] + bias_ref[:, cols]
            ).astype(BF16)
        return 0

    lax.fori_loop(0, slab_ref.shape[0] // tokens, step, 0)


def encoded(info, rings, slab, gain, bias):
    part = rings[0].shape[1]
    tokens, width = 2 * SEQ, slab.shape[1]
    pairs = tokens // SEQ * HEADS // 2
    return pl.pallas_call(
        encode_kernel,
        out_shape=jax.ShapeDtypeStruct(slab.shape, BF16),
        in_specs=[pl.BlockSpec(memory_space=pltpu.SMEM)]
        + [pl.BlockSpec(memory_space=pltpu.HBM)] * len(rings)
        + [pl.BlockSpec(memory_space=pltpu.VMEM)] * 3,
        out_specs=pl.BlockSpec(memory_space=pltpu.VMEM),
        scratch_shapes=[
            pltpu.VMEM((8, width, part), BF16),
            pltpu.VMEM((tokens, 3 * width), BF16),
            pltpu.VMEM((pairs, SEQ, 2 * SEQ), F32),
            pltpu.VMEM((pairs, SEQ, 2 * SEQ), BF16),
            pltpu.VMEM((tokens, width), BF16),
            pltpu.SemaphoreType.DMA((len(rings),)),
        ],
        compiler_params=pltpu.CompilerParams(vmem_limit_bytes=40 << 20),
    )(info, *rings, slab, gain.reshape(1, width), bias.reshape(1, width))


def score_kernel(info_ref, mine_ref, other_ref, local_ref, *refs):
    parts = refs[0:5]
    out_ref, old_ref, cent_ref, sems = refs[5:]
    step = pl.program_id(0)
    half = pl.num_programs(0) // 2

    @pl.when(step == 0)
    def _():
        shard = parts[0].shape[0] // 4
        sources, targets = [], []
        for ref, (back, first, count) in zip(parts, RING, strict=True):
            owner = lax.rem(info_ref[0] - back + 4, 4) * 4
            for k in range(2 * count):
                start = (owner + lax.rem(info_ref[6] - 2 * first - k + 4, 4)) * shard
                sources.append(ref.at[pl.ds(k * shard, shard), :])
                targets.append(cent_ref.at[pl.ds(pl.multiple_of(start, shard), shard), :])
        put(sources, targets, sems)

    block = cent_ref.shape[1]
    span = 2 * SEQ
    for n in range(mine_ref.shape[0] // span):
        rows = slice(n * span, (n + 1) * span)
        s = dot(jnp.where(step < half, mine_ref[rows, :], other_ref[rows, :]), cent_ref[...])
        peak = jnp.max(s, axis=1, keepdims=True)
        mass = jnp.sum(jnp.exp(s - peak), axis=1, keepdims=True)
        local = jnp.concatenate(
            [jnp.broadcast_to(local_ref[2 * n + z], (SEQ, SEQ)).T[:, 0:1] for z in range(2)], axis=0
        )
        picked = jnp.sum(jnp.where(local == iota((span, block), 1), s, 0.0), axis=1, keepdims=True)
        both = jnp.where(iota((span, 128), 1) == 0, peak + jnp.log(mass), picked)
        x_size = info_ref[5]
        per_step = mine_ref.shape[0] // span
        back = lax.rem(step, half) * per_step + n
        x = lax.rem(info_ref[3] - back + x_size, x_size)
        core = jnp.where(step < half, info_ref[2], 1 - info_ref[2])
        for z in range(2):
            zh = info_ref[4] if z == 0 else 1 - info_ref[4]
            out_ref[zh * (2 * x_size) + x * 2 + core] = both[z * SEQ : (z + 1) * SEQ, :].T[0:8, :]

    @pl.when(step == pl.num_programs(0) - 1)
    def _():
        per = old_ref.shape[0]
        old = cent_ref[:, pl.ds(pl.multiple_of(info_ref[1] * per, per), per)]
        old_ref[...] = old.astype(F32).T


def scored(info, mine, other, local, parts):
    tokens, width = mine.shape
    block = parts[0].shape[1]
    step = 4 * SEQ
    per = step // SEQ
    half = tokens // step
    return pl.pallas_call(
        score_kernel,
        grid=(2 * half,),
        out_shape=(
            jax.ShapeDtypeStruct((2 * tokens // SEQ, 8, SEQ), F32),
            jax.ShapeDtypeStruct((SEQ, width), F32),
        ),
        in_specs=[
            pl.BlockSpec(memory_space=pltpu.SMEM),
            pl.BlockSpec((step, width), lambda i: (jnp.minimum(i, half - 1), 0)),
            pl.BlockSpec((step, width), lambda i: (jnp.maximum(i - half, 0), 0)),
            pl.BlockSpec((per, 1, SEQ), lambda i: (i, 0, 0)),
        ]
        + [pl.BlockSpec(memory_space=pltpu.HBM)] * len(parts),
        out_specs=(
            pl.BlockSpec((2 * tokens // SEQ, 8, SEQ), lambda i: (0, 0, 0)),
            pl.BlockSpec((SEQ, width), lambda i: (0, 0)),
        ),
        scratch_shapes=[
            pltpu.VMEM((width, block), BF16),
            pltpu.SemaphoreType.DMA((16,)),
        ],
        compiler_params=pltpu.CompilerParams(vmem_limit_bytes=48 << 20),
    )(info, mine, other, local.reshape(2 * tokens // SEQ, 1, SEQ), *parts)


def choose_kernel(info_ref, local_ref, out_ref, most_ref):
    tokens = local_ref.shape[1]
    per = 128
    dests = out_ref.shape[0] // ROOM
    first_slot = info_ref[1] * SLOTS
    local = local_ref[...]
    upper = iota((per, per), 0) < iota((per, per), 1)
    diagonal = iota((per, per), 0) == iota((per, per), 1)

    def group(g, most):
        match = jnp.where(local - g * per == iota((per, tokens), 0), 1.0, 0.0)
        hits = match.astype(BF16)
        present = jnp.broadcast_to(jnp.max(match, axis=1, keepdims=True), (per, per))
        rank = jnp.sum(jnp.where(upper, present, 0.0), axis=0, keepdims=True).astype(jnp.int32)
        here = jnp.sum(jnp.where(diagonal, present, 0.0), axis=0, keepdims=True)
        slot = iota((ROOM, per), 0)
        chosen = (slot < SLOTS) & (slot == rank - first_slot) & (here > 0.5)
        packing = jnp.where(chosen, 1.0, 0.0).astype(BF16)
        out_ref[pl.ds(pl.multiple_of(g * ROOM, ROOM), ROOM), :] = dot(packing, hits).astype(BF16)
        return jnp.maximum(most, jnp.sum(here, axis=1, keepdims=True))

    most = lax.fori_loop(0, dests, group, jnp.zeros((1, 1), F32), unroll=2)
    most_ref[...] = jnp.broadcast_to(most, most_ref.shape)


def choices(info, local, dests):
    return pl.pallas_call(
        choose_kernel,
        out_shape=(
            jax.ShapeDtypeStruct((dests * ROOM, local.shape[1]), BF16),
            jax.ShapeDtypeStruct((8, 128), F32),
        ),
        in_specs=[pl.BlockSpec(memory_space=pltpu.SMEM), pl.BlockSpec(memory_space=pltpu.VMEM)],
        out_specs=(pl.BlockSpec(memory_space=pltpu.VMEM), pl.BlockSpec(memory_space=pltpu.VMEM)),
        compiler_params=pltpu.CompilerParams(vmem_limit_bytes=40 << 20),
    )(info, local)


def pack_kernel(hits_ref, most_ref, mine_ref, other_ref, out_ref):
    dests, _, width = out_ref.shape
    half = mine_ref.shape[0]
    some = dests // 2

    def pack(i, _):
        hits = hits_ref[pl.ds(pl.multiple_of(i * some * ROOM, some * ROOM), some * ROOM), :]
        sums = dot(hits[:, 0:half], mine_ref[...]) + dot(hits[:, half:], other_ref[...])
        sums = sums.reshape(some, ROOM, width)[:, 0:BLOCK, :]
        last = iota(sums.shape, 1) == SLOTS
        out_ref[pl.ds(i * some, some)] = jnp.where(
            last, most_ref[0:1, 0:1].reshape(1, 1, 1), sums
        ).astype(BF16)
        return 0

    lax.fori_loop(0, 2, pack, 0)


def packed_sums(chosen, mine, other):
    hits, most = chosen
    width = mine.shape[1]
    return pl.pallas_call(
        pack_kernel,
        out_shape=jax.ShapeDtypeStruct((hits.shape[0] // ROOM, BLOCK, width), BF16),
        in_specs=[pl.BlockSpec(memory_space=pltpu.VMEM)] * 4,
        out_specs=pl.BlockSpec(memory_space=pltpu.VMEM),
        compiler_params=pltpu.CompilerParams(vmem_limit_bytes=40 << 20),
    )(hits, most, mine, other)


def count_kernel(info_ref, assign_ref, out_ref):
    dp, slabs, _ = assign_ref.shape
    targets = iota((128, SEQ), 0) + info_ref[0]
    lane = iota(out_ref.shape, 1)

    def slab(f, out):
        acc = jnp.zeros((128, SEQ), F32)
        for d in range(dp):
            acc = acc + jnp.where(assign_ref[d, pl.ds(f, 1), :] == targets, 1.0, 0.0)
        return jnp.where(lane == f, jnp.sum(acc, axis=1, keepdims=True), out)

    out_ref[...] = lax.fori_loop(0, slabs, slab, jnp.zeros(out_ref.shape, F32))


def counted(info, assign):
    return pl.pallas_call(
        count_kernel,
        out_shape=jax.ShapeDtypeStruct((128, 128), F32),
        in_specs=[pl.BlockSpec(memory_space=pltpu.SMEM), pl.BlockSpec(memory_space=pltpu.VMEM)],
        out_specs=pl.BlockSpec(memory_space=pltpu.VMEM),
    )(info, assign)


def unpack_kernel(info_ref, counts_ref, got_ref, out_ref, most_ref):
    slabs, _, width = got_ref.shape
    counts = counts_ref[...]
    present = jnp.where(counts > 0.5, 1.0, 0.0).astype(BF16)
    lower = jnp.where(iota((128, 128), 1) < iota((128, 128), 0), 1.0, 0.0).astype(BF16)
    rank = dot(lower, present).astype(jnp.int32) - info_ref[1] * SLOTS
    slot = iota((128, BLOCK), 1)
    parts = []
    for f in range(slabs):
        chosen = (slot == rank[:, f : f + 1]) & (slot < SLOTS) & (counts[:, f : f + 1] > 0.5)
        parts.append(jnp.where(chosen, 1.0, 0.0))
    hits = jnp.concatenate(parts, axis=1).astype(BF16)
    out_ref[...] = dot(hits, got_ref[...].reshape(slabs * BLOCK, width))
    most = jnp.max(got_ref[:, SLOTS, 0:128].astype(F32), axis=0, keepdims=True)
    most_ref[...] = jnp.broadcast_to(most, most_ref.shape).astype(jnp.int32)


def unpacked_sums(info, counts, got):
    return pl.pallas_call(
        unpack_kernel,
        out_shape=(
            jax.ShapeDtypeStruct((128, got.shape[2]), F32),
            jax.ShapeDtypeStruct((8, 128), jnp.int32),
        ),
        in_specs=[pl.BlockSpec(memory_space=pltpu.SMEM)]
        + [pl.BlockSpec(memory_space=pltpu.VMEM)] * 2,
        out_specs=(pl.BlockSpec(memory_space=pltpu.VMEM), pl.BlockSpec(memory_space=pltpu.VMEM)),
    )(info, counts, got)


def exchanged(blocks, axis):
    return lax.all_to_all(blocks, axis, 0, 0, tiled=True)


def gathered(shard, axis):
    devices = lax.axis_size(axis)
    return exchanged(jnp.broadcast_to(shard[None], (devices,) + shard.shape), axis)


def swapped(shard, axis):
    return lax.ppermute(shard, axis, [(0, 1), (1, 0)])


def turned(shard, axis, by):
    devices = lax.axis_size(axis)
    return lax.ppermute(shard, axis, [(i, (i + by) % devices) for i in range(devices)])


def neighbours(block, axis):
    return turned(block, axis, 1), turned(block, axis, lax.axis_size(axis) - 1)


def far_halves(back, ahead, axis):
    half = back.shape[0] // 2
    return turned(back[:half], axis, 1), turned(ahead[half:], axis, lax.axis_size(axis) - 1)


def backwards(values, here):
    for dim, at in enumerate(here):
        size = values.shape[dim]
        values = jnp.take(values, (at - jnp.arange(size)) % size, axis=dim)
    return values


def shards(token_ids, embed_table, w_qkv, w_out, ln_gain, ln_bias, centroids_t, assignments):
    core = lax.axis_index("core")
    dp_rank = lax.axis_index(DP)
    fs_rank = lax.axis_index(FS)
    fs_size = lax.axis_size(FS)
    dp_size = lax.axis_size(DP)
    x_size = lax.axis_size("x")
    vocab, width = embed_table.shape
    zero = jnp.int32(0)
    ids = token_ids.reshape(fs_size, SEQ)

    at_x = lax.axis_index("x")

    def info_of(*values):
        return jnp.stack([jnp.asarray(v, jnp.int32) for v in values])

    by_dev = assignments.reshape(2, x_size, 2, fs_size, SEQ)
    of_slab = lax.dynamic_index_in_dim(by_dev, fs_rank, 3, keepdims=False)
    of_slab = jnp.transpose(of_slab, (2, 1, 0, 3))
    here = (core, at_x, lax.axis_index("zh"))
    of_slab = backwards(of_slab, here)
    block = centroids_t.shape[1]
    local = of_slab.reshape(1, -1) - dp_rank * block
    chosen = choices(info_of(zero, zero), local, fs_size)
    counts = counted(
        info_of(dp_rank * block + fs_rank * (block // fs_size)),
        assignments.reshape(dp_size, fs_size, SEQ),
    )

    part = (w_qkv.shape[1] + w_out.shape[1]) // (2 * x_size)
    both = jnp.concatenate([w_qkv, w_out], axis=1)
    piece = lax.dynamic_slice_in_dim(both, (core * x_size + at_x) * part, part, 1)
    column = gathered(piece, FS).reshape(width, part)

    two = jnp.concatenate([ids, swapped(ids, "zh")], axis=0)
    ids = [two] + [turned(two, "x", k) for k in range(1, x_size)]

    sent = listed_rows(info_of(fs_rank, zero), ids, embed_table)
    sent, column, local, shard = lax.optimization_barrier((sent, column, local, centroids_t))
    w_back, w_ahead = neighbours(column, "x")
    near = joined([shard] + [turned(shard, "zl", k) for k in range(1, 4)])
    places = placed_rows(info_of(fs_rank, zero, vocab), ids, fs_size)
    w_back, w_ahead, chosen, places, counts = lax.optimization_barrier(
        (w_back, w_ahead, chosen, places, counts)
    )
    rings = [column, w_back, *far_halves(w_back, w_ahead, "x"), w_ahead]
    rings += [swapped(w, "core") for w in rings]
    got = exchanged(sent, FS)
    got, near, *rings = lax.optimization_barrier((got, near, *rings))
    slab, rounds = expanded(places, got)

    def more_rows(state):
        turn, acc = state
        again = exchanged(listed_rows(info_of(fs_rank, turn), ids, embed_table), FS)
        extra, _ = expanded(placed_rows(info_of(fs_rank, turn, vocab), ids, fs_size), again)
        return turn + 1, acc + extra

    rounds = rounds[0, 0]
    _, slab = lax.while_loop(lambda state: state[0] < rounds, more_rows, (jnp.int32(1), slab))

    back, ahead = neighbours(near, "y")

    mine = encoded(info_of(core, at_x), rings, slab, ln_gain, ln_bias)
    mine, back, ahead = lax.optimization_barrier((mine, back, ahead))
    far_low, far_high = far_halves(back, ahead, "y")
    other = swapped(mine, "core")

    def one_turn(turn):
        info = info_of(zero, turn)
        got = exchanged(packed_sums(choices(info, local, fs_size), mine, other), FS)
        return unpacked_sums(info, counts, got)[0]

    packed = packed_sums(chosen, mine, other)
    packed, mine, other, far_low, far_high = lax.optimization_barrier(
        (packed, mine, other, far_low, far_high)
    )
    got = exchanged(packed, FS)

    stats, previous = scored(
        info_of(lax.axis_index("y"), fs_rank, *here, x_size, lax.axis_index("zl")),
        mine,
        other,
        local,
        [near, back, far_low, far_high, ahead],
    )
    stats, got = lax.optimization_barrier((stats, got))
    sums, widest = unpacked_sums(info_of(zero, zero), counts, got)
    widest = widest[0, 0]
    _, sums = lax.while_loop(
        lambda state: state[0] * SLOTS < widest,
        lambda state: (state[0] + 1, state[1] + one_turn(state[0])),
        (jnp.int32(1), sums),
    )

    home = exchanged(stats, DP)
    lse = home[:, 0, :]
    peak = jnp.max(lse, axis=0)
    token_loss = (
        jnp.log(jnp.sum(jnp.exp(lse - peak[None, :]), axis=0)) + peak - jnp.sum(home[:, 1, :], axis=0)
    )

    total = jnp.sum(counts[:, 0:fs_size], axis=1, keepdims=True)
    new_centroids = jnp.where(total > 0, sums / jnp.maximum(total, 1.0), previous)
    return token_loss, new_centroids


def solution(mesh):
    finer = Mesh(mesh.devices.reshape(2, 4, 2, 4, 4), ALL)
    placed = (P(DP), P(FS, None), P(FS, None), P(FS, None), P(), P(), P(FS, DP), P())
    return jax.shard_map(
        shards, mesh=finer, in_specs=placed, out_specs=(P(ALL), P(ALL, None)), check_vma=False
    )
```

```python
import jax
import jax.numpy as jnp
from jax import lax
from jax.experimental import pallas as pl
from jax.experimental.pallas import tpu as pltpu
from jax.sharding import Mesh
from jax.sharding import PartitionSpec as P

HEADS = 12
HEAD = 64
SEQ = 128
DP = ("zh", "x", "core")
FS = ("y", "zl")
ALL = DP + FS
LIST = 30
SLOTS = 25
BLOCK = 40
ROOM = 48
F32 = jnp.float32
BF16 = jnp.bfloat16


RING = ((0, 0, 2), (1, 0, 2), (2, 0, 1), (2, 1, 1), (3, 0, 2))


def iota(shape, dim):
    return lax.broadcasted_iota(jnp.int32, shape, dim)


def dot(a, b, dims=((1,), (0,))):
    return lax.dot_general(a, b, (dims, ((), ())), preferred_element_type=F32)


def ranked(present, groups):
    rows = present.shape[0]
    per = rows // groups
    upper = jnp.where(iota((128, 128), 0) < iota((128, 128), 1), 1.0, 0.0).astype(BF16)
    at, of = iota((rows, rows), 0), iota((rows, rows), 1)
    above = jnp.where((at // per == of // per) & (of < at), 1.0, 0.0).astype(BF16)
    ones = present.astype(BF16)
    return dot(ones, upper) + jnp.sum(dot(above, ones), axis=1, keepdims=True)


def tokens_of(ids_refs, dest):
    dests = ids_refs[0].shape[0] // 2
    return jnp.concatenate(
        [ref[pl.ds(z * dests + dest, 1), :] for ref in ids_refs for z in range(2)], axis=1
    )


def lists_kernel(info_ref, *refs):
    ids_refs, table_ref, rows_ref, present_ref, rank_ref, hits_ref = refs[0:4], *refs[4:]
    vocab = table_ref.shape[0]
    dests, tokens = rows_ref.shape[0], 8 * SEQ
    base = info_ref[0] * vocab
    first_slot = info_ref[1] * LIST
    high = 16

    def find(p, _):
        local = tokens_of(ids_refs, p) - base
        inside = (local >= 0) & (local < vocab)
        block = jnp.where((iota((high, tokens), 0) == (local >> 7)) & inside, 1.0, 0.0).astype(BF16)
        lane = jnp.where(iota((128, tokens), 0) == (local & 127), 1.0, 0.0).astype(BF16)
        seen = dot(block, lane, ((1,), (1,)))
        present_ref[pl.ds(pl.multiple_of(p * high, high), high), :] = jnp.where(seen > 0.5, 1.0, 0.0)
        return 0

    lax.fori_loop(0, dests, find, 0, unroll=4)
    present = present_ref[...]
    rank_ref[...] = jnp.where(present > 0.5, ranked(present, dests) - first_slot.astype(F32), -1.0)
    blocks = -(-vocab // 128)

    def choose(p, most):
        ranks = rank_ref[pl.ds(pl.multiple_of(p * high, high), high), :]
        slot = iota((ROOM, 128), 0)
        for h in range(blocks):
            chosen = (slot == ranks[h : h + 1, :].astype(jnp.int32)) & (slot < LIST)
            hits_ref[pl.ds(pl.multiple_of(p * ROOM, ROOM), ROOM), h * 128 : (h + 1) * 128] = jnp.where(
                chosen, 1.0, 0.0
            ).astype(BF16)
        return jnp.maximum(most, jnp.max(ranks))

    most = lax.fori_loop(0, dests, choose, jnp.float32(-1.0), unroll=2) + first_slot.astype(F32)
    whole = vocab // 16 * 16
    rounds = jnp.floor(most * (1.0 / LIST) + 1e-3) + 1.0
    some = 4

    def fetch(i, _):
        hits = hits_ref[pl.ds(pl.multiple_of(i * some * ROOM, some * ROOM), some * ROOM), :]
        rows = dot(hits[:, 0:whole], table_ref[0:whole, :])
        if whole < vocab:
            tail = table_ref[whole:vocab, :].astype(F32)
            for k in range(vocab - whole):
                rows = rows + hits[:, whole + k : whole + k + 1].astype(F32) * tail[k : k + 1, :]
        rows = rows.reshape(some, ROOM, rows.shape[1])
        rows_ref[pl.ds(i * some, some)] = jnp.where(iota(rows.shape, 1) == LIST, rounds, rows).astype(BF16)
        return 0

    lax.fori_loop(0, dests // some, fetch, 0)


def listed_rows(info, ids, table):
    dests = ids[0].shape[0] // 2
    width = table.shape[1]
    return pl.pallas_call(
        lists_kernel,
        out_shape=jax.ShapeDtypeStruct((dests, ROOM, width), BF16),
        in_specs=[pl.BlockSpec(memory_space=pltpu.SMEM)]
        + [pl.BlockSpec(memory_space=pltpu.VMEM)] * (len(ids) + 1),
        out_specs=pl.BlockSpec(memory_space=pltpu.VMEM),
        scratch_shapes=[
            pltpu.VMEM((dests * 16, 128), F32),
            pltpu.VMEM((dests * 16, 128), F32),
            pltpu.VMEM((dests * ROOM, 16 * 128), BF16),
        ],
        compiler_params=pltpu.CompilerParams(vmem_limit_bytes=40 << 20),
    )(info, *ids, table)


def place_kernel(info_ref, *refs):
    ids_refs, out_ref = refs[0:4], refs[4]
    tokens = 8 * SEQ
    owners = out_ref.shape[1] // ROOM
    first_slot = info_ref[1] * LIST
    vocab = info_ref[2]
    row = tokens_of(ids_refs, info_ref[0])
    owner = jnp.zeros(row.shape, jnp.int32)
    for k in range(1, owners):
        owner = owner + jnp.where(row >= k * vocab, 1, 0)
    local = row - owner * vocab
    group = owner * 16 + (local >> 7)
    block = jnp.where(iota((owners * 16, tokens), 0) == group, 1.0, 0.0).astype(BF16)
    lane = jnp.where(iota((128, tokens), 0) == (local & 127), 1.0, 0.0).astype(BF16)
    present = jnp.where(dot(block, lane, ((1,), (1,))) > 0.5, 1.0, 0.0)
    rank = ranked(present, owners) - first_slot.astype(F32)
    rank = jnp.where((rank >= 0) & (rank < LIST), rank, 255.0).astype(BF16)
    owner = owner.astype(F32)
    low = (local & 127).astype(F32)
    for t in range(tokens // 128):
        cols = slice(t * 128, (t + 1) * 128)
        found = lax.dot_general(
            block[:, cols], rank, (((0,), (0,)), ((), ())), preferred_element_type=F32
        )
        down = jnp.broadcast_to(low[:, cols], (128, 128)).T
        slot = jnp.sum(jnp.where(iota((128, 128), 1).astype(F32) == down, found, 0.0), axis=1, keepdims=True)
        of = jnp.broadcast_to(owner[:, cols], (128, 128)).T[:, 0:1]
        place = jnp.where(slot < LIST, of * ROOM + slot, -1.0).astype(jnp.int32)
        out_ref[cols, :] = jnp.where(place == iota((128, owners * ROOM), 1), 1.0, 0.0).astype(BF16)


def placed_rows(info, ids, owners):
    return pl.pallas_call(
        place_kernel,
        out_shape=jax.ShapeDtypeStruct((8 * SEQ, owners * ROOM), BF16),
        in_specs=[pl.BlockSpec(memory_space=pltpu.SMEM)]
        + [pl.BlockSpec(memory_space=pltpu.VMEM)] * len(ids),
        out_specs=pl.BlockSpec(memory_space=pltpu.VMEM),
        compiler_params=pltpu.CompilerParams(vmem_limit_bytes=40 << 20),
    )(info, *ids)


def expand_kernel(places_ref, got_ref, out_ref, rounds_ref):
    owners, room, width = got_ref.shape
    got = got_ref[...].reshape(owners * room, width)

    def fill(i, _):
        rows = pl.ds(pl.multiple_of(i * 2 * SEQ, 2 * SEQ), 2 * SEQ)
        out_ref[rows, :] = dot(places_ref[rows, :], got).astype(BF16)
        return 0

    lax.fori_loop(0, out_ref.shape[0] // (2 * SEQ), fill, 0)
    most = jnp.max(got_ref[:, LIST, 0:128].astype(F32), axis=0, keepdims=True)
    rounds_ref[...] = jnp.broadcast_to(most, rounds_ref.shape).astype(jnp.int32)


def expanded(places, got):
    return pl.pallas_call(
        expand_kernel,
        out_shape=(
            jax.ShapeDtypeStruct((places.shape[0], got.shape[2]), BF16),
            jax.ShapeDtypeStruct((8, 128), jnp.int32),
        ),
        in_specs=[pl.BlockSpec(memory_space=pltpu.VMEM)] * 2,
        out_specs=(pl.BlockSpec(memory_space=pltpu.VMEM), pl.BlockSpec(memory_space=pltpu.VMEM)),
        compiler_params=pltpu.CompilerParams(vmem_limit_bytes=40 << 20),
    )(places, got)


def join_kernel(*refs):
    parts, out_ref = refs[:-1], refs[-1]
    rows = parts[0].shape[0]
    for k, ref in enumerate(parts):
        out_ref[k * rows : (k + 1) * rows, :] = ref[...]


def joined(parts):
    rows, cols = parts[0].shape
    return pl.pallas_call(
        join_kernel,
        out_shape=jax.ShapeDtypeStruct((len(parts) * rows, cols), parts[0].dtype),
        in_specs=[pl.BlockSpec(memory_space=pltpu.VMEM)] * len(parts),
        out_specs=pl.BlockSpec(memory_space=pltpu.VMEM),
    )(*parts)


def put(sources, targets, sems):
    copies = [
        pltpu.make_async_copy(src, dst, sems.at[k])
        for k, (src, dst) in enumerate(zip(sources, targets, strict=True))
    ]
    for c in copies:
        c.start()
    for c in copies:
        c.wait()


def encode_kernel(info_ref, *refs):
    rings = refs[0:10]
    slab_ref, gain_ref, bias_ref, out_ref, w_ref, packed_ref, scores_ref, probs_ref, context_ref, sems = (
        refs[10:]
    )
    x_size = 4
    core, at_x = info_ref[0], info_ref[1]
    depth, part = w_ref.shape[1:]
    targets = []
    for core_at in (core, 1 - core):
        for back, first, count in RING:
            place = core_at * x_size + lax.rem(at_x - back + x_size, x_size)
            targets.append(w_ref.at[place, pl.ds(first * (depth // 2), count * (depth // 2)), :])
    put(rings, targets, sems)
    tokens, width = packed_ref.shape[0], slab_ref.shape[1]
    left = iota((SEQ, 2 * HEAD), 1) < HEAD
    zero = jnp.zeros((SEQ, 2 * HEAD), BF16)
    pairs = HEADS // 2
    passages = tokens // SEQ

    def stacked(values):
        return jnp.concatenate([jnp.where(left, values, zero), jnp.where(left, zero, values)], axis=0)

    def step(i, _):
        x = slab_ref[pl.ds(i * tokens, tokens), :]
        for j in range(6):
            packed_ref[:, j * part : (j + 1) * part] = dot(x, w_ref[j]).astype(BF16)
        for b in range(passages):
            rows = slice(b * SEQ, (b + 1) * SEQ)
            for pair in range(pairs):
                at = pair * 2 * HEAD
                q = packed_ref[rows, at : at + 2 * HEAD] * jnp.asarray(HEAD**-0.5, BF16)
                k = packed_ref[rows, width + at : width + at + 2 * HEAD]
                scores_ref[b * pairs + pair] = dot(q, stacked(k), ((1,), (1,)))
        for n in range(passages * pairs):
            for h in range(2):
                s = scores_ref[n, :, h * SEQ : (h + 1) * SEQ]
                e = jnp.exp(s - jnp.max(s, axis=1, keepdims=True))
                probs = e * (1.0 / jnp.sum(e, axis=1, keepdims=True))
                probs_ref[n, :, h * SEQ : (h + 1) * SEQ] = probs.astype(BF16)
        for b in range(passages):
            rows = slice(b * SEQ, (b + 1) * SEQ)
            for pair in range(pairs):
                at = pair * 2 * HEAD
                v = packed_ref[rows, 2 * width + at : 2 * width + at + 2 * HEAD]
                context_ref[rows, at : at + 2 * HEAD] = dot(
                    probs_ref[b * pairs + pair], stacked(v)
                ).astype(BF16)
        context = context_ref[...]
        half = width // 2
        mixed = [
            dot(context, w_ref[6 + k]) + x[:, k * half : (k + 1) * half].astype(F32) for k in range(2)
        ]
        mean = sum(jnp.sum(m, axis=1, keepdims=True) for m in mixed) * (1.0 / width)
        center = [m - mean for m in mixed]
        spread = sum(jnp.sum(c * c, axis=1, keepdims=True) for c in center) * (1.0 / width)
        scale = lax.rsqrt(spread + 1e-05)
        for k in range(2):
            cols = slice(k * half, (k + 1) * half)
            out_ref[pl.ds(i * tokens, tokens), cols] = (
                center[k] * scale * gain_ref[:, cols] + bias_ref[:, cols]
            ).astype(BF16)
        return 0

    lax.fori_loop(0, slab_ref.shape[0] // tokens, step, 0)


def encoded(info, rings, slab, gain, bias):
    part = rings[0].shape[1]
    tokens, width = 2 * SEQ, slab.shape[1]
    pairs = tokens // SEQ * HEADS // 2
    return pl.pallas_call(
        encode_kernel,
        out_shape=jax.ShapeDtypeStruct(slab.shape, BF16),
        in_specs=[pl.BlockSpec(memory_space=pltpu.SMEM)]
        + [pl.BlockSpec(memory_space=pltpu.HBM)] * len(rings)
        + [pl.BlockSpec(memory_space=pltpu.VMEM)] * 3,
        out_specs=pl.BlockSpec(memory_space=pltpu.VMEM),
        scratch_shapes=[
            pltpu.VMEM((8, width, part), BF16),
            pltpu.VMEM((tokens, 3 * width), BF16),
            pltpu.VMEM((pairs, SEQ, 2 * SEQ), F32),
            pltpu.VMEM((pairs, SEQ, 2 * SEQ), BF16),
            pltpu.VMEM((tokens, width), BF16),
            pltpu.SemaphoreType.DMA((len(rings),)),
        ],
        compiler_params=pltpu.CompilerParams(vmem_limit_bytes=40 << 20),
    )(info, *rings, slab, gain.reshape(1, width), bias.reshape(1, width))


def score_kernel(info_ref, mine_ref, other_ref, local_ref, *refs):
    parts = refs[0:5]
    out_ref, old_ref, cent_ref, sems = refs[5:]
    step = pl.program_id(0)
    half = pl.num_programs(0) // 2

    @pl.when(step == 0)
    def _():
        shard = parts[0].shape[0] // 4
        sources, targets = [], []
        for ref, (back, first, count) in zip(parts, RING, strict=True):
            owner = lax.rem(info_ref[0] - back + 4, 4) * 4
            for k in range(2 * count):
                start = (owner + lax.rem(info_ref[6] - 2 * first - k + 4, 4)) * shard
                sources.append(ref.at[pl.ds(k * shard, shard), :])
                targets.append(cent_ref.at[pl.ds(pl.multiple_of(start, shard), shard), :])
        put(sources, targets, sems)

    block = cent_ref.shape[1]
    span = 2 * SEQ
    for n in range(mine_ref.shape[0] // span):
        rows = slice(n * span, (n + 1) * span)
        s = dot(jnp.where(step < half, mine_ref[rows, :], other_ref[rows, :]), cent_ref[...])
        peak = jnp.max(s, axis=1, keepdims=True)
        mass = jnp.sum(jnp.exp(s - peak), axis=1, keepdims=True)
        local = jnp.concatenate(
            [jnp.broadcast_to(local_ref[2 * n + z], (SEQ, SEQ)).T[:, 0:1] for z in range(2)], axis=0
        )
        picked = jnp.sum(jnp.where(local == iota((span, block), 1), s, 0.0), axis=1, keepdims=True)
        both = jnp.where(iota((span, 128), 1) == 0, peak + jnp.log(mass), picked)
        x_size = info_ref[5]
        per_step = mine_ref.shape[0] // span
        back = lax.rem(step, half) * per_step + n
        x = lax.rem(info_ref[3] - back + x_size, x_size)
        core = jnp.where(step < half, info_ref[2], 1 - info_ref[2])
        for z in range(2):
            zh = info_ref[4] if z == 0 else 1 - info_ref[4]
            out_ref[zh * (2 * x_size) + x * 2 + core] = both[z * SEQ : (z + 1) * SEQ, :].T[0:8, :]

    @pl.when(step == pl.num_programs(0) - 1)
    def _():
        per = old_ref.shape[0]
        old = cent_ref[:, pl.ds(pl.multiple_of(info_ref[1] * per, per), per)]
        old_ref[...] = old.astype(F32).T


def scored(info, mine, other, local, parts):
    tokens, width = mine.shape
    block = parts[0].shape[1]
    step = 4 * SEQ
    per = step // SEQ
    half = tokens // step
    return pl.pallas_call(
        score_kernel,
        grid=(2 * half,),
        out_shape=(
            jax.ShapeDtypeStruct((2 * tokens // SEQ, 8, SEQ), F32),
            jax.ShapeDtypeStruct((SEQ, width), F32),
        ),
        in_specs=[
            pl.BlockSpec(memory_space=pltpu.SMEM),
            pl.BlockSpec((step, width), lambda i: (jnp.minimum(i, half - 1), 0)),
            pl.BlockSpec((step, width), lambda i: (jnp.maximum(i - half, 0), 0)),
            pl.BlockSpec((per, 1, SEQ), lambda i: (i, 0, 0)),
        ]
        + [pl.BlockSpec(memory_space=pltpu.HBM)] * len(parts),
        out_specs=(
            pl.BlockSpec((2 * tokens // SEQ, 8, SEQ), lambda i: (0, 0, 0)),
            pl.BlockSpec((SEQ, width), lambda i: (0, 0)),
        ),
        scratch_shapes=[
            pltpu.VMEM((width, block), BF16),
            pltpu.SemaphoreType.DMA((16,)),
        ],
        compiler_params=pltpu.CompilerParams(vmem_limit_bytes=48 << 20),
    )(info, mine, other, local.reshape(2 * tokens // SEQ, 1, SEQ), *parts)


def choose_kernel(info_ref, local_ref, out_ref, most_ref):
    tokens = local_ref.shape[1]
    per = 128
    dests = out_ref.shape[0] // ROOM
    first_slot = info_ref[1] * SLOTS
    local = local_ref[...]
    upper = iota((per, per), 0) < iota((per, per), 1)
    diagonal = iota((per, per), 0) == iota((per, per), 1)

    def group(g, most):
        match = jnp.where(local - g * per == iota((per, tokens), 0), 1.0, 0.0)
        hits = match.astype(BF16)
        present = jnp.broadcast_to(jnp.max(match, axis=1, keepdims=True), (per, per))
        rank = jnp.sum(jnp.where(upper, present, 0.0), axis=0, keepdims=True).astype(jnp.int32)
        here = jnp.sum(jnp.where(diagonal, present, 0.0), axis=0, keepdims=True)
        slot = iota((ROOM, per), 0)
        chosen = (slot < SLOTS) & (slot == rank - first_slot) & (here > 0.5)
        packing = jnp.where(chosen, 1.0, 0.0).astype(BF16)
        out_ref[pl.ds(pl.multiple_of(g * ROOM, ROOM), ROOM), :] = dot(packing, hits).astype(BF16)
        return jnp.maximum(most, jnp.sum(here, axis=1, keepdims=True))

    most = lax.fori_loop(0, dests, group, jnp.zeros((1, 1), F32), unroll=2)
    most_ref[...] = jnp.broadcast_to(most, most_ref.shape)


def choices(info, local, dests):
    return pl.pallas_call(
        choose_kernel,
        out_shape=(
            jax.ShapeDtypeStruct((dests * ROOM, local.shape[1]), BF16),
            jax.ShapeDtypeStruct((8, 128), F32),
        ),
        in_specs=[pl.BlockSpec(memory_space=pltpu.SMEM), pl.BlockSpec(memory_space=pltpu.VMEM)],
        out_specs=(pl.BlockSpec(memory_space=pltpu.VMEM), pl.BlockSpec(memory_space=pltpu.VMEM)),
        compiler_params=pltpu.CompilerParams(vmem_limit_bytes=40 << 20),
    )(info, local)


def pack_kernel(hits_ref, most_ref, mine_ref, other_ref, out_ref):
    dests, _, width = out_ref.shape
    half = mine_ref.shape[0]
    some = dests // 2

    def pack(i, _):
        hits = hits_ref[pl.ds(pl.multiple_of(i * some * ROOM, some * ROOM), some * ROOM), :]
        sums = dot(hits[:, 0:half], mine_ref[...]) + dot(hits[:, half:], other_ref[...])
        sums = sums.reshape(some, ROOM, width)[:, 0:BLOCK, :]
        last = iota(sums.shape, 1) == SLOTS
        out_ref[pl.ds(i * some, some)] = jnp.where(
            last, most_ref[0:1, 0:1].reshape(1, 1, 1), sums
        ).astype(BF16)
        return 0

    lax.fori_loop(0, 2, pack, 0)


def packed_sums(chosen, mine, other):
    hits, most = chosen
    width = mine.shape[1]
    return pl.pallas_call(
        pack_kernel,
        out_shape=jax.ShapeDtypeStruct((hits.shape[0] // ROOM, BLOCK, width), BF16),
        in_specs=[pl.BlockSpec(memory_space=pltpu.VMEM)] * 4,
        out_specs=pl.BlockSpec(memory_space=pltpu.VMEM),
        compiler_params=pltpu.CompilerParams(vmem_limit_bytes=40 << 20),
    )(hits, most, mine, other)


def count_kernel(info_ref, assign_ref, out_ref):
    dp, slabs, _ = assign_ref.shape
    targets = iota((128, SEQ), 0) + info_ref[0]
    lane = iota(out_ref.shape, 1)

    def slab(f, out):
        acc = jnp.zeros((128, SEQ), F32)
        for d in range(dp):
            acc = acc + jnp.where(assign_ref[d, pl.ds(f, 1), :] == targets, 1.0, 0.0)
        return jnp.where(lane == f, jnp.sum(acc, axis=1, keepdims=True), out)

    out_ref[...] = lax.fori_loop(0, slabs, slab, jnp.zeros(out_ref.shape, F32))


def counted(info, assign):
    return pl.pallas_call(
        count_kernel,
        out_shape=jax.ShapeDtypeStruct((128, 128), F32),
        in_specs=[pl.BlockSpec(memory_space=pltpu.SMEM), pl.BlockSpec(memory_space=pltpu.VMEM)],
        out_specs=pl.BlockSpec(memory_space=pltpu.VMEM),
    )(info, assign)


def unpack_kernel(info_ref, counts_ref, got_ref, out_ref, most_ref):
    slabs, _, width = got_ref.shape
    counts = counts_ref[...]
    present = jnp.where(counts > 0.5, 1.0, 0.0).astype(BF16)
    lower = jnp.where(iota((128, 128), 1) < iota((128, 128), 0), 1.0, 0.0).astype(BF16)
    rank = dot(lower, present).astype(jnp.int32) - info_ref[1] * SLOTS
    slot = iota((128, BLOCK), 1)
    parts = []
    for f in range(slabs):
        chosen = (slot == rank[:, f : f + 1]) & (slot < SLOTS) & (counts[:, f : f + 1] > 0.5)
        parts.append(jnp.where(chosen, 1.0, 0.0))
    hits = jnp.concatenate(parts, axis=1).astype(BF16)
    out_ref[...] = dot(hits, got_ref[...].reshape(slabs * BLOCK, width))
    most = jnp.max(got_ref[:, SLOTS, 0:128].astype(F32), axis=0, keepdims=True)
    most_ref[...] = jnp.broadcast_to(most, most_ref.shape).astype(jnp.int32)


def unpacked_sums(info, counts, got):
    return pl.pallas_call(
        unpack_kernel,
        out_shape=(
            jax.ShapeDtypeStruct((128, got.shape[2]), F32),
            jax.ShapeDtypeStruct((8, 128), jnp.int32),
        ),
        in_specs=[pl.BlockSpec(memory_space=pltpu.SMEM)]
        + [pl.BlockSpec(memory_space=pltpu.VMEM)] * 2,
        out_specs=(pl.BlockSpec(memory_space=pltpu.VMEM), pl.BlockSpec(memory_space=pltpu.VMEM)),
    )(info, counts, got)


def exchanged(blocks, axis):
    return lax.all_to_all(blocks, axis, 0, 0, tiled=True)


def gathered(shard, axis):
    devices = lax.axis_size(axis)
    return exchanged(jnp.broadcast_to(shard[None], (devices,) + shard.shape), axis)


def swapped(shard, axis):
    return lax.ppermute(shard, axis, [(0, 1), (1, 0)])


def turned(shard, axis, by):
    devices = lax.axis_size(axis)
    return lax.ppermute(shard, axis, [(i, (i + by) % devices) for i in range(devices)])


def neighbours(block, axis):
    return turned(block, axis, 1), turned(block, axis, lax.axis_size(axis) - 1)


def far_halves(back, ahead, axis):
    half = back.shape[0] // 2
    return turned(back[:half], axis, 1), turned(ahead[half:], axis, lax.axis_size(axis) - 1)


def backwards(values, here):
    for dim, at in enumerate(here):
        size = values.shape[dim]
        values = jnp.take(values, (at - jnp.arange(size)) % size, axis=dim)
    return values


def shards(token_ids, embed_table, w_qkv, w_out, ln_gain, ln_bias, centroids_t, assignments):
    core = lax.axis_index("core")
    dp_rank = lax.axis_index(DP)
    fs_rank = lax.axis_index(FS)
    fs_size = lax.axis_size(FS)
    dp_size = lax.axis_size(DP)
    x_size = lax.axis_size("x")
    vocab, width = embed_table.shape
    zero = jnp.int32(0)
    ids = token_ids.reshape(fs_size, SEQ)

    at_x = lax.axis_index("x")

    def info_of(*values):
        return jnp.stack([jnp.asarray(v, jnp.int32) for v in values])

    by_dev = assignments.reshape(2, x_size, 2, fs_size, SEQ)
    of_slab = lax.dynamic_index_in_dim(by_dev, fs_rank, 3, keepdims=False)
    of_slab = jnp.transpose(of_slab, (2, 1, 0, 3))
    here = (core, at_x, lax.axis_index("zh"))
    of_slab = backwards(of_slab, here)
    block = centroids_t.shape[1]
    local = of_slab.reshape(1, -1) - dp_rank * block
    chosen = choices(info_of(zero, zero), local, fs_size)
    counts = counted(
        info_of(dp_rank * block + fs_rank * (block // fs_size)),
        assignments.reshape(dp_size, fs_size, SEQ),
    )

    part = (w_qkv.shape[1] + w_out.shape[1]) // (2 * x_size)
    both = jnp.concatenate([w_qkv, w_out], axis=1)
    piece = lax.dynamic_slice_in_dim(both, (core * x_size + at_x) * part, part, 1)
    column = gathered(piece, FS).reshape(width, part)

    two = jnp.concatenate([ids, swapped(ids, "zh")], axis=0)
    ids = [two] + [turned(two, "x", k) for k in range(1, x_size)]

    sent = listed_rows(info_of(fs_rank, zero), ids, embed_table)
    sent, column, local, shard = lax.optimization_barrier((sent, column, local, centroids_t))
    w_back, w_ahead = neighbours(column, "x")
    near = joined([shard] + [turned(shard, "zl", k) for k in range(1, 4)])
    places = placed_rows(info_of(fs_rank, zero, vocab), ids, fs_size)
    w_back, w_ahead, chosen, places, counts = lax.optimization_barrier(
        (w_back, w_ahead, chosen, places, counts)
    )
    rings = [column, w_back, *far_halves(w_back, w_ahead, "x"), w_ahead]
    rings += [swapped(w, "core") for w in rings]
    got = exchanged(sent, FS)
    got, near, *rings = lax.optimization_barrier((got, near, *rings))
    slab, rounds = expanded(places, got)

    def more_rows(state):
        turn, acc = state
        again = exchanged(listed_rows(info_of(fs_rank, turn), ids, embed_table), FS)
        extra, _ = expanded(placed_rows(info_of(fs_rank, turn, vocab), ids, fs_size), again)
        return turn + 1, acc + extra

    rounds = rounds[0, 0]
    _, slab = lax.while_loop(lambda state: state[0] < rounds, more_rows, (jnp.int32(1), slab))

    back, ahead = neighbours(near, "y")

    mine = encoded(info_of(core, at_x), rings, slab, ln_gain, ln_bias)
    mine, back, ahead = lax.optimization_barrier((mine, back, ahead))
    far_low, far_high = far_halves(back, ahead, "y")
    other = swapped(mine, "core")

    def one_turn(turn):
        info = info_of(zero, turn)
        got = exchanged(packed_sums(choices(info, local, fs_size), mine, other), FS)
        return unpacked_sums(info, counts, got)[0]

    packed = packed_sums(chosen, mine, other)
    packed, mine, other, far_low, far_high = lax.optimization_barrier(
        (packed, mine, other, far_low, far_high)
    )
    got = exchanged(packed, FS)

    stats, previous = scored(
        info_of(lax.axis_index("y"), fs_rank, *here, x_size, lax.axis_index("zl")),
        mine,
        other,
        local,
        [near, back, far_low, far_high, ahead],
    )
    stats, got = lax.optimization_barrier((stats, got))
    sums, widest = unpacked_sums(info_of(zero, zero), counts, got)
    widest = widest[0, 0]
    _, sums = lax.while_loop(
        lambda state: state[0] * SLOTS < widest,
        lambda state: (state[0] + 1, state[1] + one_turn(state[0])),
        (jnp.int32(1), sums),
    )

    home = exchanged(stats, DP)
    lse = home[:, 0, :]
    peak = jnp.max(lse, axis=0)
    token_loss = (
        jnp.log(jnp.sum(jnp.exp(lse - peak[None, :]), axis=0)) + peak - jnp.sum(home[:, 1, :], axis=0)
    )

    total = jnp.sum(counts[:, 0:fs_size], axis=1, keepdims=True)
    new_centroids = jnp.where(total > 0, sums / jnp.maximum(total, 1.0), previous)
    return token_loss, new_centroids


def solution(mesh):
    finer = Mesh(mesh.devices.reshape(2, 4, 2, 4, 4), ALL)
    placed = (P(DP), P(FS, None), P(FS, None), P(FS, None), P(), P(), P(FS, DP), P())
    return jax.shard_map(
        shards, mesh=finer, in_specs=placed, out_specs=(P(ALL), P(ALL, None)), check_vma=False
    )
```

```python
import jax
import jax.numpy as jnp
from jax import lax
from jax.experimental import pallas as pl
from jax.experimental.pallas import tpu as pltpu
from jax.sharding import Mesh
from jax.sharding import PartitionSpec as P

HEADS = 12
HEAD = 64
SEQ = 128
DP = ("zh", "x", "core")
FS = ("y", "zl")
ALL = DP + FS
LIST = 47
SLOTS = 39
BLOCK = SLOTS + 1
ROOM = 48
F32 = jnp.float32
BF16 = jnp.bfloat16


RING = ((0, 0, 2), (1, 0, 2), (2, 0, 1), (2, 1, 1), (3, 0, 2))


def iota(shape, dim):
    return lax.broadcasted_iota(jnp.int32, shape, dim)


def dot(a, b, dims=((1,), (0,))):
    return lax.dot_general(a, b, (dims, ((), ())), preferred_element_type=F32)


def ranked(present, groups):
    rows = present.shape[0]
    per = rows // groups
    upper = jnp.where(iota((128, 128), 0) < iota((128, 128), 1), 1.0, 0.0).astype(BF16)
    at, of = iota((rows, rows), 0), iota((rows, rows), 1)
    above = jnp.where((at // per == of // per) & (of < at), 1.0, 0.0).astype(BF16)
    ones = present.astype(BF16)
    return dot(ones, upper) + jnp.sum(dot(above, ones), axis=1, keepdims=True)


def tokens_of(ids_refs, dest):
    dests = ids_refs[0].shape[0] // 2
    return jnp.concatenate(
        [ref[pl.ds(z * dests + dest, 1), :] for ref in ids_refs for z in range(2)], axis=1
    )


def lists_kernel(info_ref, *refs):
    ids_refs, table_ref, rows_ref, present_ref, rank_ref, hits_ref = refs[0:4], *refs[4:]
    vocab = table_ref.shape[0]
    dests, tokens = rows_ref.shape[0], 8 * SEQ
    base = info_ref[0] * vocab
    first_slot = info_ref[1] * LIST
    high = 16

    def find(p, _):
        local = tokens_of(ids_refs, p) - base
        inside = (local >= 0) & (local < vocab)
        block = jnp.where((iota((high, tokens), 0) == (local >> 7)) & inside, 1.0, 0.0).astype(BF16)
        lane = jnp.where(iota((128, tokens), 0) == (local & 127), 1.0, 0.0).astype(BF16)
        seen = dot(block, lane, ((1,), (1,)))
        present_ref[pl.ds(pl.multiple_of(p * high, high), high), :] = jnp.where(seen > 0.5, 1.0, 0.0)
        return 0

    lax.fori_loop(0, dests, find, 0, unroll=4)
    present = present_ref[...]
    rank_ref[...] = jnp.where(present > 0.5, ranked(present, dests) - first_slot.astype(F32), -1.0)
    blocks = -(-vocab // 128)

    def choose(p, most):
        ranks = rank_ref[pl.ds(pl.multiple_of(p * high, high), high), :]
        slot = iota((ROOM, 128), 0)
        for h in range(blocks):
            chosen = (slot == ranks[h : h + 1, :].astype(jnp.int32)) & (slot < LIST)
            hits_ref[pl.ds(pl.multiple_of(p * ROOM, ROOM), ROOM), h * 128 : (h + 1) * 128] = jnp.where(
                chosen, 1.0, 0.0
            ).astype(BF16)
        return jnp.maximum(most, jnp.max(ranks))

    most = lax.fori_loop(0, dests, choose, jnp.float32(-1.0), unroll=2) + first_slot.astype(F32)
    whole = vocab // 16 * 16
    rounds = jnp.floor(most * (1.0 / LIST) + 1e-3) + 1.0
    some = 4

    def fetch(i, _):
        hits = hits_ref[pl.ds(pl.multiple_of(i * some * ROOM, some * ROOM), some * ROOM), :]
        rows = dot(hits[:, 0:whole], table_ref[0:whole, :])
        if whole < vocab:
            tail = table_ref[whole:vocab, :].astype(F32)
            for k in range(vocab - whole):
                rows = rows + hits[:, whole + k : whole + k + 1].astype(F32) * tail[k : k + 1, :]
        rows = rows.reshape(some, ROOM, rows.shape[1])
        rows_ref[pl.ds(i * some, some)] = jnp.where(iota(rows.shape, 1) == LIST, rounds, rows).astype(BF16)
        return 0

    lax.fori_loop(0, dests // some, fetch, 0)


def listed_rows(info, ids, table):
    dests = ids[0].shape[0] // 2
    width = table.shape[1]
    return pl.pallas_call(
        lists_kernel,
        out_shape=jax.ShapeDtypeStruct((dests, ROOM, width), BF16),
        in_specs=[pl.BlockSpec(memory_space=pltpu.SMEM)]
        + [pl.BlockSpec(memory_space=pltpu.VMEM)] * (len(ids) + 1),
        out_specs=pl.BlockSpec(memory_space=pltpu.VMEM),
        scratch_shapes=[
            pltpu.VMEM((dests * 16, 128), F32),
            pltpu.VMEM((dests * 16, 128), F32),
            pltpu.VMEM((dests * ROOM, 16 * 128), BF16),
        ],
        compiler_params=pltpu.CompilerParams(vmem_limit_bytes=40 << 20),
    )(info, *ids, table)


def place_kernel(info_ref, *refs):
    ids_refs, out_ref = refs[0:4], refs[4]
    tokens = 8 * SEQ
    owners = out_ref.shape[1] // ROOM
    first_slot = info_ref[1] * LIST
    vocab = info_ref[2]
    row = tokens_of(ids_refs, info_ref[0])
    owner = jnp.zeros(row.shape, jnp.int32)
    for k in range(1, owners):
        owner = owner + jnp.where(row >= k * vocab, 1, 0)
    local = row - owner * vocab
    group = owner * 16 + (local >> 7)
    block = jnp.where(iota((owners * 16, tokens), 0) == group, 1.0, 0.0).astype(BF16)
    lane = jnp.where(iota((128, tokens), 0) == (local & 127), 1.0, 0.0).astype(BF16)
    present = jnp.where(dot(block, lane, ((1,), (1,))) > 0.5, 1.0, 0.0)
    rank = ranked(present, owners) - first_slot.astype(F32)
    rank = jnp.where((rank >= 0) & (rank < LIST), rank, 255.0).astype(BF16)
    owner = owner.astype(F32)
    low = (local & 127).astype(F32)
    for t in range(tokens // 128):
        cols = slice(t * 128, (t + 1) * 128)
        found = lax.dot_general(
            block[:, cols], rank, (((0,), (0,)), ((), ())), preferred_element_type=F32
        )
        down = jnp.broadcast_to(low[:, cols], (128, 128)).T
        slot = jnp.sum(jnp.where(iota((128, 128), 1).astype(F32) == down, found, 0.0), axis=1, keepdims=True)
        of = jnp.broadcast_to(owner[:, cols], (128, 128)).T[:, 0:1]
        place = jnp.where(slot < LIST, of * ROOM + slot, -1.0).astype(jnp.int32)
        out_ref[cols, :] = jnp.where(place == iota((128, owners * ROOM), 1), 1.0, 0.0).astype(BF16)


def placed_rows(info, ids, owners):
    return pl.pallas_call(
        place_kernel,
        out_shape=jax.ShapeDtypeStruct((8 * SEQ, owners * ROOM), BF16),
        in_specs=[pl.BlockSpec(memory_space=pltpu.SMEM)]
        + [pl.BlockSpec(memory_space=pltpu.VMEM)] * len(ids),
        out_specs=pl.BlockSpec(memory_space=pltpu.VMEM),
        compiler_params=pltpu.CompilerParams(vmem_limit_bytes=40 << 20),
    )(info, *ids)


def expand_kernel(places_ref, got_ref, out_ref, rounds_ref):
    owners, room, width = got_ref.shape
    got = got_ref[...].reshape(owners * room, width)

    def fill(i, _):
        rows = pl.ds(pl.multiple_of(i * 2 * SEQ, 2 * SEQ), 2 * SEQ)
        out_ref[rows, :] = dot(places_ref[rows, :], got).astype(BF16)
        return 0

    lax.fori_loop(0, out_ref.shape[0] // (2 * SEQ), fill, 0)
    most = jnp.max(got_ref[:, LIST, 0:128].astype(F32), axis=0, keepdims=True)
    rounds_ref[...] = jnp.broadcast_to(most, rounds_ref.shape).astype(jnp.int32)


def expanded(places, got):
    return pl.pallas_call(
        expand_kernel,
        out_shape=(
            jax.ShapeDtypeStruct((places.shape[0], got.shape[2]), BF16),
            jax.ShapeDtypeStruct((8, 128), jnp.int32),
        ),
        in_specs=[pl.BlockSpec(memory_space=pltpu.VMEM)] * 2,
        out_specs=(pl.BlockSpec(memory_space=pltpu.VMEM), pl.BlockSpec(memory_space=pltpu.VMEM)),
        compiler_params=pltpu.CompilerParams(vmem_limit_bytes=40 << 20),
    )(places, got)


def join_kernel(*refs):
    parts, out_ref = refs[:-1], refs[-1]
    rows = parts[0].shape[0]
    for k, ref in enumerate(parts):
        out_ref[k * rows : (k + 1) * rows, :] = ref[...]


def joined(parts):
    rows, cols = parts[0].shape
    return pl.pallas_call(
        join_kernel,
        out_shape=jax.ShapeDtypeStruct((len(parts) * rows, cols), parts[0].dtype),
        in_specs=[pl.BlockSpec(memory_space=pltpu.VMEM)] * len(parts),
        out_specs=pl.BlockSpec(memory_space=pltpu.VMEM),
    )(*parts)


def put(sources, targets, sems):
    copies = [
        pltpu.make_async_copy(src, dst, sems.at[k])
        for k, (src, dst) in enumerate(zip(sources, targets, strict=True))
    ]
    for c in copies:
        c.start()
    for c in copies:
        c.wait()


def encode_kernel(info_ref, *refs):
    rings = refs[0:10]
    slab_ref, gain_ref, bias_ref, out_ref, w_ref, packed_ref, scores_ref, probs_ref, context_ref, sems = (
        refs[10:]
    )
    x_size = 4
    core, at_x = info_ref[0], info_ref[1]
    depth, part = w_ref.shape[1:]
    targets = []
    for core_at in (core, 1 - core):
        for back, first, count in RING:
            place = core_at * x_size + lax.rem(at_x - back + x_size, x_size)
            targets.append(w_ref.at[place, pl.ds(first * (depth // 2), count * (depth // 2)), :])
    put(rings, targets, sems)
    tokens, width = packed_ref.shape[0], slab_ref.shape[1]
    left = iota((SEQ, 2 * HEAD), 1) < HEAD
    zero = jnp.zeros((SEQ, 2 * HEAD), BF16)
    pairs = HEADS // 2
    passages = tokens // SEQ

    def stacked(values):
        return jnp.concatenate([jnp.where(left, values, zero), jnp.where(left, zero, values)], axis=0)

    def step(i, _):
        x = slab_ref[pl.ds(i * tokens, tokens), :]
        for j in range(6):
            packed_ref[:, j * part : (j + 1) * part] = dot(x, w_ref[j]).astype(BF16)
        for b in range(passages):
            rows = slice(b * SEQ, (b + 1) * SEQ)
            for pair in range(pairs):
                at = pair * 2 * HEAD
                q = packed_ref[rows, at : at + 2 * HEAD] * jnp.asarray(HEAD**-0.5, BF16)
                k = packed_ref[rows, width + at : width + at + 2 * HEAD]
                scores_ref[b * pairs + pair] = dot(q, stacked(k), ((1,), (1,)))
        for n in range(passages * pairs):
            for h in range(2):
                s = scores_ref[n, :, h * SEQ : (h + 1) * SEQ]
                e = jnp.exp(s - jnp.max(s, axis=1, keepdims=True))
                probs = e * (1.0 / jnp.sum(e, axis=1, keepdims=True))
                probs_ref[n, :, h * SEQ : (h + 1) * SEQ] = probs.astype(BF16)
        for b in range(passages):
            rows = slice(b * SEQ, (b + 1) * SEQ)
            for pair in range(pairs):
                at = pair * 2 * HEAD
                v = packed_ref[rows, 2 * width + at : 2 * width + at + 2 * HEAD]
                context_ref[rows, at : at + 2 * HEAD] = dot(
                    probs_ref[b * pairs + pair], stacked(v)
                ).astype(BF16)
        context = context_ref[...]
        half = width // 2
        mixed = [
            dot(context, w_ref[6 + k]) + x[:, k * half : (k + 1) * half].astype(F32) for k in range(2)
        ]
        mean = sum(jnp.sum(m, axis=1, keepdims=True) for m in mixed) * (1.0 / width)
        center = [m - mean for m in mixed]
        spread = sum(jnp.sum(c * c, axis=1, keepdims=True) for c in center) * (1.0 / width)
        scale = lax.rsqrt(spread + 1e-05)
        for k in range(2):
            cols = slice(k * half, (k + 1) * half)
            out_ref[pl.ds(i * tokens, tokens), cols] = (
                center[k] * scale * gain_ref[:, cols] + bias_ref[:, cols]
            ).astype(BF16)
        return 0

    lax.fori_loop(0, slab_ref.shape[0] // tokens, step, 0)


def encoded(info, rings, slab, gain, bias):
    part = rings[0].shape[1]
    tokens, width = 2 * SEQ, slab.shape[1]
    pairs = tokens // SEQ * HEADS // 2
    return pl.pallas_call(
        encode_kernel,
        out_shape=jax.ShapeDtypeStruct(slab.shape, BF16),
        in_specs=[pl.BlockSpec(memory_space=pltpu.SMEM)]
        + [pl.BlockSpec(memory_space=pltpu.HBM)] * len(rings)
        + [pl.BlockSpec(memory_space=pltpu.VMEM)] * 3,
        out_specs=pl.BlockSpec(memory_space=pltpu.VMEM),
        scratch_shapes=[
            pltpu.VMEM((8, width, part), BF16),
            pltpu.VMEM((tokens, 3 * width), BF16),
            pltpu.VMEM((pairs, SEQ, 2 * SEQ), F32),
            pltpu.VMEM((pairs, SEQ, 2 * SEQ), BF16),
            pltpu.VMEM((tokens, width), BF16),
            pltpu.SemaphoreType.DMA((len(rings),)),
        ],
        compiler_params=pltpu.CompilerParams(vmem_limit_bytes=40 << 20),
    )(info, *rings, slab, gain.reshape(1, width), bias.reshape(1, width))


def score_kernel(info_ref, mine_ref, other_ref, local_ref, *refs):
    parts = refs[0:5]
    out_ref, old_ref, cent_ref, sems = refs[5:]
    step = pl.program_id(0)
    half = pl.num_programs(0) // 2

    @pl.when(step == 0)
    def _():
        shard = parts[0].shape[0] // 4
        sources, targets = [], []
        for ref, (back, first, count) in zip(parts, RING, strict=True):
            owner = lax.rem(info_ref[0] - back + 4, 4) * 4
            for k in range(2 * count):
                start = (owner + lax.rem(info_ref[6] - 2 * first - k + 4, 4)) * shard
                sources.append(ref.at[pl.ds(k * shard, shard), :])
                targets.append(cent_ref.at[pl.ds(pl.multiple_of(start, shard), shard), :])
        put(sources, targets, sems)

    block = cent_ref.shape[1]
    span = 2 * SEQ
    for n in range(mine_ref.shape[0] // span):
        rows = slice(n * span, (n + 1) * span)
        s = dot(jnp.where(step < half, mine_ref[rows, :], other_ref[rows, :]), cent_ref[...])
        peak = jnp.max(s, axis=1, keepdims=True)
        mass = jnp.sum(jnp.exp(s - peak), axis=1, keepdims=True)
        local = jnp.concatenate(
            [jnp.broadcast_to(local_ref[2 * n + z], (SEQ, SEQ)).T[:, 0:1] for z in range(2)], axis=0
        )
        picked = jnp.sum(jnp.where(local == iota((span, block), 1), s, 0.0), axis=1, keepdims=True)
        both = jnp.where(iota((span, 128), 1) == 0, peak + jnp.log(mass), picked)
        x_size = info_ref[5]
        per_step = mine_ref.shape[0] // span
        back = lax.rem(step, half) * per_step + n
        x = lax.rem(info_ref[3] - back + x_size, x_size)
        core = jnp.where(step < half, info_ref[2], 1 - info_ref[2])
        for z in range(2):
            zh = info_ref[4] if z == 0 else 1 - info_ref[4]
            out_ref[zh * (2 * x_size) + x * 2 + core] = both[z * SEQ : (z + 1) * SEQ, :].T[0:8, :]

    @pl.when(step == pl.num_programs(0) - 1)
    def _():
        per = old_ref.shape[0]
        old = cent_ref[:, pl.ds(pl.multiple_of(info_ref[1] * per, per), per)]
        old_ref[...] = old.astype(F32).T


def scored(info, mine, other, local, parts):
    tokens, width = mine.shape
    block = parts[0].shape[1]
    step = 4 * SEQ
    per = step // SEQ
    half = tokens // step
    return pl.pallas_call(
        score_kernel,
        grid=(2 * half,),
        out_shape=(
            jax.ShapeDtypeStruct((2 * tokens // SEQ, 8, SEQ), F32),
            jax.ShapeDtypeStruct((SEQ, width), F32),
        ),
        in_specs=[
            pl.BlockSpec(memory_space=pltpu.SMEM),
            pl.BlockSpec((step, width), lambda i: (jnp.minimum(i, half - 1), 0)),
            pl.BlockSpec((step, width), lambda i: (jnp.maximum(i - half, 0), 0)),
            pl.BlockSpec((per, 1, SEQ), lambda i: (i, 0, 0)),
        ]
        + [pl.BlockSpec(memory_space=pltpu.HBM)] * len(parts),
        out_specs=(
            pl.BlockSpec((2 * tokens // SEQ, 8, SEQ), lambda i: (0, 0, 0)),
            pl.BlockSpec((SEQ, width), lambda i: (0, 0)),
        ),
        scratch_shapes=[
            pltpu.VMEM((width, block), BF16),
            pltpu.SemaphoreType.DMA((16,)),
        ],
        compiler_params=pltpu.CompilerParams(vmem_limit_bytes=48 << 20),
    )(info, mine, other, local.reshape(2 * tokens // SEQ, 1, SEQ), *parts)


def choose_kernel(info_ref, local_ref, out_ref, most_ref):
    tokens = local_ref.shape[1]
    per = 128
    dests = out_ref.shape[0] // ROOM
    first_slot = info_ref[1] * SLOTS
    local = local_ref[...]
    upper = iota((per, per), 0) < iota((per, per), 1)
    diagonal = iota((per, per), 0) == iota((per, per), 1)

    def group(g, most):
        match = jnp.where(local - g * per == iota((per, tokens), 0), 1.0, 0.0)
        hits = match.astype(BF16)
        present = jnp.broadcast_to(jnp.max(match, axis=1, keepdims=True), (per, per))
        rank = jnp.sum(jnp.where(upper, present, 0.0), axis=0, keepdims=True).astype(jnp.int32)
        here = jnp.sum(jnp.where(diagonal, present, 0.0), axis=0, keepdims=True)
        slot = iota((ROOM, per), 0)
        chosen = (slot < SLOTS) & (slot == rank - first_slot) & (here > 0.5)
        packing = jnp.where(chosen, 1.0, 0.0).astype(BF16)
        out_ref[pl.ds(pl.multiple_of(g * ROOM, ROOM), ROOM), :] = dot(packing, hits).astype(BF16)
        return jnp.maximum(most, jnp.sum(here, axis=1, keepdims=True))

    most = lax.fori_loop(0, dests, group, jnp.zeros((1, 1), F32), unroll=2)
    most_ref[...] = jnp.broadcast_to(most, most_ref.shape)


def choices(info, local, dests):
    return pl.pallas_call(
        choose_kernel,
        out_shape=(
            jax.ShapeDtypeStruct((dests * ROOM, local.shape[1]), BF16),
            jax.ShapeDtypeStruct((8, 128), F32),
        ),
        in_specs=[pl.BlockSpec(memory_space=pltpu.SMEM), pl.BlockSpec(memory_space=pltpu.VMEM)],
        out_specs=(pl.BlockSpec(memory_space=pltpu.VMEM), pl.BlockSpec(memory_space=pltpu.VMEM)),
        compiler_params=pltpu.CompilerParams(vmem_limit_bytes=40 << 20),
    )(info, local)


def pack_kernel(hits_ref, most_ref, mine_ref, other_ref, out_ref):
    dests, _, width = out_ref.shape
    half = mine_ref.shape[0]
    some = dests // 2

    def pack(i, _):
        hits = hits_ref[pl.ds(pl.multiple_of(i * some * ROOM, some * ROOM), some * ROOM), :]
        sums = dot(hits[:, 0:half], mine_ref[...]) + dot(hits[:, half:], other_ref[...])
        sums = sums.reshape(some, ROOM, width)[:, 0:BLOCK, :]
        last = iota(sums.shape, 1) == SLOTS
        out_ref[pl.ds(i * some, some)] = jnp.where(
            last, most_ref[0:1, 0:1].reshape(1, 1, 1), sums
        ).astype(BF16)
        return 0

    lax.fori_loop(0, 2, pack, 0)


def packed_sums(chosen, mine, other):
    hits, most = chosen
    width = mine.shape[1]
    return pl.pallas_call(
        pack_kernel,
        out_shape=jax.ShapeDtypeStruct((hits.shape[0] // ROOM, BLOCK, width), BF16),
        in_specs=[pl.BlockSpec(memory_space=pltpu.VMEM)] * 4,
        out_specs=pl.BlockSpec(memory_space=pltpu.VMEM),
        compiler_params=pltpu.CompilerParams(vmem_limit_bytes=40 << 20),
    )(hits, most, mine, other)


def count_kernel(info_ref, assign_ref, out_ref):
    dp, slabs, _ = assign_ref.shape
    targets = iota((128, SEQ), 0) + info_ref[0]
    lane = iota(out_ref.shape, 1)

    def slab(f, out):
        acc = jnp.zeros((128, SEQ), F32)
        for d in range(dp):
            acc = acc + jnp.where(assign_ref[d, pl.ds(f, 1), :] == targets, 1.0, 0.0)
        return jnp.where(lane == f, jnp.sum(acc, axis=1, keepdims=True), out)

    out_ref[...] = lax.fori_loop(0, slabs, slab, jnp.zeros(out_ref.shape, F32))


def counted(info, assign):
    return pl.pallas_call(
        count_kernel,
        out_shape=jax.ShapeDtypeStruct((128, 128), F32),
        in_specs=[pl.BlockSpec(memory_space=pltpu.SMEM), pl.BlockSpec(memory_space=pltpu.VMEM)],
        out_specs=pl.BlockSpec(memory_space=pltpu.VMEM),
    )(info, assign)


def unpack_kernel(info_ref, counts_ref, got_ref, out_ref, most_ref):
    slabs, _, width = got_ref.shape
    counts = counts_ref[...]
    present = jnp.where(counts > 0.5, 1.0, 0.0).astype(BF16)
    lower = jnp.where(iota((128, 128), 1) < iota((128, 128), 0), 1.0, 0.0).astype(BF16)
    rank = dot(lower, present).astype(jnp.int32) - info_ref[1] * SLOTS
    slot = iota((128, BLOCK), 1)
    parts = []
    for f in range(slabs):
        chosen = (slot == rank[:, f : f + 1]) & (slot < SLOTS) & (counts[:, f : f + 1] > 0.5)
        parts.append(jnp.where(chosen, 1.0, 0.0))
    hits = jnp.concatenate(parts, axis=1).astype(BF16)
    out_ref[...] = dot(hits, got_ref[...].reshape(slabs * BLOCK, width))
    most = jnp.max(got_ref[:, SLOTS, 0:128].astype(F32), axis=0, keepdims=True)
    most_ref[...] = jnp.broadcast_to(most, most_ref.shape).astype(jnp.int32)


def unpacked_sums(info, counts, got):
    return pl.pallas_call(
        unpack_kernel,
        out_shape=(
            jax.ShapeDtypeStruct((128, got.shape[2]), F32),
            jax.ShapeDtypeStruct((8, 128), jnp.int32),
        ),
        in_specs=[pl.BlockSpec(memory_space=pltpu.SMEM)]
        + [pl.BlockSpec(memory_space=pltpu.VMEM)] * 2,
        out_specs=(pl.BlockSpec(memory_space=pltpu.VMEM), pl.BlockSpec(memory_space=pltpu.VMEM)),
    )(info, counts, got)


def exchanged(blocks, axis):
    return lax.all_to_all(blocks, axis, 0, 0, tiled=True)


def gathered(shard, axis):
    devices = lax.axis_size(axis)
    return exchanged(jnp.broadcast_to(shard[None], (devices,) + shard.shape), axis)


def swapped(shard, axis):
    return lax.ppermute(shard, axis, [(0, 1), (1, 0)])


def turned(shard, axis, by):
    devices = lax.axis_size(axis)
    return lax.ppermute(shard, axis, [(i, (i + by) % devices) for i in range(devices)])


def neighbours(block, axis):
    return turned(block, axis, 1), turned(block, axis, lax.axis_size(axis) - 1)


def far_halves(back, ahead, axis):
    half = back.shape[0] // 2
    return turned(back[:half], axis, 1), turned(ahead[half:], axis, lax.axis_size(axis) - 1)


def backwards(values, here):
    for dim, at in enumerate(here):
        size = values.shape[dim]
        values = jnp.take(values, (at - jnp.arange(size)) % size, axis=dim)
    return values


def shards(token_ids, embed_table, w_qkv, w_out, ln_gain, ln_bias, centroids_t, assignments):
    core = lax.axis_index("core")
    dp_rank = lax.axis_index(DP)
    fs_rank = lax.axis_index(FS)
    fs_size = lax.axis_size(FS)
    dp_size = lax.axis_size(DP)
    x_size = lax.axis_size("x")
    vocab, width = embed_table.shape
    zero = jnp.int32(0)
    ids = token_ids.reshape(fs_size, SEQ)

    at_x = lax.axis_index("x")

    def info_of(*values):
        return jnp.stack([jnp.asarray(v, jnp.int32) for v in values])

    by_dev = assignments.reshape(2, x_size, 2, fs_size, SEQ)
    of_slab = lax.dynamic_index_in_dim(by_dev, fs_rank, 3, keepdims=False)
    of_slab = jnp.transpose(of_slab, (2, 1, 0, 3))
    here = (core, at_x, lax.axis_index("zh"))
    of_slab = backwards(of_slab, here)
    block = centroids_t.shape[1]
    local = of_slab.reshape(1, -1) - dp_rank * block
    chosen = choices(info_of(zero, zero), local, fs_size)
    counts = counted(
        info_of(dp_rank * block + fs_rank * (block // fs_size)),
        assignments.reshape(dp_size, fs_size, SEQ),
    )

    part = (w_qkv.shape[1] + w_out.shape[1]) // (2 * x_size)
    both = jnp.concatenate([w_qkv, w_out], axis=1)
    piece = lax.dynamic_slice_in_dim(both, (core * x_size + at_x) * part, part, 1)
    column = gathered(piece, FS).reshape(width, part)

    two = jnp.concatenate([ids, swapped(ids, "zh")], axis=0)
    ids = [two] + [turned(two, "x", k) for k in range(1, x_size)]

    sent = listed_rows(info_of(fs_rank, zero), ids, embed_table)
    first = turned(centroids_t, "zl", 1)
    sent, column, local, shard, first = lax.optimization_barrier(
        (sent, column, local, centroids_t, first)
    )
    w_back, w_ahead = neighbours(column, "x")
    near = joined([shard, first] + [turned(shard, "zl", k) for k in range(2, 4)])
    places = placed_rows(info_of(fs_rank, zero, vocab), ids, fs_size)
    w_back, w_ahead, chosen, places, counts = lax.optimization_barrier(
        (w_back, w_ahead, chosen, places, counts)
    )
    rings = [column, w_back, *far_halves(w_back, w_ahead, "x"), w_ahead]
    rings += [swapped(w, "core") for w in rings]
    got = exchanged(sent, FS)
    got, near, *rings = lax.optimization_barrier((got, near, *rings))
    slab, rounds = expanded(places, got)

    def more_rows(state):
        turn, acc = state
        again = exchanged(listed_rows(info_of(fs_rank, turn), ids, embed_table), FS)
        extra, _ = expanded(placed_rows(info_of(fs_rank, turn, vocab), ids, fs_size), again)
        return turn + 1, acc + extra

    rounds = rounds[0, 0]
    _, slab = lax.while_loop(lambda state: state[0] < rounds, more_rows, (jnp.int32(1), slab))

    back, ahead = neighbours(near, "y")

    mine = encoded(info_of(core, at_x), rings, slab, ln_gain, ln_bias)
    mine, back, ahead = lax.optimization_barrier((mine, back, ahead))
    far_low, far_high = far_halves(back, ahead, "y")
    other = swapped(mine, "core")

    def one_turn(turn):
        info = info_of(zero, turn)
        got = exchanged(packed_sums(choices(info, local, fs_size), mine, other), FS)
        return unpacked_sums(info, counts, got)[0]

    packed = packed_sums(chosen, mine, other)
    packed, mine, other, far_low, far_high = lax.optimization_barrier(
        (packed, mine, other, far_low, far_high)
    )
    got = exchanged(packed, FS)

    stats, previous = scored(
        info_of(lax.axis_index("y"), fs_rank, *here, x_size, lax.axis_index("zl")),
        mine,
        other,
        local,
        [near, back, far_low, far_high, ahead],
    )
    stats, got = lax.optimization_barrier((stats, got))
    sums, widest = unpacked_sums(info_of(zero, zero), counts, got)
    widest = widest[0, 0]
    _, sums = lax.while_loop(
        lambda state: state[0] * SLOTS < widest,
        lambda state: (state[0] + 1, state[1] + one_turn(state[0])),
        (jnp.int32(1), sums),
    )

    home = exchanged(stats, DP)
    lse = home[:, 0, :]
    peak = jnp.max(lse, axis=0)
    token_loss = (
        jnp.log(jnp.sum(jnp.exp(lse - peak[None, :]), axis=0)) + peak - jnp.sum(home[:, 1, :], axis=0)
    )

    total = jnp.sum(counts[:, 0:fs_size], axis=1, keepdims=True)
    new_centroids = jnp.where(total > 0, sums / jnp.maximum(total, 1.0), previous)
    return token_loss, new_centroids


def solution(mesh):
    finer = Mesh(mesh.devices.reshape(2, 4, 2, 4, 4), ALL)
    placed = (P(DP), P(FS, None), P(FS, None), P(FS, None), P(), P(), P(FS, DP), P())
    return jax.shard_map(
        shards, mesh=finer, in_specs=placed, out_specs=(P(ALL), P(ALL, None)), check_vma=False
    )
```

```python
import jax
import jax.numpy as jnp
from jax import lax
from jax.experimental import pallas as pl
from jax.experimental.pallas import tpu as pltpu
from jax.sharding import Mesh
from jax.sharding import PartitionSpec as P

HEADS = 12
HEAD = 64
SEQ = 128
DP = ("zh", "x", "core")
FS = ("y", "zl")
ALL = DP + FS
LIST = 47
SLOTS = 39
BLOCK = SLOTS + 1
ROOM = 48
F32 = jnp.float32
BF16 = jnp.bfloat16


RING = ((0, 0, 2), (1, 0, 2), (2, 0, 1), (2, 1, 1), (3, 0, 2))


def iota(shape, dim):
    return lax.broadcasted_iota(jnp.int32, shape, dim)


def dot(a, b, dims=((1,), (0,))):
    return lax.dot_general(a, b, (dims, ((), ())), preferred_element_type=F32)


def ranked(present, groups):
    rows = present.shape[0]
    per = rows // groups
    upper = jnp.where(iota((128, 128), 0) < iota((128, 128), 1), 1.0, 0.0).astype(BF16)
    at, of = iota((rows, rows), 0), iota((rows, rows), 1)
    above = jnp.where((at // per == of // per) & (of < at), 1.0, 0.0).astype(BF16)
    ones = present.astype(BF16)
    return dot(ones, upper) + jnp.sum(dot(above, ones), axis=1, keepdims=True)


def tokens_of(ids_refs, dest):
    dests = ids_refs[0].shape[0] // 2
    return jnp.concatenate(
        [ref[pl.ds(z * dests + dest, 1), :] for ref in ids_refs for z in range(2)], axis=1
    )


def lists_kernel(info_ref, *refs):
    ids_refs, table_ref, rows_ref, present_ref, rank_ref, hits_ref = refs[0:4], *refs[4:]
    vocab = table_ref.shape[0]
    dests, tokens = rows_ref.shape[0], 8 * SEQ
    base = info_ref[0] * vocab
    first_slot = info_ref[1] * LIST
    high = 16

    def find(p, _):
        local = tokens_of(ids_refs, p) - base
        inside = (local >= 0) & (local < vocab)
        block = jnp.where((iota((high, tokens), 0) == (local >> 7)) & inside, 1.0, 0.0).astype(BF16)
        lane = jnp.where(iota((128, tokens), 0) == (local & 127), 1.0, 0.0).astype(BF16)
        seen = dot(block, lane, ((1,), (1,)))
        present_ref[pl.ds(pl.multiple_of(p * high, high), high), :] = jnp.where(seen > 0.5, 1.0, 0.0)
        return 0

    lax.fori_loop(0, dests, find, 0, unroll=4)
    present = present_ref[...]
    rank_ref[...] = jnp.where(present > 0.5, ranked(present, dests) - first_slot.astype(F32), -1.0)
    blocks = -(-vocab // 128)

    def choose(p, most):
        ranks = rank_ref[pl.ds(pl.multiple_of(p * high, high), high), :]
        slot = iota((ROOM, 128), 0)
        for h in range(blocks):
            chosen = (slot == ranks[h : h + 1, :].astype(jnp.int32)) & (slot < LIST)
            hits_ref[pl.ds(pl.multiple_of(p * ROOM, ROOM), ROOM), h * 128 : (h + 1) * 128] = jnp.where(
                chosen, 1.0, 0.0
            ).astype(BF16)
        return jnp.maximum(most, jnp.max(ranks))

    most = lax.fori_loop(0, dests, choose, jnp.float32(-1.0), unroll=2) + first_slot.astype(F32)
    whole = vocab // 16 * 16
    rounds = jnp.floor(most * (1.0 / LIST) + 1e-3) + 1.0
    some = 4

    def fetch(i, _):
        hits = hits_ref[pl.ds(pl.multiple_of(i * some * ROOM, some * ROOM), some * ROOM), :]
        rows = dot(hits[:, 0:whole], table_ref[0:whole, :])
        if whole < vocab:
            tail = table_ref[whole:vocab, :].astype(F32)
            for k in range(vocab - whole):
                rows = rows + hits[:, whole + k : whole + k + 1].astype(F32) * tail[k : k + 1, :]
        rows = rows.reshape(some, ROOM, rows.shape[1])
        rows_ref[pl.ds(i * some, some)] = jnp.where(iota(rows.shape, 1) == LIST, rounds, rows).astype(BF16)
        return 0

    lax.fori_loop(0, dests // some, fetch, 0)


def listed_rows(info, ids, table):
    dests = ids[0].shape[0] // 2
    width = table.shape[1]
    return pl.pallas_call(
        lists_kernel,
        out_shape=jax.ShapeDtypeStruct((dests, ROOM, width), BF16),
        in_specs=[pl.BlockSpec(memory_space=pltpu.SMEM)]
        + [pl.BlockSpec(memory_space=pltpu.VMEM)] * (len(ids) + 1),
        out_specs=pl.BlockSpec(memory_space=pltpu.VMEM),
        scratch_shapes=[
            pltpu.VMEM((dests * 16, 128), F32),
            pltpu.VMEM((dests * 16, 128), F32),
            pltpu.VMEM((dests * ROOM, 16 * 128), BF16),
        ],
        compiler_params=pltpu.CompilerParams(vmem_limit_bytes=40 << 20),
    )(info, *ids, table)


def place_kernel(info_ref, *refs):
    ids_refs, out_ref = refs[0:4], refs[4]
    tokens = 8 * SEQ
    owners = out_ref.shape[1] // ROOM
    first_slot = info_ref[1] * LIST
    vocab = info_ref[2]
    row = tokens_of(ids_refs, info_ref[0])
    owner = jnp.zeros(row.shape, jnp.int32)
    for k in range(1, owners):
        owner = owner + jnp.where(row >= k * vocab, 1, 0)
    local = row - owner * vocab
    group = owner * 16 + (local >> 7)
    block = jnp.where(iota((owners * 16, tokens), 0) == group, 1.0, 0.0).astype(BF16)
    lane = jnp.where(iota((128, tokens), 0) == (local & 127), 1.0, 0.0).astype(BF16)
    present = jnp.where(dot(block, lane, ((1,), (1,))) > 0.5, 1.0, 0.0)
    rank = ranked(present, owners) - first_slot.astype(F32)
    rank = jnp.where((rank >= 0) & (rank < LIST), rank, 255.0).astype(BF16)
    owner = owner.astype(F32)
    low = (local & 127).astype(F32)
    for t in range(tokens // 128):
        cols = slice(t * 128, (t + 1) * 128)
        found = lax.dot_general(
            block[:, cols], rank, (((0,), (0,)), ((), ())), preferred_element_type=F32
        )
        down = jnp.broadcast_to(low[:, cols], (128, 128)).T
        slot = jnp.sum(jnp.where(iota((128, 128), 1).astype(F32) == down, found, 0.0), axis=1, keepdims=True)
        of = jnp.broadcast_to(owner[:, cols], (128, 128)).T[:, 0:1]
        place = jnp.where(slot < LIST, of * ROOM + slot, -1.0).astype(jnp.int32)
        out_ref[cols, :] = jnp.where(place == iota((128, owners * ROOM), 1), 1.0, 0.0).astype(BF16)


def placed_rows(info, ids, owners):
    return pl.pallas_call(
        place_kernel,
        out_shape=jax.ShapeDtypeStruct((8 * SEQ, owners * ROOM), BF16),
        in_specs=[pl.BlockSpec(memory_space=pltpu.SMEM)]
        + [pl.BlockSpec(memory_space=pltpu.VMEM)] * len(ids),
        out_specs=pl.BlockSpec(memory_space=pltpu.VMEM),
        compiler_params=pltpu.CompilerParams(vmem_limit_bytes=40 << 20),
    )(info, *ids)


def expand_kernel(places_ref, got_ref, out_ref, rounds_ref):
    owners, room, width = got_ref.shape
    got = got_ref[...].reshape(owners * room, width)

    def fill(i, _):
        rows = pl.ds(pl.multiple_of(i * 2 * SEQ, 2 * SEQ), 2 * SEQ)
        out_ref[rows, :] = dot(places_ref[rows, :], got).astype(BF16)
        return 0

    lax.fori_loop(0, out_ref.shape[0] // (2 * SEQ), fill, 0)
    most = jnp.max(got_ref[:, LIST, 0:128].astype(F32), axis=0, keepdims=True)
    rounds_ref[...] = jnp.broadcast_to(most, rounds_ref.shape).astype(jnp.int32)


def expanded(places, got):
    return pl.pallas_call(
        expand_kernel,
        out_shape=(
            jax.ShapeDtypeStruct((places.shape[0], got.shape[2]), BF16),
            jax.ShapeDtypeStruct((8, 128), jnp.int32),
        ),
        in_specs=[pl.BlockSpec(memory_space=pltpu.VMEM)] * 2,
        out_specs=(pl.BlockSpec(memory_space=pltpu.VMEM), pl.BlockSpec(memory_space=pltpu.VMEM)),
        compiler_params=pltpu.CompilerParams(vmem_limit_bytes=40 << 20),
    )(places, got)


def join_kernel(*refs):
    parts, out_ref = refs[:-1], refs[-1]
    rows = parts[0].shape[0]
    for k, ref in enumerate(parts):
        out_ref[k * rows : (k + 1) * rows, :] = ref[...]


def joined(parts):
    rows, cols = parts[0].shape
    return pl.pallas_call(
        join_kernel,
        out_shape=jax.ShapeDtypeStruct((len(parts) * rows, cols), parts[0].dtype),
        in_specs=[pl.BlockSpec(memory_space=pltpu.VMEM)] * len(parts),
        out_specs=pl.BlockSpec(memory_space=pltpu.VMEM),
    )(*parts)


def put(sources, targets, sems):
    copies = [
        pltpu.make_async_copy(src, dst, sems.at[k])
        for k, (src, dst) in enumerate(zip(sources, targets, strict=True))
    ]
    for c in copies:
        c.start()
    for c in copies:
        c.wait()


def encode_kernel(info_ref, *refs):
    rings = refs[0:10]
    slab_ref, gain_ref, bias_ref, out_ref, w_ref, packed_ref, scores_ref, probs_ref, context_ref, sems = (
        refs[10:]
    )
    x_size = 4
    core, at_x = info_ref[0], info_ref[1]
    depth, part = w_ref.shape[1:]
    targets = []
    for core_at in (core, 1 - core):
        for back, first, count in RING:
            place = core_at * x_size + lax.rem(at_x - back + x_size, x_size)
            targets.append(w_ref.at[place, pl.ds(first * (depth // 2), count * (depth // 2)), :])
    put(rings, targets, sems)
    tokens, width = packed_ref.shape[0], slab_ref.shape[1]
    left = iota((SEQ, 2 * HEAD), 1) < HEAD
    zero = jnp.zeros((SEQ, 2 * HEAD), BF16)
    pairs = HEADS // 2
    passages = tokens // SEQ

    def stacked(values):
        return jnp.concatenate([jnp.where(left, values, zero), jnp.where(left, zero, values)], axis=0)

    def step(i, _):
        x = slab_ref[pl.ds(i * tokens, tokens), :]
        for j in range(6):
            packed_ref[:, j * part : (j + 1) * part] = dot(x, w_ref[j]).astype(BF16)
        for b in range(passages):
            rows = slice(b * SEQ, (b + 1) * SEQ)
            for pair in range(pairs):
                at = pair * 2 * HEAD
                q = packed_ref[rows, at : at + 2 * HEAD] * jnp.asarray(HEAD**-0.5, BF16)
                k = packed_ref[rows, width + at : width + at + 2 * HEAD]
                scores_ref[b * pairs + pair] = dot(q, stacked(k), ((1,), (1,)))
        for n in range(passages * pairs):
            for h in range(2):
                s = scores_ref[n, :, h * SEQ : (h + 1) * SEQ]
                e = jnp.exp(s - jnp.max(s, axis=1, keepdims=True))
                probs = e * (1.0 / jnp.sum(e, axis=1, keepdims=True))
                probs_ref[n, :, h * SEQ : (h + 1) * SEQ] = probs.astype(BF16)
        for b in range(passages):
            rows = slice(b * SEQ, (b + 1) * SEQ)
            for pair in range(pairs):
                at = pair * 2 * HEAD
                v = packed_ref[rows, 2 * width + at : 2 * width + at + 2 * HEAD]
                context_ref[rows, at : at + 2 * HEAD] = dot(
                    probs_ref[b * pairs + pair], stacked(v)
                ).astype(BF16)
        context = context_ref[...]
        half = width // 2
        mixed = [
            dot(context, w_ref[6 + k]) + x[:, k * half : (k + 1) * half].astype(F32) for k in range(2)
        ]
        mean = sum(jnp.sum(m, axis=1, keepdims=True) for m in mixed) * (1.0 / width)
        center = [m - mean for m in mixed]
        spread = sum(jnp.sum(c * c, axis=1, keepdims=True) for c in center) * (1.0 / width)
        scale = lax.rsqrt(spread + 1e-05)
        for k in range(2):
            cols = slice(k * half, (k + 1) * half)
            out_ref[pl.ds(i * tokens, tokens), cols] = (
                center[k] * scale * gain_ref[:, cols] + bias_ref[:, cols]
            ).astype(BF16)
        return 0

    lax.fori_loop(0, slab_ref.shape[0] // tokens, step, 0)


def encoded(info, rings, slab, gain, bias):
    part = rings[0].shape[1]
    tokens, width = 2 * SEQ, slab.shape[1]
    pairs = tokens // SEQ * HEADS // 2
    return pl.pallas_call(
        encode_kernel,
        out_shape=jax.ShapeDtypeStruct(slab.shape, BF16),
        in_specs=[pl.BlockSpec(memory_space=pltpu.SMEM)]
        + [pl.BlockSpec(memory_space=pltpu.HBM)] * len(rings)
        + [pl.BlockSpec(memory_space=pltpu.VMEM)] * 3,
        out_specs=pl.BlockSpec(memory_space=pltpu.VMEM),
        scratch_shapes=[
            pltpu.VMEM((8, width, part), BF16),
            pltpu.VMEM((tokens, 3 * width), BF16),
            pltpu.VMEM((pairs, SEQ, 2 * SEQ), F32),
            pltpu.VMEM((pairs, SEQ, 2 * SEQ), BF16),
            pltpu.VMEM((tokens, width), BF16),
            pltpu.SemaphoreType.DMA((len(rings),)),
        ],
        compiler_params=pltpu.CompilerParams(vmem_limit_bytes=40 << 20),
    )(info, *rings, slab, gain.reshape(1, width), bias.reshape(1, width))


def score_kernel(info_ref, mine_ref, other_ref, local_ref, *refs):
    parts = refs[0:5]
    out_ref, old_ref, cent_ref, sems = refs[5:]
    step = pl.program_id(0)
    half = pl.num_programs(0) // 2

    @pl.when(step == 0)
    def _():
        shard = parts[0].shape[0] // 4
        sources, targets = [], []
        for ref, (back, first, count) in zip(parts, RING, strict=True):
            owner = lax.rem(info_ref[0] - back + 4, 4) * 4
            for k in range(2 * count):
                start = (owner + lax.rem(info_ref[6] - 2 * first - k + 4, 4)) * shard
                sources.append(ref.at[pl.ds(k * shard, shard), :])
                targets.append(cent_ref.at[pl.ds(pl.multiple_of(start, shard), shard), :])
        put(sources, targets, sems)

    block = cent_ref.shape[1]
    span = 2 * SEQ
    for n in range(mine_ref.shape[0] // span):
        rows = slice(n * span, (n + 1) * span)
        s = dot(jnp.where(step < half, mine_ref[rows, :], other_ref[rows, :]), cent_ref[...])
        peak = jnp.max(s, axis=1, keepdims=True)
        mass = jnp.sum(jnp.exp(s - peak), axis=1, keepdims=True)
        local = jnp.concatenate(
            [jnp.broadcast_to(local_ref[2 * n + z], (SEQ, SEQ)).T[:, 0:1] for z in range(2)], axis=0
        )
        picked = jnp.sum(jnp.where(local == iota((span, block), 1), s, 0.0), axis=1, keepdims=True)
        both = jnp.where(iota((span, 128), 1) == 0, peak + jnp.log(mass), picked)
        x_size = info_ref[5]
        per_step = mine_ref.shape[0] // span
        back = lax.rem(step, half) * per_step + n
        x = lax.rem(info_ref[3] - back + x_size, x_size)
        core = jnp.where(step < half, info_ref[2], 1 - info_ref[2])
        for z in range(2):
            zh = info_ref[4] if z == 0 else 1 - info_ref[4]
            out_ref[zh * (2 * x_size) + x * 2 + core] = both[z * SEQ : (z + 1) * SEQ, :].T[0:8, :]

    @pl.when(step == pl.num_programs(0) - 1)
    def _():
        per = old_ref.shape[0]
        old = cent_ref[:, pl.ds(pl.multiple_of(info_ref[1] * per, per), per)]
        old_ref[...] = old.astype(F32).T


def scored(info, mine, other, local, parts):
    tokens, width = mine.shape
    block = parts[0].shape[1]
    step = 4 * SEQ
    per = step // SEQ
    half = tokens // step
    return pl.pallas_call(
        score_kernel,
        grid=(2 * half,),
        out_shape=(
            jax.ShapeDtypeStruct((2 * tokens // SEQ, 8, SEQ), F32),
            jax.ShapeDtypeStruct((SEQ, width), F32),
        ),
        in_specs=[
            pl.BlockSpec(memory_space=pltpu.SMEM),
            pl.BlockSpec((step, width), lambda i: (jnp.minimum(i, half - 1), 0)),
            pl.BlockSpec((step, width), lambda i: (jnp.maximum(i - half, 0), 0)),
            pl.BlockSpec((per, 1, SEQ), lambda i: (i, 0, 0)),
        ]
        + [pl.BlockSpec(memory_space=pltpu.HBM)] * len(parts),
        out_specs=(
            pl.BlockSpec((2 * tokens // SEQ, 8, SEQ), lambda i: (0, 0, 0)),
            pl.BlockSpec((SEQ, width), lambda i: (0, 0)),
        ),
        scratch_shapes=[
            pltpu.VMEM((width, block), BF16),
            pltpu.SemaphoreType.DMA((16,)),
        ],
        compiler_params=pltpu.CompilerParams(vmem_limit_bytes=48 << 20),
    )(info, mine, other, local.reshape(2 * tokens // SEQ, 1, SEQ), *parts)


def choose_kernel(info_ref, local_ref, out_ref, most_ref):
    tokens = local_ref.shape[1]
    per = 128
    dests = out_ref.shape[0] // ROOM
    first_slot = info_ref[1] * SLOTS
    local = local_ref[...]
    upper = iota((per, per), 0) < iota((per, per), 1)
    diagonal = iota((per, per), 0) == iota((per, per), 1)

    def group(g, most):
        match = jnp.where(local - g * per == iota((per, tokens), 0), 1.0, 0.0)
        hits = match.astype(BF16)
        present = jnp.broadcast_to(jnp.max(match, axis=1, keepdims=True), (per, per))
        rank = jnp.sum(jnp.where(upper, present, 0.0), axis=0, keepdims=True).astype(jnp.int32)
        here = jnp.sum(jnp.where(diagonal, present, 0.0), axis=0, keepdims=True)
        slot = iota((ROOM, per), 0)
        chosen = (slot < SLOTS) & (slot == rank - first_slot) & (here > 0.5)
        packing = jnp.where(chosen, 1.0, 0.0).astype(BF16)
        out_ref[pl.ds(pl.multiple_of(g * ROOM, ROOM), ROOM), :] = dot(packing, hits).astype(BF16)
        return jnp.maximum(most, jnp.sum(here, axis=1, keepdims=True))

    most = lax.fori_loop(0, dests, group, jnp.zeros((1, 1), F32), unroll=2)
    most_ref[...] = jnp.broadcast_to(most, most_ref.shape)


def choices(info, local, dests):
    return pl.pallas_call(
        choose_kernel,
        out_shape=(
            jax.ShapeDtypeStruct((dests * ROOM, local.shape[1]), BF16),
            jax.ShapeDtypeStruct((8, 128), F32),
        ),
        in_specs=[pl.BlockSpec(memory_space=pltpu.SMEM), pl.BlockSpec(memory_space=pltpu.VMEM)],
        out_specs=(pl.BlockSpec(memory_space=pltpu.VMEM), pl.BlockSpec(memory_space=pltpu.VMEM)),
        compiler_params=pltpu.CompilerParams(vmem_limit_bytes=40 << 20),
    )(info, local)


def pack_kernel(hits_ref, most_ref, mine_ref, other_ref, out_ref):
    dests, _, width = out_ref.shape
    half = mine_ref.shape[0]
    some = dests // 2

    def pack(i, _):
        hits = hits_ref[pl.ds(pl.multiple_of(i * some * ROOM, some * ROOM), some * ROOM), :]
        sums = dot(hits[:, 0:half], mine_ref[...]) + dot(hits[:, half:], other_ref[...])
        sums = sums.reshape(some, ROOM, width)[:, 0:BLOCK, :]
        last = iota(sums.shape, 1) == SLOTS
        out_ref[pl.ds(i * some, some)] = jnp.where(
            last, most_ref[0:1, 0:1].reshape(1, 1, 1), sums
        ).astype(BF16)
        return 0

    lax.fori_loop(0, 2, pack, 0)


def packed_sums(chosen, mine, other):
    hits, most = chosen
    width = mine.shape[1]
    return pl.pallas_call(
        pack_kernel,
        out_shape=jax.ShapeDtypeStruct((hits.shape[0] // ROOM, BLOCK, width), BF16),
        in_specs=[pl.BlockSpec(memory_space=pltpu.VMEM)] * 4,
        out_specs=pl.BlockSpec(memory_space=pltpu.VMEM),
        compiler_params=pltpu.CompilerParams(vmem_limit_bytes=40 << 20),
    )(hits, most, mine, other)


def count_kernel(info_ref, assign_ref, out_ref):
    dp, slabs, _ = assign_ref.shape
    targets = iota((128, SEQ), 0) + info_ref[0]
    lane = iota(out_ref.shape, 1)

    def slab(f, out):
        acc = jnp.zeros((128, SEQ), F32)
        for d in range(dp):
            acc = acc + jnp.where(assign_ref[d, pl.ds(f, 1), :] == targets, 1.0, 0.0)
        return jnp.where(lane == f, jnp.sum(acc, axis=1, keepdims=True), out)

    out_ref[...] = lax.fori_loop(0, slabs, slab, jnp.zeros(out_ref.shape, F32))


def counted(info, assign):
    return pl.pallas_call(
        count_kernel,
        out_shape=jax.ShapeDtypeStruct((128, 128), F32),
        in_specs=[pl.BlockSpec(memory_space=pltpu.SMEM), pl.BlockSpec(memory_space=pltpu.VMEM)],
        out_specs=pl.BlockSpec(memory_space=pltpu.VMEM),
    )(info, assign)


def unpack_kernel(info_ref, counts_ref, got_ref, out_ref, most_ref):
    slabs, _, width = got_ref.shape
    counts = counts_ref[...]
    present = jnp.where(counts > 0.5, 1.0, 0.0).astype(BF16)
    lower = jnp.where(iota((128, 128), 1) < iota((128, 128), 0), 1.0, 0.0).astype(BF16)
    rank = dot(lower, present).astype(jnp.int32) - info_ref[1] * SLOTS
    slot = iota((128, BLOCK), 1)
    parts = []
    for f in range(slabs):
        chosen = (slot == rank[:, f : f + 1]) & (slot < SLOTS) & (counts[:, f : f + 1] > 0.5)
        parts.append(jnp.where(chosen, 1.0, 0.0))
    hits = jnp.concatenate(parts, axis=1).astype(BF16)
    out_ref[...] = dot(hits, got_ref[...].reshape(slabs * BLOCK, width))
    most = jnp.max(got_ref[:, SLOTS, 0:128].astype(F32), axis=0, keepdims=True)
    most_ref[...] = jnp.broadcast_to(most, most_ref.shape).astype(jnp.int32)


def unpacked_sums(info, counts, got):
    return pl.pallas_call(
        unpack_kernel,
        out_shape=(
            jax.ShapeDtypeStruct((128, got.shape[2]), F32),
            jax.ShapeDtypeStruct((8, 128), jnp.int32),
        ),
        in_specs=[pl.BlockSpec(memory_space=pltpu.SMEM)]
        + [pl.BlockSpec(memory_space=pltpu.VMEM)] * 2,
        out_specs=(pl.BlockSpec(memory_space=pltpu.VMEM), pl.BlockSpec(memory_space=pltpu.VMEM)),
    )(info, counts, got)


def exchanged(blocks, axis):
    return lax.all_to_all(blocks, axis, 0, 0, tiled=True)


def gathered(shard, axis):
    devices = lax.axis_size(axis)
    return exchanged(jnp.broadcast_to(shard[None], (devices,) + shard.shape), axis)


def swapped(shard, axis):
    return lax.ppermute(shard, axis, [(0, 1), (1, 0)])


def turned(shard, axis, by):
    devices = lax.axis_size(axis)
    return lax.ppermute(shard, axis, [(i, (i + by) % devices) for i in range(devices)])


def neighbours(block, axis):
    return turned(block, axis, 1), turned(block, axis, lax.axis_size(axis) - 1)


def far_halves(back, ahead, axis):
    half = back.shape[0] // 2
    return turned(back[:half], axis, 1), turned(ahead[half:], axis, lax.axis_size(axis) - 1)


def backwards(values, here):
    for dim, at in enumerate(here):
        size = values.shape[dim]
        values = jnp.take(values, (at - jnp.arange(size)) % size, axis=dim)
    return values


def shards(token_ids, embed_table, w_qkv, w_out, ln_gain, ln_bias, centroids_t, assignments):
    core = lax.axis_index("core")
    dp_rank = lax.axis_index(DP)
    fs_rank = lax.axis_index(FS)
    fs_size = lax.axis_size(FS)
    dp_size = lax.axis_size(DP)
    x_size = lax.axis_size("x")
    vocab, width = embed_table.shape
    zero = jnp.int32(0)
    ids = token_ids.reshape(fs_size, SEQ)

    at_x = lax.axis_index("x")

    def info_of(*values):
        return jnp.stack([jnp.asarray(v, jnp.int32) for v in values])

    by_dev = assignments.reshape(2, x_size, 2, fs_size, SEQ)
    of_slab = lax.dynamic_index_in_dim(by_dev, fs_rank, 3, keepdims=False)
    of_slab = jnp.transpose(of_slab, (2, 1, 0, 3))
    here = (core, at_x, lax.axis_index("zh"))
    of_slab = backwards(of_slab, here)
    block = centroids_t.shape[1]
    local = of_slab.reshape(1, -1) - dp_rank * block
    chosen = choices(info_of(zero, zero), local, fs_size)
    counts = counted(
        info_of(dp_rank * block + fs_rank * (block // fs_size)),
        assignments.reshape(dp_size, fs_size, SEQ),
    )

    part = (w_qkv.shape[1] + w_out.shape[1]) // (2 * x_size)
    both = jnp.concatenate([w_qkv, w_out], axis=1)
    piece = lax.dynamic_slice_in_dim(both, (core * x_size + at_x) * part, part, 1)
    column = gathered(piece, FS).reshape(width, part)

    two = jnp.concatenate([ids, swapped(ids, "zh")], axis=0)
    ids = [two] + [turned(two, "x", k) for k in range(1, x_size)]

    sent = listed_rows(info_of(fs_rank, zero), ids, embed_table)
    first, last = turned(centroids_t, "zl", 1), turned(centroids_t, "zl", 3)
    sent, column, local, shard, first, last = lax.optimization_barrier(
        (sent, column, local, centroids_t, first, last)
    )
    w_back, w_ahead = neighbours(column, "x")
    near = joined([shard, first, turned(shard, "zl", 2), last])
    places = placed_rows(info_of(fs_rank, zero, vocab), ids, fs_size)
    w_back, w_ahead, chosen, places, counts = lax.optimization_barrier(
        (w_back, w_ahead, chosen, places, counts)
    )
    rings = [column, w_back, *far_halves(w_back, w_ahead, "x"), w_ahead]
    rings += [swapped(w, "core") for w in rings]
    got = exchanged(sent, FS)
    got, near, *rings = lax.optimization_barrier((got, near, *rings))
    slab, rounds = expanded(places, got)

    def more_rows(state):
        turn, acc = state
        again = exchanged(listed_rows(info_of(fs_rank, turn), ids, embed_table), FS)
        extra, _ = expanded(placed_rows(info_of(fs_rank, turn, vocab), ids, fs_size), again)
        return turn + 1, acc + extra

    rounds = rounds[0, 0]
    _, slab = lax.while_loop(lambda state: state[0] < rounds, more_rows, (jnp.int32(1), slab))

    back, ahead = neighbours(near, "y")

    mine = encoded(info_of(core, at_x), rings, slab, ln_gain, ln_bias)
    mine, back, ahead = lax.optimization_barrier((mine, back, ahead))
    far_low, far_high = far_halves(back, ahead, "y")
    other = swapped(mine, "core")

    def one_turn(turn):
        info = info_of(zero, turn)
        got = exchanged(packed_sums(choices(info, local, fs_size), mine, other), FS)
        return unpacked_sums(info, counts, got)[0]

    packed = packed_sums(chosen, mine, other)
    packed, mine, other, far_low, far_high = lax.optimization_barrier(
        (packed, mine, other, far_low, far_high)
    )
    got = exchanged(packed, FS)

    stats, previous = scored(
        info_of(lax.axis_index("y"), fs_rank, *here, x_size, lax.axis_index("zl")),
        mine,
        other,
        local,
        [near, back, far_low, far_high, ahead],
    )
    stats, got = lax.optimization_barrier((stats, got))
    sums, widest = unpacked_sums(info_of(zero, zero), counts, got)
    widest = widest[0, 0]
    _, sums = lax.while_loop(
        lambda state: state[0] * SLOTS < widest,
        lambda state: (state[0] + 1, state[1] + one_turn(state[0])),
        (jnp.int32(1), sums),
    )

    home = exchanged(stats, DP)
    lse = home[:, 0, :]
    peak = jnp.max(lse, axis=0)
    token_loss = (
        jnp.log(jnp.sum(jnp.exp(lse - peak[None, :]), axis=0)) + peak - jnp.sum(home[:, 1, :], axis=0)
    )

    total = jnp.sum(counts[:, 0:fs_size], axis=1, keepdims=True)
    new_centroids = jnp.where(total > 0, sums / jnp.maximum(total, 1.0), previous)
    return token_loss, new_centroids


def solution(mesh):
    finer = Mesh(mesh.devices.reshape(2, 4, 2, 4, 4), ALL)
    placed = (P(DP), P(FS, None), P(FS, None), P(FS, None), P(), P(), P(FS, DP), P())
    return jax.shard_map(
        shards, mesh=finer, in_specs=placed, out_specs=(P(ALL), P(ALL, None)), check_vma=False
    )
```
